256 devices in a mesh: level: 2 (over z_hi), gx: 8 (over y, core), gy: 16 (over x, z_lo).
Axes of the slice: x: 4, y: 4, z: 8 (z_hi: 2, z_lo: 4; z = z_hi * 4 + z_lo), core: 2. Of those that a mesh axis runs over, the one named last changes fastest.
Arguments:
- populations: float32 [2, 107, 32, 64, 128], P('level', None, 'gx', 'gy'), as said below
- solid_mask: int32 [2, 32, 64, 128], P('level', 'gx', 'gy'), may hold values 0 or 1
- recv_tiles: int32 [2, 8, 16, 16], P('level', 'gx', 'gy'), may hold values from 0 to 15, each once within a row
- owner_gy: int32 [2, 8, 16, 16, 1], P('level', 'gx', 'gy'), may hold values from 0 to 15; in each aligned block of 16 rows (0 to 15, 16 to 31, ..., all dimensions but the last counted through in order) at most 2 rows name the same one
- owner_tiles: int32 [2, 8, 16, 16], P('level', 'gx', 'gy'), may hold values from 0 to 15
Outputs:
- evolved: float32 [2, 107, 32, 64, 128], P('level', None, 'gx', 'gy')
The draws below stay inside these ranges and needn't reach their ends.
Inputs may be any that keep to these rules, and one draw needn't show every extreme that they name: `populations`: every population is positive. `recv_tiles`: each row is a permutation of a device's columns, numbered x * 4 + y; its first 16 entries are the device's interface columns. `owner_gy`: among the 16 interface columns of one device at most 2 name the same owner, a bound that some block reaches. `owner_tiles`: columns of the owner device, numbered x * 4 + y.
All inputs are finite; a program needn't handle non-finite values. No bound on the sum of `solid_mask` on one device may be relied on, other than what follows from the above.
Results may differ from the reference program's by a relative error of at most 0.0003.
Values sent between devices are 32-bit elements; how exact they have to be, the bound alone decides.
No kernel may reach another device: no remote copies, remote signals or barrier semaphores. Data moves between devices by JAX's collectives and lax.ppermute only.
A program may use at most 64 MiB of HBM per device.

```python
import math
import jax
import jax.numpy as jnp
import numpy as np
from jax import lax

Q = 107
CX = 4
CY = 4
CAP = 2
TILES = 16
KI = 16
NX = 32
NY = 64
NZ = 128
N_GX = 8
N_GY = 16


def lattice_drawn():
    shells = [(0, 0, 0), (0, 0, 1), (0, 1, 1), (1, 1, 1), (0, 0, 2), (0, 2, 2), (2, 2, 2), (0, 0, 3), (0, 1, 2), (1, 1, 2)]
    vectors = []
    for first in range(-3, 4):
        for second in range(-3, 4):
            for third in range(-3, 4):
                if tuple(sorted((abs(first), abs(second), abs(third)))) in shells:
                    vectors.append((first, second, third))
    speeds = np.array(vectors) * 1.0
    weights = np.exp(-0.5 * np.sum(speeds * speeds, axis=1))
    weights = weights / np.sum(weights)
    theta = float(np.sum(weights * speeds[:, 0] * speeds[:, 0]))
    return (speeds, weights, theta)


def draw_populations(key, part):
    speeds, weights, theta = lattice_drawn()
    keys = jax.random.split(key, 3)
    density = jax.random.uniform(keys[0], (2, 1, NX, NY, NZ), jnp.float32, 0.9, 1.1)
    velocity = jax.random.uniform(keys[1], (2, 3, NX, NY, NZ), jnp.float32, -0.05, 0.05)
    spread = jax.random.uniform(keys[2], (2, Q, NX, NY, NZ), jnp.float32, -0.7, 0.9)
    phase = jnp.zeros((2, Q, NX, NY, NZ), jnp.float32)
    for axis_index in range(3):
        column = jnp.asarray(speeds[:, axis_index], jnp.float32)[None, :, None, None, None]
        phase = phase + column * velocity[:, axis_index:axis_index + 1]
    scaled = jnp.asarray(weights, jnp.float32)[None, :, None, None, None]
    return (scaled * density * jnp.exp(phase / theta + spread)).astype(jnp.float32)


def touch_ends(values, rng, least, high):
    longest = values.shape.index(max(values.shape))
    spots = []
    for shift in (0, 1):
        where = [jax.random.randint(jax.random.fold_in(rng, axis), (), 0, length) for axis, length in enumerate(values.shape)]
        where[longest] = (where[longest] + shift) % values.shape[longest]
        spots.append(tuple(where))
    return values.at[spots[0]].set(least).at[spots[1]].set(high)


def routed_block(stream_key, own, number, rows, number_of, top, bound, lean):
    order = jax.random.permutation(stream_key, number_of)
    heavy_load, common = load_shares(number_of, rows * top, bound, lean, True), load_shares(number_of, rows * top, bound, lean, False)
    places = jnp.arange(number_of)

    def named(sizes, turn):
        used = int((sizes > 0).sum())
        fixed = max(1, used // 4)
        moved = fixed + (places - fixed + turn * (used - fixed)) % max(1, number_of - fixed)
        return jnp.zeros((number_of,), jnp.int32).at[order[jnp.where(places < fixed, places, moved)]].set(jnp.asarray(sizes, jnp.int32))

    sizes = jnp.where(number % 4 == 0, named(heavy_load, number // 4), named(common, number - number // 4 - 1))
    mixed = jax.random.permutation(jax.random.fold_in(own, 3), number_of)
    giver, taker = mixed[0:number_of // 2 * 2:2], mixed[1:number_of // 2 * 2:2]
    slack = jnp.minimum(sizes[giver] - 1, bound - sizes[taker]) // 2
    slack = jnp.where((giver == order[0]) | (taker == order[0]) | (sizes[taker] == 0), 0, jnp.maximum(slack, 0))
    moved = jax.random.randint(jax.random.fold_in(own, 4), (number_of // 2,), 0, 1 << 20) % (slack + 1)
    sizes = sizes.at[giver].add(-moved).at[taker].add(moved)
    items = jnp.searchsorted(jnp.cumsum(sizes), jnp.arange(rows * top), side="right").astype(jnp.int32)
    listing = items.reshape(top, rows).T
    listing = listing[jax.random.permutation(jax.random.fold_in(own, 1), rows)]
    turn = jax.random.randint(jax.random.fold_in(own, 2), (rows, 1), 0, top)
    return jnp.take_along_axis(listing, (jnp.arange(top)[None, :] + turn) % top, axis=1)


def load_shares(number_of, total, most, skew, full):
    weights = [(1 << 20) // math.isqrt(standing ** skew) + 1 for standing in range(1, number_of + 1)]
    largest = most if full else min(most, max(-(-total // number_of), total * weights[0] // sum(weights)))
    least = 1 if total - largest >= number_of - 1 else 0
    given, spare = [largest] + [least] * (number_of - 1), total - largest - least * (number_of - 1)
    while spare > 0:
        free = [i for i in range(1, number_of) if given[i] < largest] or [i for i in range(1, number_of) if given[i] < most]
        whole, remaining = sum([weights[i] for i in free]), spare
        for i in free:
            extra = min(most - given[i], max(1, remaining * weights[i] // whole), spare)
            given[i] = given[i] + extra
            spare = spare - extra
    return np.array(given)


def setup_inputs(seed: int = 0) -> dict:
    arg_keys = jax.random.split(jax.random.key(seed), 6)
    populations = draw_populations(jax.random.fold_in(arg_keys[5], 71), 0)
    solid_mask = touch_ends((jax.random.randint(arg_keys[1], (2, NX, NY, NZ), 0, 8) < 1).astype(jnp.int32), jax.random.fold_in(arg_keys[1], 1), 0, 1)
    recv_tiles = jax.vmap(lambda own: jax.random.permutation(own, TILES))(jax.random.split(arg_keys[2], 2 * N_GX * N_GY)).reshape((2, N_GX, N_GY, TILES)).astype(jnp.int32)
    owner_gy_keys = jax.random.split(jax.random.fold_in(arg_keys[3], 1), 2 * N_GX * N_GY * KI // KI)
    owner_gy_turns = jax.random.permutation(jax.random.fold_in(arg_keys[3], 3), 2 * N_GX * N_GY * KI // KI)
    owner_gy = jax.vmap(lambda own, number: routed_block(jax.random.fold_in(arg_keys[3], 2), own, number, KI, N_GY, 1, CAP, 2))(owner_gy_keys, owner_gy_turns).reshape((2, N_GX, N_GY, KI, 1))
    owner_tiles = touch_ends(jax.random.randint(arg_keys[4], (2, N_GX, N_GY, KI), 0, TILES), jax.random.fold_in(arg_keys[4], 1), 0, TILES - 1).astype(jnp.int32)
    return dict(populations=populations, solid_mask=solid_mask, recv_tiles=recv_tiles, owner_gy=owner_gy, owner_tiles=owner_tiles)


FLOOR = 0.05
BETA_COARSE = 0.9
BETA_FINE = 0.8
SCALE_FINE = 0.5
SCALE_COARSE = 1.5
precise = lax.Precision.HIGHEST


def lattice():
    shells = [(0, 0, 0), (0, 0, 1), (0, 1, 1), (1, 1, 1), (0, 0, 2), (0, 2, 2), (2, 2, 2), (0, 0, 3), (0, 1, 2), (1, 1, 2)]
    vectors = []
    for first in range(-3, 4):
        for second in range(-3, 4):
            for third in range(-3, 4):
                if tuple(sorted((abs(first), abs(second), abs(third)))) in shells:
                    vectors.append((first, second, third))
    offsets = np.array(vectors)
    speeds = offsets * 1.0
    weights = np.exp(-0.5 * np.sum(speeds * speeds, axis=1))
    weights = weights / np.sum(weights)
    theta = float(np.sum(weights * speeds[:, 0] * speeds[:, 0]))
    return offsets, speeds, weights, theta


def index_lists():
    pairs = [(first, second) for first in range(3) for second in range(first, 3)]
    triples = [(first, second, third) for first in range(3) for second in range(first, 3) for third in range(second, 3)]
    return pairs, triples


def hermite_tables():
    offsets, speeds, weights, theta = lattice()
    pairs, triples = index_lists()
    table_rows = [np.ones(speeds.shape[0])]
    for first in range(3):
        table_rows.append(speeds[:, first])
    for first, second in pairs:
        table_rows.append(speeds[:, first] * speeds[:, second] - theta * float(first == second))
    for first, second, third in triples:
        table_rows.append(speeds[:, first] * speeds[:, second] * speeds[:, third] - theta * (speeds[:, first] * float(second == third) + speeds[:, second] * float(first == third) + speeds[:, third] * float(first == second)))
    basis = np.stack(table_rows)
    norms = (basis * basis) @ weights
    rebuild = basis.T * weights[:, None] / norms[None, :]
    return jnp.asarray(basis, jnp.float32), jnp.asarray(rebuild, jnp.float32)


def reconstruct(moments, scale):
    pairs, triples = index_lists()
    basis, rebuild = hermite_tables()
    density = moments[:, 0]
    flux = moments[:, 1:4]
    eq_two = jnp.stack([flux[:, first] * flux[:, second] for first, second in pairs], 1) / density[:, None]
    eq_three = jnp.stack([flux[:, first] * flux[:, second] * flux[:, third] for first, second, third in triples], 1) / (density * density)[:, None]
    mixed = jnp.concatenate([moments[:, :4], eq_two + scale * (moments[:, 4:10] - eq_two), eq_three + scale * (moments[:, 10:] - eq_three)], 1)
    return jnp.einsum("qn,tnz->tqz", rebuild, mixed, precision=precise)


def collide(pops, solid, beta):
    offsets, speeds_np, weights_np, theta = lattice()
    speeds = jnp.asarray(speeds_np, jnp.float32)
    weights = jnp.asarray(weights_np, jnp.float32)[:, None]
    density = jnp.sum(pops, axis=0)
    flux = jnp.dot(speeds.T, pops, precision=precise)
    velocity = flux / density[None, :]
    tilted = weights * jnp.exp(jnp.dot(speeds, velocity, precision=precise) / theta)
    equil = density[None, :] * tilted / jnp.sum(tilted, axis=0)[None, :]
    delta = equil - pops
    floored = jnp.maximum(pops, FLOOR * weights)
    excess = jnp.max(-delta / floored, axis=0)
    ceiling = 0.95 / jnp.maximum(excess, 0.2375)
    curvature = jnp.sum(delta * delta / floored, axis=0) + 1e-6
    start_entropy = jnp.sum(floored * jnp.log(floored / weights), axis=0)
    alpha = jnp.full(density.shape, 2.0, jnp.float32)
    for turn in range(3):
        path = jnp.maximum(pops + alpha[None, :] * delta, FLOOR * weights)
        logs = jnp.log(path / weights)
        value = jnp.sum(path * logs, axis=0) - start_entropy
        slope = jnp.sum(delta * logs, axis=0)
        alpha = jnp.minimum(jnp.maximum(alpha - value / jnp.maximum(slope, 0.25 * curvature), 1.0), ceiling)
    post = pops + (alpha * beta)[None, :] * delta
    wall = weights * density[None, :]
    return jnp.where(solid[None, :] == 1, wall, post)


def stream(post):
    offsets = lattice()[0]
    moved = []
    for index in range(post.shape[0]):
        shift = (int(offsets[index, 0]), int(offsets[index, 1]), int(offsets[index, 2]))
        moved.append(jnp.roll(post[index], shift, axis=(0, 1, 2)))
    return jnp.stack(moved)


def substep(pops, solid, beta):
    stacked = jnp.moveaxis(pops.reshape(pops.shape[0], pops.shape[1], -1), 1, 0)
    walls = solid.reshape(solid.shape[0], -1)
    post = lax.map(lambda item: collide(item[0], item[1], beta), (stacked, walls))
    post = jnp.moveaxis(post, 0, 1).reshape(pops.shape)
    return stream(post)


def interface(target, source, recv, owners, wanted, scale):
    basis, rebuild = hermite_tables()
    across, along, count = wanted.shape
    column = jnp.arange(across, dtype=jnp.int32)[:, None, None]
    row = jnp.arange(along, dtype=jnp.int32)[None, :, None]
    owner_rows = owners[..., 0]
    src_x = column * CX + wanted // CY
    src_y = owner_rows * CY + wanted % CY
    picked = source[:, src_x, src_y, :]
    velocities = picked.shape[0]
    depth = picked.shape[-1]
    flat = picked.reshape(velocities, -1, depth)
    moments = jnp.einsum("nq,qtz->tnz", basis, flat, precision=precise)
    rebuilt = reconstruct(moments, scale)
    fresh = jnp.moveaxis(rebuilt, 1, 0).reshape(velocities, across, along, count, depth)
    targets = recv[..., :count]
    dst_x = column * CX + targets // CY
    dst_y = row * CY + targets % CY
    return target.at[:, dst_x, dst_y, :].set(fresh)


def reference(populations, solid_mask, recv_tiles, owner_gy, owner_tiles):
    coarse = interface(populations[0], populations[1], recv_tiles[0], owner_gy[0], owner_tiles[0], SCALE_COARSE)
    fine = interface(populations[1], populations[0], recv_tiles[1], owner_gy[1], owner_tiles[1], SCALE_FINE)
    coarse = substep(coarse, solid_mask[0], BETA_COARSE)
    fine = substep(fine, solid_mask[1], BETA_FINE)
    fine = substep(fine, solid_mask[1], BETA_FINE)
    return jnp.stack([coarse, fine])
```

```python
import functools
import jax
import jax.numpy as jnp
import numpy as np
from jax import lax
from jax.experimental import pallas as pl
from jax.experimental.pallas import tpu as pltpu
from jax.sharding import PartitionSpec as P


CAP = 2
FLOOR = 0.05
BETA_COARSE = 0.9
BETA_FINE = 0.8
SCALE_FINE = 0.5
SCALE_COARSE = 1.5
WIDTH = 4
TILES = 16
LANES = 128


def lattice():
    shells = [
        (0, 0, 0),
        (0, 0, 1),
        (0, 1, 1),
        (1, 1, 1),
        (0, 0, 2),
        (0, 2, 2),
        (2, 2, 2),
        (0, 0, 3),
        (0, 1, 2),
        (1, 1, 2),
    ]
    vectors = []
    for first in range(-3, 4):
        for second in range(-3, 4):
            for third in range(-3, 4):
                if tuple(sorted((abs(first), abs(second), abs(third)))) in shells:
                    vectors.append((first, second, third))
    offsets = np.array(vectors)
    speeds = offsets * 1.0
    raw = np.exp(-0.5 * np.sum(speeds * speeds, axis=1))
    total = np.sum(raw)
    weights = raw / total
    theta = float(np.sum(weights * speeds[:, 0] * speeds[:, 0]))
    return vectors, speeds, weights, theta, float(total)


VECTORS, SPEEDS, WEIGHTS, THETA, TOTAL = lattice()
Q = len(VECTORS)
ROWS = Q * TILES
INDEX = {v: i for i, v in enumerate(VECTORS)}
PAIRS = [(a, b) for a in range(3) for b in range(a, 3)]
TRIPLES = [(a, b, c) for a in range(3) for b in range(a, 3) for c in range(b, 3)]
MOMENTS = 1 + 3 + len(PAIRS) + len(TRIPLES)
GROUPS = {}
for _i, (_x, _y, _z) in enumerate(VECTORS):
    GROUPS.setdefault((_x, _y), []).append((_z, _i))


def norms():
    rows = [np.ones(Q)]
    for a in range(3):
        rows.append(SPEEDS[:, a])
    for a, b in PAIRS:
        rows.append(SPEEDS[:, a] * SPEEDS[:, b] - THETA * float(a == b))
    for a, b, c in TRIPLES:
        rows.append(
            SPEEDS[:, a] * SPEEDS[:, b] * SPEEDS[:, c]
            - THETA
            * (
                SPEEDS[:, a] * float(b == c)
                + SPEEDS[:, b] * float(a == c)
                + SPEEDS[:, c] * float(a == b)
            )
        )
    basis = np.stack(rows)
    return (basis * basis) @ WEIGHTS


NORMS = norms()


def face_layout(axis):
    sides = {}
    for sign in (1, -1):
        order = [i for n in (2, 1, 3) for i in range(Q) if VECTORS[i][axis] == sign * n]
        place, at = {}, 0
        for i in order:
            place[i] = at
            at += abs(VECTORS[i][axis])
        sides[sign] = (place, at)
    return sides


FACE_X = face_layout(0)
FACE_Y = face_layout(1)
FACE_ROWS = FACE_X[1][1] * WIDTH


def scaled(k, value):
    return value if k == 1 else value * float(k)


def combine(terms):
    total = None
    for k, value in terms:
        if k == 0:
            continue
        if total is None:
            total = scaled(k, value)
        elif k > 0:
            total = total + scaled(k, value)
        else:
            total = total - scaled(-k, value)
    return total


def tree(values):
    values = list(values)
    while len(values) > 1:
        values = [
            values[i] + values[i + 1] if i + 1 < len(values) else values[i]
            for i in range(0, len(values), 2)
        ]
    return values[0]


class Sums:
    def __init__(self, parts=4):
        self.parts = [None] * parts
        self.turn = 0

    def add(self, value):
        k = self.turn % len(self.parts)
        self.turn += 1
        self.parts[k] = value if self.parts[k] is None else self.parts[k] + value

    def total(self):
        return tree([p for p in self.parts if p is not None])


def half_rows(i, half):
    return pl.ds(pl.multiple_of(half * 8 + i * TILES, 8), 8)


def request_tables(owner_ref, wanted_ref, target_ref, ask_ref, pick_ref):
    own = owner_ref[...]
    count = own.shape[1]
    sub = lax.broadcasted_iota(jnp.int32, (count, count), 0)
    lane = lax.broadcasted_iota(jnp.int32, (count, count), 1)

    def down(row):
        return jnp.sum(
            jnp.where(sub == lane, jnp.broadcast_to(row, (count, count)), 0), axis=1, keepdims=True
        )

    same = jnp.where(
        jnp.logical_and(jnp.broadcast_to(own, (count, count)) == down(own), sub < lane), 1, 0
    )
    slot = own * CAP + jnp.sum(same, axis=0, keepdims=True)
    width = ask_ref.shape[0]
    by_slot = jnp.where(
        lax.broadcasted_iota(jnp.int32, (width, count), 0) == jnp.broadcast_to(slot, (width, count)),
        1.0,
        0.0,
    )
    wide = lax.broadcasted_iota(jnp.int32, (count, LANES), 1)
    tiles = jnp.where(wide == down(wanted_ref[...]), 1.0, 0.0)
    ask_ref[...] = jnp.dot(by_slot, tiles, preferred_element_type=jnp.float32)
    by_target = jnp.where(sub == jnp.broadcast_to(target_ref[...], (count, count)), 1.0, 0.0)
    slots = jnp.where(wide == down(slot), 1.0, 0.0)
    pick_ref[...] = jnp.dot(by_target, slots, preferred_element_type=jnp.float32)


def moments_kernel(pops_ref, owner_ref, wanted_ref, target_ref, mom_ref, ask_ref, pick_ref):
    request_tables(owner_ref, wanted_ref, target_ref, ask_ref, pick_ref)

    def one(half, carry):
        raw = {}

        def put(key, k, value):
            if k == 0:
                return
            old = raw.get(key)
            term = scaled(abs(k), value)
            if old is None:
                raw[key] = term if k > 0 else -term
            else:
                raw[key] = old + term if k > 0 else old - term

        for x in range(-3, 4):
            inner = {}
            for y in range(-3, 4):
                if (x, y) not in GROUPS:
                    continue
                f = {z: pops_ref[half_rows(i, half), :] for z, i in GROUPS[(x, y)]}
                even = {k: f[k] + f[-k] for k in (1, 2, 3) if k in f}
                odd = {k: f[k] - f[-k] for k in (1, 2, 3) if k in f}
                sums = [
                    combine([(1, f[0])] + [(1, v) for v in even.values()]),
                    combine([(k, v) for k, v in odd.items()]),
                    combine([(k * k, v) for k, v in even.items()]),
                    combine([(k * k * k, v) for k, v in odd.items()]),
                ]
                for c in range(4):
                    if sums[c] is None:
                        continue
                    for b in range(4 - c):
                        k = y**b
                        if k:
                            inner.setdefault((b, c), []).append((k, sums[c]))
            for (b, c), terms in inner.items():
                terms.sort(key=lambda t: -t[0])
                value = combine(terms) if terms[0][0] > 0 else -combine([(-k, v) for k, v in terms])
                for a in range(4 - b - c):
                    put((a, b, c), x**a, value)
        out = [raw[(0, 0, 0)], raw[(1, 0, 0)], raw[(0, 1, 0)], raw[(0, 0, 1)]]

        def power(*axes):
            return tuple(sum(1 for a in axes if a == d) for d in range(3))

        for a, b in PAIRS:
            value = raw[power(a, b)]
            out.append(value - THETA * out[0] if a == b else value)
        for a, b, c in TRIPLES:
            value = raw[power(a, b, c)]
            if a == b == c:
                value = value - (3.0 * THETA) * out[1 + a]
            elif a == b:
                value = value - THETA * out[1 + c]
            elif b == c:
                value = value - THETA * out[1 + a]
            out.append(value)
        for n in range(MOMENTS):
            mom_ref[half_rows(n, half), :] = out[n]
        return carry

    lax.fori_loop(0, 2, one, 0)


def pack_kernel(mom_ref, ask_ref, reply_ref):
    ask = ask_ref[:, :TILES]
    width = ask_ref.shape[0]
    step = 4
    for first in range(0, MOMENTS, step):
        block = jnp.concatenate(
            [mom_ref[n * TILES : (n + 1) * TILES, :] for n in range(first, first + step)], axis=1
        )
        chosen = jnp.dot(
            ask, block, precision=lax.Precision.HIGHEST, preferred_element_type=jnp.float32
        )
        for k in range(step):
            reply_ref[pl.ds(first + k, width, stride=MOMENTS), :] = chosen[
                :, k * LANES : (k + 1) * LANES
            ]


def rebuild(col_ref, half, scale, f_ref):
    a = [col_ref[half_rows(n, half), :] for n in range(MOMENTS)]
    rho = a[0]
    inverse = 1.0 / rho
    flux = a[1:4]
    speed = [v * inverse for v in flux]
    b = [a[n] * (1.0 / NORMS[n]) for n in range(4)]
    n = 4
    names = {}
    for first, second in PAIRS:
        eq = flux[first] * speed[second]
        names[(first, second)] = (eq + scale * (a[n] - eq)) * (1.0 / NORMS[n])
        n += 1
    for first, second, third in TRIPLES:
        eq = flux[first] * speed[second] * speed[third]
        names[(first, second, third)] = (eq + scale * (a[n] - eq)) * (1.0 / NORMS[n])
        n += 1
    k0 = b[0] - THETA * (names[(0, 0)] + names[(1, 1)] + names[(2, 2)])
    lin = []
    for d in range(3):
        others = [names[tuple(sorted((d, e, e)))] for e in range(3) if e != d]
        lin.append(b[1 + d] - THETA * (3.0 * names[(d, d, d)] + (others[0] + others[1])))
    cubes = {k: names[(2, 2, 2)] * float(k**3) for k in (1, 2, 3)}

    def horner(k, parts):
        value = parts[-1]
        for part in parts[-2::-1]:
            if k == 0:
                value = part
            elif k == 1:
                value = part + value
            elif k == -1:
                value = part - value
            else:
                value = part + float(k) * value
        return value

    for x in range(-3, 4):
        q = [
            horner(x, [k0, lin[0], names[(0, 0)], names[(0, 0, 0)]]),
            horner(x, [lin[1], names[(0, 1)], names[(0, 0, 1)]]),
            horner(x, [names[(1, 1)], names[(0, 1, 1)]]),
            names[(1, 1, 1)],
        ]
        r = [
            horner(x, [lin[2], names[(0, 2)], names[(0, 0, 2)]]),
            horner(x, [names[(1, 2)], names[(0, 1, 2)]]),
            names[(1, 1, 2)],
        ]
        s = [horner(x, [names[(2, 2)], names[(0, 2, 2)]]), names[(1, 2, 2)]]
        for y in range(-3, 4):
            if (x, y) not in GROUPS:
                continue
            place = dict(GROUPS[(x, y)])
            p0, p1, p2 = horner(y, q), horner(y, r), horner(y, s)
            f_ref[half_rows(place[0], half), :] = p0
            for k in (1, 2, 3):
                if k in place:
                    even = p0 + scaled(k * k, p2)
                    odd = scaled(k, p1) + cubes[k]
                    f_ref[half_rows(place[k], half), :] = even + odd
                    f_ref[half_rows(place[-k], half), :] = even - odd


def collide(f_ref, d_ref, half, solid, beta, own_ref, weighted):
    w = [float(v) for v in WEIGHTS]

    def load(ref, i):
        return ref[half_rows(i, half), :]

    rho_s, flux_s = Sums(), [Sums(2) for _ in range(3)]
    rho_s.add(w[INDEX[(0, 0, 0)]] * load(f_ref, INDEX[(0, 0, 0)]))
    for i, v in enumerate(VECTORS):
        opposite = INDEX[tuple(-c for c in v)]
        if i >= opposite:
            continue
        plus, minus = load(f_ref, opposite), load(f_ref, i)
        rho_s.add(w[i] * (plus + minus))
        odd = w[i] * (plus - minus)
        for d in range(3):
            k = -v[d]
            if k:
                flux_s[d].add(odd if k == 1 else odd * float(k))
    rho = rho_s.total()
    inverse = 1.0 / rho
    powers, gauss = [], []
    for d in range(3):
        rate = flux_s[d].total() * inverse * (1.0 / THETA)
        up, down = jnp.exp(rate), jnp.exp(-rate)
        one = {0: None, 1: up, -1: down, 2: up * up, -2: down * down}
        one[3], one[-3] = one[2] * up, one[-2] * down
        powers.append(one)
        gauss.append({k: float(np.exp(-0.5 * k * k)) for k in range(-3, 4)})

    def pair_sum(d, k):
        return (powers[d][k] + powers[d][-k]) * gauss[d][k]

    zs = [pair_sum(2, k) for k in (1, 2, 3)]
    upto = {
        (0,): 1.0,
        (0, 1): 1.0 + zs[0],
        (0, 1, 2): 1.0 + zs[0] + zs[1],
        (0, 2): 1.0 + zs[1],
        (0, 1, 2, 3): 1.0 + zs[0] + zs[1] + zs[2],
    }
    xs = [1.0] + [pair_sum(0, k) for k in (1, 2, 3)]
    ys = [1.0] + [pair_sum(1, k) for k in (1, 2, 3)]
    rows = []
    for x in range(4):
        line = []
        for y in range(4):
            if (x, y) not in GROUPS:
                continue
            key = tuple(sorted(z for z, _ in GROUPS[(x, y)] if z >= 0))
            line.append(ys[y] * upto[key])
        rows.append(xs[x] * functools.reduce(lambda p, q: p + q, line))
    norm = functools.reduce(lambda p, q: p + q, rows)
    factor = rho * float(TOTAL) / norm

    least, curve, start = None, Sums(), Sums()
    for x in range(-3, 4):
        base = factor if x == 0 else factor * powers[0][x]
        for y in range(-3, 4):
            if (x, y) not in GROUPS:
                continue
            plane = base if y == 0 else base * powers[1][y]
            for z, i in GROUPS[(x, y)]:
                f = load(f_ref, i)
                equil = plane if z == 0 else plane * powers[2][z]
                delta = equil - f
                d_ref[half_rows(i, half), :] = delta
                floored = jnp.maximum(f, FLOOR)
                ratio = delta / floored
                least = ratio if least is None else jnp.minimum(least, ratio)
                curve.add(w[i] * (delta * ratio))
                start.add(w[i] * (floored * jnp.log(floored)))
    ceiling = 0.95 / jnp.maximum(-least, 0.2375)
    bound = 0.25 * (curve.total() + 1e-6)
    entropy = start.total()

    def newton(turn, alpha):
        value, slope = Sums(), Sums()
        for i in range(Q):
            delta = load(d_ref, i)
            path = jnp.maximum(load(f_ref, i) + alpha * delta, FLOOR)
            logs = w[i] * jnp.log(path)
            value.add(path * logs)
            slope.add(delta * logs)
        change = (value.total() - entropy) / jnp.maximum(slope.total(), bound)
        return jnp.minimum(jnp.maximum(alpha - change, 1.0), ceiling)

    alpha = lax.fori_loop(0, 3, newton, jnp.full(rho.shape, 2.0, jnp.float32))
    step = alpha * beta
    for i, v in enumerate(VECTORS):
        post = jnp.where(solid == 1, rho, load(f_ref, i) + step * load(d_ref, i))
        if weighted:
            post = post * w[i]
        if v[2]:
            post = pltpu.roll(post, v[2] % LANES, 1)
        own_ref[half_rows(i, half), :] = post


def send_x(own_ref, xp_ref, xm_ref):
    for sign, out_ref in ((1, xp_ref), (-1, xm_ref)):
        place, _ = FACE_X[sign]
        for i, at in place.items():
            n = abs(VECTORS[i][0]) * WIDTH
            first = i * TILES + (TILES - n if sign > 0 else 0)
            out_ref[at * WIDTH : at * WIDTH + n, :] = own_ref[first : first + n, :]


def rebuild_kernel(reply_ref, pick_ref, solid_ref, own_ref, xp_ref, xm_ref, col_ref, f_ref, d_ref):
    level = lax.axis_index("level")
    scale = jnp.where(level == 1, SCALE_FINE, SCALE_COARSE)
    beta = jnp.where(level == 1, BETA_FINE, BETA_COARSE)
    width = reply_ref.shape[0] // MOMENTS
    pick = pick_ref[:, :width]
    step = 4
    for first in range(0, MOMENTS, step):
        block = jnp.concatenate(
            [
                reply_ref[pl.ds(n, width, stride=MOMENTS), :]
                for n in range(first, first + step)
            ],
            axis=1,
        )
        chosen = jnp.dot(
            pick, block, precision=lax.Precision.HIGHEST, preferred_element_type=jnp.float32
        )
        for k in range(step):
            n = first + k
            col_ref[n * TILES : (n + 1) * TILES, :] = chosen[:, k * LANES : (k + 1) * LANES]

    def one(half, carry):
        rebuild(col_ref, half, scale, f_ref)
        solid = solid_ref[pl.ds(pl.multiple_of(half * 8, 8), 8), :]
        collide(f_ref, d_ref, half, solid, beta, own_ref, False)
        return carry

    lax.fori_loop(0, 2, one, 0)
    send_x(own_ref, xp_ref, xm_ref)


def copy_rows(src_ref, dst_ref):
    def step(k, carry):
        rows = pl.ds(pl.multiple_of(k * TILES, 8), TILES)
        dst_ref[rows, :] = src_ref[rows, :]
        return carry

    lax.fori_loop(0, Q, step, 0)


def shift_x(own_ref, low_ref, high_ref, x_ref, yp_ref, ym_ref):
    for i, v in enumerate(VECTORS):
        n = abs(v[0]) * WIDTH
        base = i * TILES
        if n == 0:
            x_ref[base : base + TILES, :] = own_ref[base : base + TILES, :]
        elif v[0] > 0:
            at = FACE_X[1][0][i] * WIDTH
            x_ref[base + n : base + TILES, :] = own_ref[base : base + TILES - n, :]
            x_ref[base : base + n, :] = low_ref[at : at + n, :]
        else:
            at = FACE_X[-1][0][i] * WIDTH
            x_ref[base : base + TILES - n, :] = own_ref[base + n : base + TILES, :]
            x_ref[base + TILES - n : base + TILES, :] = high_ref[at : at + n, :]
    for sign, out_ref in ((1, yp_ref), (-1, ym_ref)):
        place, _ = FACE_Y[sign]
        for i, at in place.items():
            n = abs(VECTORS[i][1])
            for k in range(n):
                row = WIDTH - n + k if sign > 0 else k
                out_ref[(at + k) * WIDTH : (at + k + 1) * WIDTH, :] = x_ref[
                    pl.ds(i * TILES + row, WIDTH, stride=WIDTH), :
                ]


def shift_kernel(last, own_ref, low_ref, high_ref, x_ref, yp_ref, ym_ref):
    if not last:
        shift_x(own_ref, low_ref, high_ref, x_ref, yp_ref, ym_ref)
        return
    fine = lax.axis_index("level") == 1

    @pl.when(fine)
    def _():
        shift_x(own_ref, low_ref, high_ref, x_ref, yp_ref, ym_ref)

    @pl.when(jnp.logical_not(fine))
    def _():
        copy_rows(own_ref, x_ref)
        yp_ref[...] = jnp.zeros_like(yp_ref)
        ym_ref[...] = jnp.zeros_like(ym_ref)


def assemble(x_ref, low_ref, high_ref, out_ref):
    for i, v in enumerate(VECTORS):
        base = i * TILES
        out_ref[base : base + TILES, :] = x_ref[base - v[1] : base - v[1] + TILES, :]
        n = abs(v[1])
        for k in range(n):
            if v[1] > 0:
                src_ref, at, row = low_ref, FACE_Y[1][0][i] + k, k
            else:
                src_ref, at, row = high_ref, FACE_Y[-1][0][i] + k, WIDTH - n + k
            out_ref[pl.ds(base + row, WIDTH, stride=WIDTH), :] = src_ref[
                at * WIDTH : (at + 1) * WIDTH, :
            ]


def second_kernel(x_ref, low_ref, high_ref, solid_ref, own_ref, xp_ref, xm_ref, f_ref, d_ref):
    fine = lax.axis_index("level") == 1
    assemble(x_ref, low_ref, high_ref, f_ref)

    @pl.when(fine)
    def _():
        def one(half, carry):
            solid = solid_ref[pl.ds(pl.multiple_of(half * 8, 8), 8), :]
            collide(f_ref, d_ref, half, solid, BETA_FINE, own_ref, True)
            return carry

        lax.fori_loop(0, 2, one, 0)
        send_x(own_ref, xp_ref, xm_ref)

    @pl.when(jnp.logical_not(fine))
    def _():
        for i in range(Q):
            rows = slice(i * TILES, (i + 1) * TILES)
            own_ref[rows, :] = f_ref[rows, :] * float(WEIGHTS[i])
        xp_ref[...] = jnp.zeros_like(xp_ref)
        xm_ref[...] = jnp.zeros_like(xm_ref)


def last_kernel(x_ref, low_ref, high_ref, out_ref):
    fine = lax.axis_index("level") == 1

    @pl.when(fine)
    def _():
        assemble(x_ref, low_ref, high_ref, out_ref)

    @pl.when(jnp.logical_not(fine))
    def _():
        copy_rows(x_ref, out_ref)


def call(kernel, outs, args, name, scratch=(), flops=4_000_000):
    whole = pl.BlockSpec(memory_space=pltpu.VMEM)
    shapes = [jax.ShapeDtypeStruct((rows, LANES), jnp.float32) for rows in outs]
    moved = sum(int(np.prod(s.shape)) for s in shapes) + sum(int(np.prod(a.shape)) for a in args)
    return pl.pallas_call(
        kernel,
        out_shape=shapes,
        in_specs=[whole] * len(args),
        out_specs=[whole] * len(shapes),
        scratch_shapes=[pltpu.VMEM((rows, LANES), jnp.float32) for rows in scratch],
        compiler_params=pltpu.CompilerParams(vmem_limit_bytes=24 << 20),
        cost_estimate=pl.CostEstimate(flops=flops, bytes_accessed=4 * moved, transcendentals=0),
        name=name,
    )(*args)


def both_ways(up, down, axis):
    count = lax.axis_size(axis)
    low = lax.ppermute(up, axis, [(i, (i + 1) % count) for i in range(count)])
    high = lax.ppermute(down, axis, [((i + 1) % count, i) for i in range(count)])
    return low, high


def shards(populations, solid_mask, recv_tiles, owner_gy, owner_tiles):
    peers = lax.axis_size("gy")
    count = owner_tiles.shape[-1]
    pops = populations.reshape(ROWS, LANES)
    solid = solid_mask.reshape(TILES, LANES)
    owners = owner_gy.reshape(1, count)
    wanted = owner_tiles.reshape(1, count)
    targets = recv_tiles.reshape(1, count)
    slots = peers * CAP
    mom, ask, pick = call(
        moments_kernel,
        [MOMENTS * TILES, slots, TILES],
        [pops, owners, wanted, targets],
        "moments",
    )
    crossed = lax.ppermute(mom, "level", [(0, 1), (1, 0)])
    asked = lax.all_to_all(
        ask.reshape(peers, CAP, LANES), "gy", split_axis=0, concat_axis=0, tiled=True
    ).reshape(slots, LANES)
    (answer,) = call(pack_kernel, [slots * MOMENTS], [crossed, asked], "pack")
    reply = lax.all_to_all(
        answer.reshape(peers, CAP * MOMENTS, LANES), "gy", split_axis=0, concat_axis=0, tiled=True
    ).reshape(slots * MOMENTS, LANES)
    faces = [ROWS, FACE_ROWS, FACE_ROWS]
    own, xp, xm = call(
        rebuild_kernel, faces, [reply, pick, solid], "collide1", [MOMENTS * TILES, ROWS, ROWS]
    )
    low, high = both_ways(xp, xm, "gx")
    moved, yp, ym = call(
        functools.partial(shift_kernel, False), faces, [own, low, high], "shift1"
    )
    low, high = both_ways(yp, ym, "gy")
    own, xp, xm = call(second_kernel, faces, [moved, low, high, solid], "collide2", [ROWS, ROWS])
    low, high = both_ways(xp, xm, "gx")
    moved, yp, ym = call(functools.partial(shift_kernel, True), faces, [own, low, high], "shift2")
    low, high = both_ways(yp, ym, "gy")
    (out,) = call(last_kernel, [ROWS], [moved, low, high], "last")
    return out.reshape(populations.shape)


def solution(mesh):
    placed = (
        P("level", None, "gx", "gy", None),
        P("level", "gx", "gy", None),
        P("level", "gx", "gy", None),
        P("level", "gx", "gy", None, None),
        P("level", "gx", "gy", None),
    )
    return jax.shard_map(
        shards,
        mesh=mesh,
        in_specs=placed,
        out_specs=P("level", None, "gx", "gy", None),
        check_vma=False,
    )
```

```python
import functools
import jax
import jax.numpy as jnp
import numpy as np
from jax import lax
from jax.experimental import pallas as pl
from jax.experimental.pallas import tpu as pltpu
from jax.sharding import PartitionSpec as P


CAP = 2
FLOOR = 0.05
BETA_COARSE = 0.9
BETA_FINE = 0.8
SCALE_FINE = 0.5
SCALE_COARSE = 1.5
WIDTH = 4
TILES = 16
LANES = 128


def lattice():
    shells = [
        (0, 0, 0),
        (0, 0, 1),
        (0, 1, 1),
        (1, 1, 1),
        (0, 0, 2),
        (0, 2, 2),
        (2, 2, 2),
        (0, 0, 3),
        (0, 1, 2),
        (1, 1, 2),
    ]
    vectors = []
    for first in range(-3, 4):
        for second in range(-3, 4):
            for third in range(-3, 4):
                if tuple(sorted((abs(first), abs(second), abs(third)))) in shells:
                    vectors.append((first, second, third))
    offsets = np.array(vectors)
    speeds = offsets * 1.0
    raw = np.exp(-0.5 * np.sum(speeds * speeds, axis=1))
    total = np.sum(raw)
    weights = raw / total
    theta = float(np.sum(weights * speeds[:, 0] * speeds[:, 0]))
    return vectors, speeds, weights, theta, float(total)


VECTORS, SPEEDS, WEIGHTS, THETA, TOTAL = lattice()
Q = len(VECTORS)
ROWS = Q * TILES
INDEX = {v: i for i, v in enumerate(VECTORS)}
PAIRS = [(a, b) for a in range(3) for b in range(a, 3)]
TRIPLES = [(a, b, c) for a in range(3) for b in range(a, 3) for c in range(b, 3)]
MOMENTS = 1 + 3 + len(PAIRS) + len(TRIPLES)
GROUPS = {}
for _i, (_x, _y, _z) in enumerate(VECTORS):
    GROUPS.setdefault((_x, _y), []).append((_z, _i))


def norms():
    rows = [np.ones(Q)]
    for a in range(3):
        rows.append(SPEEDS[:, a])
    for a, b in PAIRS:
        rows.append(SPEEDS[:, a] * SPEEDS[:, b] - THETA * float(a == b))
    for a, b, c in TRIPLES:
        rows.append(
            SPEEDS[:, a] * SPEEDS[:, b] * SPEEDS[:, c]
            - THETA
            * (
                SPEEDS[:, a] * float(b == c)
                + SPEEDS[:, b] * float(a == c)
                + SPEEDS[:, c] * float(a == b)
            )
        )
    basis = np.stack(rows)
    return (basis * basis) @ WEIGHTS


NORMS = norms()


def face_layout(axis):
    sides = {}
    for sign in (1, -1):
        order = [i for n in (2, 1, 3) for i in range(Q) if VECTORS[i][axis] == sign * n]
        place, at = {}, 0
        for i in order:
            place[i] = at
            at += abs(VECTORS[i][axis])
        sides[sign] = (place, at)
    return sides


FACE_X = face_layout(0)
FACE_Y = face_layout(1)
FACE_ROWS = FACE_X[1][1] * WIDTH


def scaled(k, value):
    return value if k == 1 else value * float(k)


def combine(terms):
    total = None
    for k, value in terms:
        if k == 0:
            continue
        if total is None:
            total = scaled(k, value)
        elif k > 0:
            total = total + scaled(k, value)
        else:
            total = total - scaled(-k, value)
    return total


def tree(values):
    values = list(values)
    while len(values) > 1:
        values = [
            values[i] + values[i + 1] if i + 1 < len(values) else values[i]
            for i in range(0, len(values), 2)
        ]
    return values[0]


class Sums:
    def __init__(self, parts=4):
        self.parts = [None] * parts
        self.turn = 0

    def add(self, value):
        k = self.turn % len(self.parts)
        self.turn += 1
        self.parts[k] = value if self.parts[k] is None else self.parts[k] + value

    def total(self):
        return tree([p for p in self.parts if p is not None])


def half_rows(i, half):
    return pl.ds(pl.multiple_of(half * 8 + i * TILES, 8), 8)


def request_tables(owner_ref, wanted_ref, target_ref, ask_ref, pick_ref):
    own = owner_ref[...]
    count = own.shape[1]
    sub = lax.broadcasted_iota(jnp.int32, (count, count), 0)
    lane = lax.broadcasted_iota(jnp.int32, (count, count), 1)

    def down(row):
        return jnp.sum(
            jnp.where(sub == lane, jnp.broadcast_to(row, (count, count)), 0), axis=1, keepdims=True
        )

    same = jnp.where(
        jnp.logical_and(jnp.broadcast_to(own, (count, count)) == down(own), sub < lane), 1, 0
    )
    slot = own * CAP + jnp.sum(same, axis=0, keepdims=True)
    width = ask_ref.shape[0]
    by_slot = jnp.where(
        lax.broadcasted_iota(jnp.int32, (width, count), 0) == jnp.broadcast_to(slot, (width, count)),
        1.0,
        0.0,
    )
    wide = lax.broadcasted_iota(jnp.int32, (count, LANES), 1)
    tiles = jnp.where(wide == down(wanted_ref[...]), 1.0, 0.0)
    ask_ref[...] = jnp.dot(by_slot, tiles, preferred_element_type=jnp.float32)
    by_target = jnp.where(sub == jnp.broadcast_to(target_ref[...], (count, count)), 1.0, 0.0)
    slots = jnp.where(wide == down(slot), 1.0, 0.0)
    pick_ref[...] = jnp.dot(by_target, slots, preferred_element_type=jnp.float32)


def moments_kernel(pops_ref, mom_ref):
    def one(half, carry):
        raw = {}

        def put(key, k, value):
            if k == 0:
                return
            old = raw.get(key)
            term = scaled(abs(k), value)
            if old is None:
                raw[key] = term if k > 0 else -term
            else:
                raw[key] = old + term if k > 0 else old - term

        for x in range(-3, 4):
            inner = {}
            for y in range(-3, 4):
                if (x, y) not in GROUPS:
                    continue
                f = {z: pops_ref[half_rows(i, half), :] for z, i in GROUPS[(x, y)]}
                even = {k: f[k] + f[-k] for k in (1, 2, 3) if k in f}
                odd = {k: f[k] - f[-k] for k in (1, 2, 3) if k in f}
                sums = [
                    combine([(1, f[0])] + [(1, v) for v in even.values()]),
                    combine([(k, v) for k, v in odd.items()]),
                    combine([(k * k, v) for k, v in even.items()]),
                    combine([(k * k * k, v) for k, v in odd.items()]),
                ]
                for c in range(4):
                    if sums[c] is None:
                        continue
                    for b in range(4 - c):
                        k = y**b
                        if k:
                            inner.setdefault((b, c), []).append((k, sums[c]))
            for (b, c), terms in inner.items():
                terms.sort(key=lambda t: -t[0])
                value = combine(terms) if terms[0][0] > 0 else -combine([(-k, v) for k, v in terms])
                for a in range(4 - b - c):
                    put((a, b, c), x**a, value)
        out = [raw[(0, 0, 0)], raw[(1, 0, 0)], raw[(0, 1, 0)], raw[(0, 0, 1)]]

        def power(*axes):
            return tuple(sum(1 for a in axes if a == d) for d in range(3))

        for a, b in PAIRS:
            value = raw[power(a, b)]
            out.append(value - THETA * out[0] if a == b else value)
        for a, b, c in TRIPLES:
            value = raw[power(a, b, c)]
            if a == b == c:
                value = value - (3.0 * THETA) * out[1 + a]
            elif a == b:
                value = value - THETA * out[1 + c]
            elif b == c:
                value = value - THETA * out[1 + a]
            out.append(value)
        for n in range(MOMENTS):
            mom_ref[half_rows(n, half), :] = out[n]
        return carry

    lax.fori_loop(0, 2, one, 0)


def pack_kernel(mom_ref, ask_ref, reply_ref):
    ask = ask_ref[:, :TILES]
    width = ask_ref.shape[0]
    step = 4
    for first in range(0, MOMENTS, step):
        block = jnp.concatenate(
            [mom_ref[n * TILES : (n + 1) * TILES, :] for n in range(first, first + step)], axis=1
        )
        chosen = jnp.dot(
            ask, block, precision=lax.Precision.HIGHEST, preferred_element_type=jnp.float32
        )
        for k in range(step):
            reply_ref[pl.ds(first + k, width, stride=MOMENTS), :] = chosen[
                :, k * LANES : (k + 1) * LANES
            ]


def rebuild(col_ref, half, scale, f_ref):
    a = [col_ref[half_rows(n, half), :] for n in range(MOMENTS)]
    rho = a[0]
    inverse = 1.0 / rho
    flux = a[1:4]
    speed = [v * inverse for v in flux]
    b = [a[n] * (1.0 / NORMS[n]) for n in range(4)]
    n = 4
    names = {}
    for first, second in PAIRS:
        eq = flux[first] * speed[second]
        names[(first, second)] = (eq + scale * (a[n] - eq)) * (1.0 / NORMS[n])
        n += 1
    for first, second, third in TRIPLES:
        eq = flux[first] * speed[second] * speed[third]
        names[(first, second, third)] = (eq + scale * (a[n] - eq)) * (1.0 / NORMS[n])
        n += 1
    k0 = b[0] - THETA * (names[(0, 0)] + names[(1, 1)] + names[(2, 2)])
    lin = []
    for d in range(3):
        others = [names[tuple(sorted((d, e, e)))] for e in range(3) if e != d]
        lin.append(b[1 + d] - THETA * (3.0 * names[(d, d, d)] + (others[0] + others[1])))
    cubes = {k: names[(2, 2, 2)] * float(k**3) for k in (1, 2, 3)}

    def horner(k, parts):
        value = parts[-1]
        for part in parts[-2::-1]:
            if k == 0:
                value = part
            elif k == 1:
                value = part + value
            elif k == -1:
                value = part - value
            else:
                value = part + float(k) * value
        return value

    for x in range(-3, 4):
        q = [
            horner(x, [k0, lin[0], names[(0, 0)], names[(0, 0, 0)]]),
            horner(x, [lin[1], names[(0, 1)], names[(0, 0, 1)]]),
            horner(x, [names[(1, 1)], names[(0, 1, 1)]]),
            names[(1, 1, 1)],
        ]
        r = [
            horner(x, [lin[2], names[(0, 2)], names[(0, 0, 2)]]),
            horner(x, [names[(1, 2)], names[(0, 1, 2)]]),
            names[(1, 1, 2)],
        ]
        s = [horner(x, [names[(2, 2)], names[(0, 2, 2)]]), names[(1, 2, 2)]]
        for y in range(-3, 4):
            if (x, y) not in GROUPS:
                continue
            place = dict(GROUPS[(x, y)])
            p0, p1, p2 = horner(y, q), horner(y, r), horner(y, s)
            f_ref[half_rows(place[0], half), :] = p0
            for k in (1, 2, 3):
                if k in place:
                    even = p0 + scaled(k * k, p2)
                    odd = scaled(k, p1) + cubes[k]
                    f_ref[half_rows(place[k], half), :] = even + odd
                    f_ref[half_rows(place[-k], half), :] = even - odd


def collide(f_ref, d_ref, half, solid, beta, own_ref, weighted):
    w = [float(v) for v in WEIGHTS]

    def load(ref, i):
        return ref[half_rows(i, half), :]

    rho_s, flux_s = Sums(), [Sums(2) for _ in range(3)]
    rho_s.add(w[INDEX[(0, 0, 0)]] * load(f_ref, INDEX[(0, 0, 0)]))
    for i, v in enumerate(VECTORS):
        opposite = INDEX[tuple(-c for c in v)]
        if i >= opposite:
            continue
        plus, minus = load(f_ref, opposite), load(f_ref, i)
        rho_s.add(w[i] * (plus + minus))
        odd = w[i] * (plus - minus)
        for d in range(3):
            k = -v[d]
            if k:
                flux_s[d].add(odd if k == 1 else odd * float(k))
    rho = rho_s.total()
    inverse = 1.0 / rho
    powers, gauss = [], []
    for d in range(3):
        rate = flux_s[d].total() * inverse * (1.0 / THETA)
        up, down = jnp.exp(rate), jnp.exp(-rate)
        one = {0: None, 1: up, -1: down, 2: up * up, -2: down * down}
        one[3], one[-3] = one[2] * up, one[-2] * down
        powers.append(one)
        gauss.append({k: float(np.exp(-0.5 * k * k)) for k in range(-3, 4)})

    def pair_sum(d, k):
        return (powers[d][k] + powers[d][-k]) * gauss[d][k]

    zs = [pair_sum(2, k) for k in (1, 2, 3)]
    upto = {
        (0,): 1.0,
        (0, 1): 1.0 + zs[0],
        (0, 1, 2): 1.0 + zs[0] + zs[1],
        (0, 2): 1.0 + zs[1],
        (0, 1, 2, 3): 1.0 + zs[0] + zs[1] + zs[2],
    }
    xs = [1.0] + [pair_sum(0, k) for k in (1, 2, 3)]
    ys = [1.0] + [pair_sum(1, k) for k in (1, 2, 3)]
    rows = []
    for x in range(4):
        line = []
        for y in range(4):
            if (x, y) not in GROUPS:
                continue
            key = tuple(sorted(z for z, _ in GROUPS[(x, y)] if z >= 0))
            line.append(ys[y] * upto[key])
        rows.append(xs[x] * functools.reduce(lambda p, q: p + q, line))
    norm = functools.reduce(lambda p, q: p + q, rows)
    factor = rho * float(TOTAL) / norm

    least, curve, start = None, Sums(), Sums()
    for x in range(-3, 4):
        base = factor if x == 0 else factor * powers[0][x]
        for y in range(-3, 4):
            if (x, y) not in GROUPS:
                continue
            plane = base if y == 0 else base * powers[1][y]
            for z, i in GROUPS[(x, y)]:
                f = load(f_ref, i)
                equil = plane if z == 0 else plane * powers[2][z]
                delta = equil - f
                d_ref[half_rows(i, half), :] = delta
                floored = jnp.maximum(f, FLOOR)
                ratio = delta / floored
                least = ratio if least is None else jnp.minimum(least, ratio)
                curve.add(w[i] * (delta * ratio))
                start.add(w[i] * (floored * jnp.log(floored)))
    ceiling = 0.95 / jnp.maximum(-least, 0.2375)
    bound = 0.25 * (curve.total() + 1e-6)
    entropy = start.total()

    def newton(turn, alpha):
        value, slope = Sums(), Sums()
        for i in range(Q):
            delta = load(d_ref, i)
            path = jnp.maximum(load(f_ref, i) + alpha * delta, FLOOR)
            logs = w[i] * jnp.log(path)
            value.add(path * logs)
            slope.add(delta * logs)
        change = (value.total() - entropy) / jnp.maximum(slope.total(), bound)
        return jnp.minimum(jnp.maximum(alpha - change, 1.0), ceiling)

    alpha = lax.fori_loop(0, 3, newton, jnp.full(rho.shape, 2.0, jnp.float32))
    step = alpha * beta
    for i, v in enumerate(VECTORS):
        post = jnp.where(solid == 1, rho, load(f_ref, i) + step * load(d_ref, i))
        if weighted:
            post = post * w[i]
        if v[2]:
            post = pltpu.roll(post, v[2] % LANES, 1)
        own_ref[half_rows(i, half), :] = post


def route(axis, odd_ref, even_ref, one_ref, two_ref):
    odd = lax.axis_index(axis) % 2 == 1
    a, b = odd_ref[...], even_ref[...]
    one_ref[...] = jnp.where(odd, a, b)
    two_ref[...] = jnp.where(odd, b, a)


def send_x(own_ref, xa_ref, xb_ref, up_ref, down_ref):
    for sign, out_ref in ((1, up_ref), (-1, down_ref)):
        place, _ = FACE_X[sign]
        for i, at in place.items():
            n = abs(VECTORS[i][0]) * WIDTH
            first = i * TILES + (TILES - n if sign > 0 else 0)
            out_ref[at * WIDTH : at * WIDTH + n, :] = own_ref[first : first + n, :]
    route("gx", up_ref, down_ref, xa_ref, xb_ref)


def rebuild_kernel(
    reply_ref, pick_ref, solid_ref, own_ref, xa_ref, xb_ref, col_ref, f_ref, d_ref, up_ref, down_ref
):
    level = lax.axis_index("level")
    scale = jnp.where(level == 1, SCALE_FINE, SCALE_COARSE)
    beta = jnp.where(level == 1, BETA_FINE, BETA_COARSE)
    width = reply_ref.shape[0] // MOMENTS
    pick = pick_ref[:, :width]
    step = 4
    for first in range(0, MOMENTS, step):
        block = jnp.concatenate(
            [
                reply_ref[pl.ds(n, width, stride=MOMENTS), :]
                for n in range(first, first + step)
            ],
            axis=1,
        )
        chosen = jnp.dot(
            pick, block, precision=lax.Precision.HIGHEST, preferred_element_type=jnp.float32
        )
        for k in range(step):
            n = first + k
            col_ref[n * TILES : (n + 1) * TILES, :] = chosen[:, k * LANES : (k + 1) * LANES]

    def one(half, carry):
        rebuild(col_ref, half, scale, f_ref)
        solid = solid_ref[pl.ds(pl.multiple_of(half * 8, 8), 8), :]
        collide(f_ref, d_ref, half, solid, beta, own_ref, False)
        return carry

    lax.fori_loop(0, 2, one, 0)
    send_x(own_ref, xa_ref, xb_ref, up_ref, down_ref)


def copy_rows(src_ref, dst_ref):
    def step(k, carry):
        rows = pl.ds(pl.multiple_of(k * TILES, 8), TILES)
        dst_ref[rows, :] = src_ref[rows, :]
        return carry

    lax.fori_loop(0, Q, step, 0)


def shift_x(own_ref, xa_ref, xb_ref, x_ref, ya_ref, yb_ref, low_ref, high_ref, up_ref, down_ref):
    route("gx", xb_ref, xa_ref, low_ref, high_ref)
    for i, v in enumerate(VECTORS):
        n = abs(v[0]) * WIDTH
        base = i * TILES
        if n == 0:
            x_ref[base : base + TILES, :] = own_ref[base : base + TILES, :]
        elif v[0] > 0:
            at = FACE_X[1][0][i] * WIDTH
            x_ref[base + n : base + TILES, :] = own_ref[base : base + TILES - n, :]
            x_ref[base : base + n, :] = low_ref[at : at + n, :]
        else:
            at = FACE_X[-1][0][i] * WIDTH
            x_ref[base : base + TILES - n, :] = own_ref[base + n : base + TILES, :]
            x_ref[base + TILES - n : base + TILES, :] = high_ref[at : at + n, :]
    for sign, out_ref in ((1, up_ref), (-1, down_ref)):
        place, _ = FACE_Y[sign]
        for i, at in place.items():
            n = abs(VECTORS[i][1])
            for k in range(n):
                row = WIDTH - n + k if sign > 0 else k
                out_ref[(at + k) * WIDTH : (at + k + 1) * WIDTH, :] = x_ref[
                    pl.ds(i * TILES + row, WIDTH, stride=WIDTH), :
                ]
    route("gy", up_ref, down_ref, ya_ref, yb_ref)


def shift_kernel(last, own_ref, xa_ref, xb_ref, x_ref, ya_ref, yb_ref, *scratch):
    if not last:
        shift_x(own_ref, xa_ref, xb_ref, x_ref, ya_ref, yb_ref, *scratch)
        return
    fine = lax.axis_index("level") == 1

    @pl.when(fine)
    def _():
        shift_x(own_ref, xa_ref, xb_ref, x_ref, ya_ref, yb_ref, *scratch)

    @pl.when(jnp.logical_not(fine))
    def _():
        copy_rows(own_ref, x_ref)
        ya_ref[...] = jnp.zeros_like(ya_ref)
        yb_ref[...] = jnp.zeros_like(yb_ref)


def assemble(x_ref, low_ref, high_ref, out_ref, first=0, last=Q):
    for i in range(first, last):
        v = VECTORS[i]
        base = i * TILES
        out_ref[base : base + TILES, :] = x_ref[base - v[1] : base - v[1] + TILES, :]
        n = abs(v[1])
        for k in range(n):
            if v[1] > 0:
                src_ref, at, row = low_ref, FACE_Y[1][0][i] + k, k
            else:
                src_ref, at, row = high_ref, FACE_Y[-1][0][i] + k, WIDTH - n + k
            out_ref[pl.ds(base + row, WIDTH, stride=WIDTH), :] = src_ref[
                at * WIDTH : (at + 1) * WIDTH, :
            ]


def second_kernel(
    x_ref, ya_ref, yb_ref, solid_ref, own_ref, xa_ref, xb_ref, f_ref, d_ref, low_ref, high_ref
):
    fine = lax.axis_index("level") == 1
    route("gy", yb_ref, ya_ref, low_ref, high_ref)
    assemble(x_ref, low_ref, high_ref, f_ref)

    @pl.when(fine)
    def _():
        def one(half, carry):
            solid = solid_ref[pl.ds(pl.multiple_of(half * 8, 8), 8), :]
            collide(f_ref, d_ref, half, solid, BETA_FINE, own_ref, True)
            return carry

        lax.fori_loop(0, 2, one, 0)
        send_x(own_ref, xa_ref, xb_ref, low_ref, high_ref)

    @pl.when(jnp.logical_not(fine))
    def _():
        for i in range(Q):
            rows = slice(i * TILES, (i + 1) * TILES)
            own_ref[rows, :] = f_ref[rows, :] * float(WEIGHTS[i])
        xa_ref[...] = jnp.zeros_like(xa_ref)
        xb_ref[...] = jnp.zeros_like(xb_ref)


PIECES = [(Q * k // 4, Q * (k + 1) // 4) for k in range(4)]


def last_kernel(x_ref, ya_ref, yb_ref, out_ref, new_ref, low_ref, high_ref, sems):
    fine = lax.axis_index("level") == 1

    def piece(src_ref, k):
        first, last = PIECES[k]
        rows = pl.ds(first * TILES, (last - first) * TILES)
        return pltpu.make_async_copy(src_ref.at[rows, :], out_ref.at[rows, :], sems.at[k])

    @pl.when(fine)
    def _():
        route("gy", yb_ref, ya_ref, low_ref, high_ref)
        for k, (first, last) in enumerate(PIECES):
            assemble(x_ref, low_ref, high_ref, new_ref, first, last)
            piece(new_ref, k).start()
        for k in range(len(PIECES)):
            piece(new_ref, k).wait()

    @pl.when(jnp.logical_not(fine))
    def _():
        for k in range(len(PIECES)):
            piece(x_ref, k).start()
        for k in range(len(PIECES)):
            piece(x_ref, k).wait()


def call(kernel, outs, args, name, scratch=(), flops=4_000_000, far_outs=False, more=()):
    whole = pl.BlockSpec(memory_space=pltpu.VMEM)
    far = pl.BlockSpec(memory_space=pltpu.HBM)
    shapes = [jax.ShapeDtypeStruct((rows, LANES), jnp.float32) for rows in outs]
    moved = sum(int(np.prod(s.shape)) for s in shapes) + sum(int(np.prod(a.shape)) for a in args)
    return pl.pallas_call(
        kernel,
        out_shape=shapes,
        in_specs=[whole] * len(args),
        out_specs=[far if far_outs else whole] * len(shapes),
        scratch_shapes=[pltpu.VMEM((rows, LANES), jnp.float32) for rows in scratch] + list(more),
        compiler_params=pltpu.CompilerParams(vmem_limit_bytes=24 << 20),
        cost_estimate=pl.CostEstimate(flops=flops, bytes_accessed=4 * moved, transcendentals=0),
        name=name,
    )(*args)


def swap_edges(first, second, axis):
    count = lax.axis_size(axis)
    odd = [(i, (i + 1) % count if i % 2 else (i - 1) % count) for i in range(count)]
    even = [(i, i ^ 1) for i in range(count)]
    return lax.ppermute(first, axis, odd), lax.ppermute(second, axis, even)


def shards(populations, solid_mask, recv_tiles, owner_gy, owner_tiles):
    peers = lax.axis_size("gy")
    count = owner_tiles.shape[-1]
    pops = populations.reshape(ROWS, LANES)
    solid = solid_mask.reshape(TILES, LANES)
    owners = owner_gy.reshape(1, count)
    wanted = owner_tiles.reshape(1, count)
    targets = recv_tiles.reshape(1, count)
    slots = peers * CAP
    (mom,) = call(moments_kernel, [MOMENTS * TILES], [pops], "moments")
    ask, pick = call(request_tables, [slots, TILES], [owners, wanted, targets], "requests")
    crossed = lax.ppermute(mom, "level", [(0, 1), (1, 0)])
    asked = lax.all_to_all(
        ask.reshape(peers, CAP, LANES), "gy", split_axis=0, concat_axis=0, tiled=True
    ).reshape(slots, LANES)
    (answer,) = call(pack_kernel, [slots * MOMENTS], [crossed, asked], "pack")
    reply = lax.all_to_all(
        answer.reshape(peers, CAP * MOMENTS, LANES), "gy", split_axis=0, concat_axis=0, tiled=True
    ).reshape(slots * MOMENTS, LANES)
    faces = [ROWS, FACE_ROWS, FACE_ROWS]
    own, xa, xb = call(
        rebuild_kernel,
        faces,
        [reply, pick, solid],
        "collide1",
        [MOMENTS * TILES, ROWS, ROWS] + [FACE_ROWS] * 2,
    )
    first, second = swap_edges(xa, xb, "gx")
    moved, ya, yb = call(
        functools.partial(shift_kernel, False),
        faces,
        [own, first, second],
        "shift1",
        [FACE_ROWS] * 4,
    )
    first, second = swap_edges(ya, yb, "gy")
    own, xa, xb = call(
        second_kernel,
        faces,
        [moved, first, second, solid],
        "collide2",
        [ROWS, ROWS] + [FACE_ROWS] * 2,
    )
    first, second = swap_edges(xa, xb, "gx")
    moved, ya, yb = call(
        functools.partial(shift_kernel, True),
        faces,
        [own, first, second],
        "shift2",
        [FACE_ROWS] * 4,
    )
    first, second = swap_edges(ya, yb, "gy")
    (out,) = call(
        last_kernel,
        [ROWS],
        [moved, first, second],
        "last",
        [ROWS] + [FACE_ROWS] * 2,
        far_outs=True,
        more=[pltpu.SemaphoreType.DMA((len(PIECES),))],
    )
    return out.reshape(populations.shape)


def solution(mesh):
    placed = (
        P("level", None, "gx", "gy", None),
        P("level", "gx", "gy", None),
        P("level", "gx", "gy", None),
        P("level", "gx", "gy", None, None),
        P("level", "gx", "gy", None),
    )
    return jax.shard_map(
        shards,
        mesh=mesh,
        in_specs=placed,
        out_specs=P("level", None, "gx", "gy", None),
        check_vma=False,
    )
```

```python
import functools
import jax
import jax.numpy as jnp
import numpy as np
from jax import lax
from jax.experimental import pallas as pl
from jax.experimental.pallas import tpu as pltpu
from jax.sharding import PartitionSpec as P


CAP = 2
FLOOR = 0.05
BETA_COARSE = 0.9
BETA_FINE = 0.8
SCALE_FINE = 0.5
SCALE_COARSE = 1.5
WIDTH = 4
TILES = 16
LANES = 128


def lattice():
    shells = [
        (0, 0, 0),
        (0, 0, 1),
        (0, 1, 1),
        (1, 1, 1),
        (0, 0, 2),
        (0, 2, 2),
        (2, 2, 2),
        (0, 0, 3),
        (0, 1, 2),
        (1, 1, 2),
    ]
    vectors = []
    for first in range(-3, 4):
        for second in range(-3, 4):
            for third in range(-3, 4):
                if tuple(sorted((abs(first), abs(second), abs(third)))) in shells:
                    vectors.append((first, second, third))
    offsets = np.array(vectors)
    speeds = offsets * 1.0
    raw = np.exp(-0.5 * np.sum(speeds * speeds, axis=1))
    total = np.sum(raw)
    weights = raw / total
    theta = float(np.sum(weights * speeds[:, 0] * speeds[:, 0]))
    return vectors, speeds, weights, theta, float(total)


VECTORS, SPEEDS, WEIGHTS, THETA, TOTAL = lattice()
Q = len(VECTORS)
ROWS = Q * TILES
INDEX = {v: i for i, v in enumerate(VECTORS)}
PAIRS = [(a, b) for a in range(3) for b in range(a, 3)]
TRIPLES = [(a, b, c) for a in range(3) for b in range(a, 3) for c in range(b, 3)]
MOMENTS = 1 + 3 + len(PAIRS) + len(TRIPLES)
GROUPS = {}
for _i, (_x, _y, _z) in enumerate(VECTORS):
    GROUPS.setdefault((_x, _y), []).append((_z, _i))


def norms():
    rows = [np.ones(Q)]
    for a in range(3):
        rows.append(SPEEDS[:, a])
    for a, b in PAIRS:
        rows.append(SPEEDS[:, a] * SPEEDS[:, b] - THETA * float(a == b))
    for a, b, c in TRIPLES:
        rows.append(
            SPEEDS[:, a] * SPEEDS[:, b] * SPEEDS[:, c]
            - THETA
            * (
                SPEEDS[:, a] * float(b == c)
                + SPEEDS[:, b] * float(a == c)
                + SPEEDS[:, c] * float(a == b)
            )
        )
    basis = np.stack(rows)
    return (basis * basis) @ WEIGHTS


NORMS = norms()


def face_layout(axis):
    sides = {}
    for sign in (1, -1):
        order = [i for n in (2, 1, 3) for i in range(Q) if VECTORS[i][axis] == sign * n]
        place, at = {}, 0
        for i in order:
            place[i] = at
            at += abs(VECTORS[i][axis])
        sides[sign] = (place, at)
    return sides


FACE_X = face_layout(0)
FACE_Y = face_layout(1)
FACE_ROWS = FACE_X[1][1] * WIDTH


def scaled(k, value):
    return value if k == 1 else value * float(k)


def combine(terms):
    total = None
    for k, value in terms:
        if k == 0:
            continue
        if total is None:
            total = scaled(k, value)
        elif k > 0:
            total = total + scaled(k, value)
        else:
            total = total - scaled(-k, value)
    return total


def tree(values):
    values = list(values)
    while len(values) > 1:
        values = [
            values[i] + values[i + 1] if i + 1 < len(values) else values[i]
            for i in range(0, len(values), 2)
        ]
    return values[0]


class Sums:
    def __init__(self, parts=4):
        self.parts = [None] * parts
        self.turn = 0

    def add(self, value):
        k = self.turn % len(self.parts)
        self.turn += 1
        self.parts[k] = value if self.parts[k] is None else self.parts[k] + value

    def total(self):
        return tree([p for p in self.parts if p is not None])


def half_rows(i, half):
    return pl.ds(pl.multiple_of(half * 8 + i * TILES, 8), 8)


def request_tables(owner_ref, wanted_ref, target_ref, ask_ref, pick_ref):
    own = owner_ref[...]
    count = own.shape[1]
    sub = lax.broadcasted_iota(jnp.int32, (count, count), 0)
    lane = lax.broadcasted_iota(jnp.int32, (count, count), 1)

    def down(row):
        return jnp.sum(
            jnp.where(sub == lane, jnp.broadcast_to(row, (count, count)), 0), axis=1, keepdims=True
        )

    same = jnp.where(
        jnp.logical_and(jnp.broadcast_to(own, (count, count)) == down(own), sub < lane), 1, 0
    )
    slot = own * CAP + jnp.sum(same, axis=0, keepdims=True)
    width = ask_ref.shape[0]
    by_slot = jnp.where(
        lax.broadcasted_iota(jnp.int32, (width, count), 0) == jnp.broadcast_to(slot, (width, count)),
        1.0,
        0.0,
    )
    wide = lax.broadcasted_iota(jnp.int32, (count, LANES), 1)
    tiles = jnp.where(wide == down(wanted_ref[...]), 1.0, 0.0)
    ask_ref[...] = jnp.dot(by_slot, tiles, preferred_element_type=jnp.float32)
    by_target = jnp.where(sub == jnp.broadcast_to(target_ref[...], (count, count)), 1.0, 0.0)
    slots = jnp.where(wide == down(slot), 1.0, 0.0)
    pick_ref[...] = jnp.dot(by_target, slots, preferred_element_type=jnp.float32)


def moments_kernel(pops_ref, mom_ref):
    def one(half, carry):
        raw = {}

        def put(key, k, value):
            if k == 0:
                return
            old = raw.get(key)
            term = scaled(abs(k), value)
            if old is None:
                raw[key] = term if k > 0 else -term
            else:
                raw[key] = old + term if k > 0 else old - term

        for x in range(-3, 4):
            inner = {}
            for y in range(-3, 4):
                if (x, y) not in GROUPS:
                    continue
                f = {z: pops_ref[half_rows(i, half), :] for z, i in GROUPS[(x, y)]}
                even = {k: f[k] + f[-k] for k in (1, 2, 3) if k in f}
                odd = {k: f[k] - f[-k] for k in (1, 2, 3) if k in f}
                sums = [
                    combine([(1, f[0])] + [(1, v) for v in even.values()]),
                    combine([(k, v) for k, v in odd.items()]),
                    combine([(k * k, v) for k, v in even.items()]),
                    combine([(k * k * k, v) for k, v in odd.items()]),
                ]
                for c in range(4):
                    if sums[c] is None:
                        continue
                    for b in range(4 - c):
                        k = y**b
                        if k:
                            inner.setdefault((b, c), []).append((k, sums[c]))
            for (b, c), terms in inner.items():
                terms.sort(key=lambda t: -t[0])
                value = combine(terms) if terms[0][0] > 0 else -combine([(-k, v) for k, v in terms])
                for a in range(4 - b - c):
                    put((a, b, c), x**a, value)
        out = [raw[(0, 0, 0)], raw[(1, 0, 0)], raw[(0, 1, 0)], raw[(0, 0, 1)]]

        def power(*axes):
            return tuple(sum(1 for a in axes if a == d) for d in range(3))

        for a, b in PAIRS:
            value = raw[power(a, b)]
            out.append(value - THETA * out[0] if a == b else value)
        for a, b, c in TRIPLES:
            value = raw[power(a, b, c)]
            if a == b == c:
                value = value - (3.0 * THETA) * out[1 + a]
            elif a == b:
                value = value - THETA * out[1 + c]
            elif b == c:
                value = value - THETA * out[1 + a]
            out.append(value)
        for n in range(MOMENTS):
            mom_ref[half_rows(n, half), :] = out[n]
        return carry

    lax.fori_loop(0, 2, one, 0)


def pack_kernel(mom_ref, ask_ref, reply_ref):
    ask = ask_ref[:, :TILES]
    width = ask_ref.shape[0]
    step = 4
    for first in range(0, MOMENTS, step):
        block = jnp.concatenate(
            [mom_ref[n * TILES : (n + 1) * TILES, :] for n in range(first, first + step)], axis=1
        )
        chosen = jnp.dot(
            ask, block, precision=lax.Precision.HIGHEST, preferred_element_type=jnp.float32
        )
        for k in range(step):
            reply_ref[pl.ds(first + k, width, stride=MOMENTS), :] = chosen[
                :, k * LANES : (k + 1) * LANES
            ]


def rebuild(col_ref, half, scale, f_ref):
    a = [col_ref[half_rows(n, half), :] for n in range(MOMENTS)]
    rho = a[0]
    inverse = 1.0 / rho
    flux = a[1:4]
    speed = [v * inverse for v in flux]
    b = [a[n] * (1.0 / NORMS[n]) for n in range(4)]
    n = 4
    names = {}
    for first, second in PAIRS:
        eq = flux[first] * speed[second]
        names[(first, second)] = (eq + scale * (a[n] - eq)) * (1.0 / NORMS[n])
        n += 1
    for first, second, third in TRIPLES:
        eq = flux[first] * speed[second] * speed[third]
        names[(first, second, third)] = (eq + scale * (a[n] - eq)) * (1.0 / NORMS[n])
        n += 1
    k0 = b[0] - THETA * (names[(0, 0)] + names[(1, 1)] + names[(2, 2)])
    lin = []
    for d in range(3):
        others = [names[tuple(sorted((d, e, e)))] for e in range(3) if e != d]
        lin.append(b[1 + d] - THETA * (3.0 * names[(d, d, d)] + (others[0] + others[1])))
    cubes = {k: names[(2, 2, 2)] * float(k**3) for k in (1, 2, 3)}

    def horner(k, parts):
        value = parts[-1]
        for part in parts[-2::-1]:
            if k == 0:
                value = part
            elif k == 1:
                value = part + value
            elif k == -1:
                value = part - value
            else:
                value = part + float(k) * value
        return value

    for x in range(-3, 4):
        q = [
            horner(x, [k0, lin[0], names[(0, 0)], names[(0, 0, 0)]]),
            horner(x, [lin[1], names[(0, 1)], names[(0, 0, 1)]]),
            horner(x, [names[(1, 1)], names[(0, 1, 1)]]),
            names[(1, 1, 1)],
        ]
        r = [
            horner(x, [lin[2], names[(0, 2)], names[(0, 0, 2)]]),
            horner(x, [names[(1, 2)], names[(0, 1, 2)]]),
            names[(1, 1, 2)],
        ]
        s = [horner(x, [names[(2, 2)], names[(0, 2, 2)]]), names[(1, 2, 2)]]
        for y in range(-3, 4):
            if (x, y) not in GROUPS:
                continue
            place = dict(GROUPS[(x, y)])
            p0, p1, p2 = horner(y, q), horner(y, r), horner(y, s)
            f_ref[half_rows(place[0], half), :] = p0
            for k in (1, 2, 3):
                if k in place:
                    even = p0 + scaled(k * k, p2)
                    odd = scaled(k, p1) + cubes[k]
                    f_ref[half_rows(place[k], half), :] = even + odd
                    f_ref[half_rows(place[-k], half), :] = even - odd


def collide(f_ref, d_ref, half, solid, beta, own_ref, weighted):
    w = [float(v) for v in WEIGHTS]

    def load(ref, i):
        return ref[half_rows(i, half), :]

    rho_s, flux_s = Sums(), [Sums(2) for _ in range(3)]
    rho_s.add(w[INDEX[(0, 0, 0)]] * load(f_ref, INDEX[(0, 0, 0)]))
    for i, v in enumerate(VECTORS):
        opposite = INDEX[tuple(-c for c in v)]
        if i >= opposite:
            continue
        plus, minus = load(f_ref, opposite), load(f_ref, i)
        rho_s.add(w[i] * (plus + minus))
        odd = w[i] * (plus - minus)
        for d in range(3):
            k = -v[d]
            if k:
                flux_s[d].add(odd if k == 1 else odd * float(k))
    rho = rho_s.total()
    inverse = 1.0 / rho
    powers, gauss = [], []
    for d in range(3):
        rate = flux_s[d].total() * inverse * (1.0 / THETA)
        up, down = jnp.exp(rate), jnp.exp(-rate)
        one = {0: None, 1: up, -1: down, 2: up * up, -2: down * down}
        one[3], one[-3] = one[2] * up, one[-2] * down
        powers.append(one)
        gauss.append({k: float(np.exp(-0.5 * k * k)) for k in range(-3, 4)})

    def pair_sum(d, k):
        return (powers[d][k] + powers[d][-k]) * gauss[d][k]

    zs = [pair_sum(2, k) for k in (1, 2, 3)]
    upto = {
        (0,): 1.0,
        (0, 1): 1.0 + zs[0],
        (0, 1, 2): 1.0 + zs[0] + zs[1],
        (0, 2): 1.0 + zs[1],
        (0, 1, 2, 3): 1.0 + zs[0] + zs[1] + zs[2],
    }
    xs = [1.0] + [pair_sum(0, k) for k in (1, 2, 3)]
    ys = [1.0] + [pair_sum(1, k) for k in (1, 2, 3)]
    rows = []
    for x in range(4):
        line = []
        for y in range(4):
            if (x, y) not in GROUPS:
                continue
            key = tuple(sorted(z for z, _ in GROUPS[(x, y)] if z >= 0))
            line.append(ys[y] * upto[key])
        rows.append(xs[x] * functools.reduce(lambda p, q: p + q, line))
    norm = functools.reduce(lambda p, q: p + q, rows)
    factor = rho * float(TOTAL) / norm

    least, curve, start = None, Sums(), Sums()
    for x in range(-3, 4):
        base = factor if x == 0 else factor * powers[0][x]
        for y in range(-3, 4):
            if (x, y) not in GROUPS:
                continue
            plane = base if y == 0 else base * powers[1][y]
            for z, i in GROUPS[(x, y)]:
                f = load(f_ref, i)
                equil = plane if z == 0 else plane * powers[2][z]
                delta = equil - f
                d_ref[half_rows(i, half), :] = delta
                floored = jnp.maximum(f, FLOOR)
                ratio = delta / floored
                least = ratio if least is None else jnp.minimum(least, ratio)
                curve.add(w[i] * (delta * ratio))
                start.add(w[i] * (floored * jnp.log(floored)))
    ceiling = 0.95 / jnp.maximum(-least, 0.2375)
    bound = 0.25 * (curve.total() + 1e-6)
    entropy = start.total()

    def newton(turn, alpha):
        value, slope = Sums(), Sums()
        for i in range(Q):
            delta = load(d_ref, i)
            path = jnp.maximum(load(f_ref, i) + alpha * delta, FLOOR)
            logs = w[i] * jnp.log(path)
            value.add(path * logs)
            slope.add(delta * logs)
        change = (value.total() - entropy) / jnp.maximum(slope.total(), bound)
        return jnp.minimum(jnp.maximum(alpha - change, 1.0), ceiling)

    alpha = lax.fori_loop(0, 3, newton, jnp.full(rho.shape, 2.0, jnp.float32))
    step = alpha * beta
    for i, v in enumerate(VECTORS):
        post = jnp.where(solid == 1, rho, load(f_ref, i) + step * load(d_ref, i))
        if weighted:
            post = post * w[i]
        if v[2]:
            post = pltpu.roll(post, v[2] % LANES, 1)
        own_ref[half_rows(i, half), :] = post


def route(axis, odd_ref, even_ref, one_ref, two_ref):
    odd = lax.axis_index(axis) % 2 == 1
    a, b = odd_ref[...], even_ref[...]
    one_ref[...] = jnp.where(odd, a, b)
    two_ref[...] = jnp.where(odd, b, a)


def send_x(own_ref, xa_ref, xb_ref, up_ref, down_ref):
    for sign, out_ref in ((1, up_ref), (-1, down_ref)):
        place, _ = FACE_X[sign]
        for i, at in place.items():
            n = abs(VECTORS[i][0]) * WIDTH
            first = i * TILES + (TILES - n if sign > 0 else 0)
            out_ref[at * WIDTH : at * WIDTH + n, :] = own_ref[first : first + n, :]
    route("gx", up_ref, down_ref, xa_ref, xb_ref)


def rebuild_kernel(
    reply_ref, pick_ref, solid_ref, own_ref, xa_ref, xb_ref, col_ref, f_ref, d_ref, up_ref, down_ref
):
    level = lax.axis_index("level")
    scale = jnp.where(level == 1, SCALE_FINE, SCALE_COARSE)
    beta = jnp.where(level == 1, BETA_FINE, BETA_COARSE)
    width = reply_ref.shape[0] // MOMENTS
    pick = pick_ref[:, :width]
    step = 4
    for first in range(0, MOMENTS, step):
        block = jnp.concatenate(
            [
                reply_ref[pl.ds(n, width, stride=MOMENTS), :]
                for n in range(first, first + step)
            ],
            axis=1,
        )
        chosen = jnp.dot(
            pick, block, precision=lax.Precision.HIGHEST, preferred_element_type=jnp.float32
        )
        for k in range(step):
            n = first + k
            col_ref[n * TILES : (n + 1) * TILES, :] = chosen[:, k * LANES : (k + 1) * LANES]

    def one(half, carry):
        rebuild(col_ref, half, scale, f_ref)
        solid = solid_ref[pl.ds(pl.multiple_of(half * 8, 8), 8), :]
        collide(f_ref, d_ref, half, solid, beta, own_ref, False)
        return carry

    lax.fori_loop(0, 2, one, 0)
    send_x(own_ref, xa_ref, xb_ref, up_ref, down_ref)


def copy_rows(src_ref, dst_ref):
    def step(k, carry):
        rows = pl.ds(pl.multiple_of(k * TILES, 8), TILES)
        dst_ref[rows, :] = src_ref[rows, :]
        return carry

    lax.fori_loop(0, Q, step, 0)


def shift_x(own_ref, xa_ref, xb_ref, x_ref, ya_ref, yb_ref, low_ref, high_ref, up_ref, down_ref):
    route("gx", xb_ref, xa_ref, low_ref, high_ref)
    for i, v in enumerate(VECTORS):
        n = abs(v[0]) * WIDTH
        base = i * TILES
        if n == 0:
            x_ref[base : base + TILES, :] = own_ref[base : base + TILES, :]
        elif v[0] > 0:
            at = FACE_X[1][0][i] * WIDTH
            x_ref[base + n : base + TILES, :] = own_ref[base : base + TILES - n, :]
            x_ref[base : base + n, :] = low_ref[at : at + n, :]
        else:
            at = FACE_X[-1][0][i] * WIDTH
            x_ref[base : base + TILES - n, :] = own_ref[base + n : base + TILES, :]
            x_ref[base + TILES - n : base + TILES, :] = high_ref[at : at + n, :]
    for sign, out_ref in ((1, up_ref), (-1, down_ref)):
        place, _ = FACE_Y[sign]
        for i, at in place.items():
            n = abs(VECTORS[i][1])
            for k in range(n):
                row = WIDTH - n + k if sign > 0 else k
                out_ref[(at + k) * WIDTH : (at + k + 1) * WIDTH, :] = x_ref[
                    pl.ds(i * TILES + row, WIDTH, stride=WIDTH), :
                ]
    route("gy", up_ref, down_ref, ya_ref, yb_ref)


def shift_kernel(last, own_ref, xa_ref, xb_ref, x_ref, ya_ref, yb_ref, *scratch):
    if not last:
        shift_x(own_ref, xa_ref, xb_ref, x_ref, ya_ref, yb_ref, *scratch)
        return
    fine = lax.axis_index("level") == 1

    @pl.when(fine)
    def _():
        shift_x(own_ref, xa_ref, xb_ref, x_ref, ya_ref, yb_ref, *scratch)

    @pl.when(jnp.logical_not(fine))
    def _():
        copy_rows(own_ref, x_ref)
        ya_ref[...] = jnp.zeros_like(ya_ref)
        yb_ref[...] = jnp.zeros_like(yb_ref)


def assemble(x_ref, low_ref, high_ref, out_ref, first=0, last=Q):
    for i in range(first, last):
        v = VECTORS[i]
        base = i * TILES
        out_ref[base : base + TILES, :] = x_ref[base - v[1] : base - v[1] + TILES, :]
        n = abs(v[1])
        for k in range(n):
            if v[1] > 0:
                src_ref, at, row = low_ref, FACE_Y[1][0][i] + k, k
            else:
                src_ref, at, row = high_ref, FACE_Y[-1][0][i] + k, WIDTH - n + k
            out_ref[pl.ds(base + row, WIDTH, stride=WIDTH), :] = src_ref[
                at * WIDTH : (at + 1) * WIDTH, :
            ]


def second_kernel(
    x_ref, ya_ref, yb_ref, solid_ref, own_ref, xa_ref, xb_ref, f_ref, d_ref, low_ref, high_ref
):
    fine = lax.axis_index("level") == 1
    route("gy", yb_ref, ya_ref, low_ref, high_ref)
    assemble(x_ref, low_ref, high_ref, f_ref)

    @pl.when(fine)
    def _():
        def one(half, carry):
            solid = solid_ref[pl.ds(pl.multiple_of(half * 8, 8), 8), :]
            collide(f_ref, d_ref, half, solid, BETA_FINE, own_ref, True)
            return carry

        lax.fori_loop(0, 2, one, 0)
        send_x(own_ref, xa_ref, xb_ref, low_ref, high_ref)

    @pl.when(jnp.logical_not(fine))
    def _():
        for i in range(Q):
            rows = slice(i * TILES, (i + 1) * TILES)
            own_ref[rows, :] = f_ref[rows, :] * float(WEIGHTS[i])
        xa_ref[...] = jnp.zeros_like(xa_ref)
        xb_ref[...] = jnp.zeros_like(xb_ref)


PIECES = [(Q * k // 4, Q * (k + 1) // 4) for k in range(4)]


def last_kernel(x_ref, ya_ref, yb_ref, out_ref, new_ref, low_ref, high_ref, sems):
    fine = lax.axis_index("level") == 1

    def piece(src_ref, k):
        first, last = PIECES[k]
        rows = pl.ds(first * TILES, (last - first) * TILES)
        return pltpu.make_async_copy(src_ref.at[rows, :], out_ref.at[rows, :], sems.at[k])

    @pl.when(fine)
    def _():
        route("gy", yb_ref, ya_ref, low_ref, high_ref)
        for k, (first, last) in enumerate(PIECES):
            assemble(x_ref, low_ref, high_ref, new_ref, first, last)
            piece(new_ref, k).start()
        for k in range(len(PIECES)):
            piece(new_ref, k).wait()

    @pl.when(jnp.logical_not(fine))
    def _():
        for k in range(len(PIECES)):
            piece(x_ref, k).start()
        for k in range(len(PIECES)):
            piece(x_ref, k).wait()


def call(kernel, outs, args, name, scratch=(), flops=4_000_000, far_outs=False, more=()):
    whole = pl.BlockSpec(memory_space=pltpu.VMEM)
    far = pl.BlockSpec(memory_space=pltpu.HBM)
    shapes = [jax.ShapeDtypeStruct((rows, LANES), jnp.float32) for rows in outs]
    moved = sum(int(np.prod(s.shape)) for s in shapes) + sum(int(np.prod(a.shape)) for a in args)
    return pl.pallas_call(
        kernel,
        out_shape=shapes,
        in_specs=[whole] * len(args),
        out_specs=[far if far_outs else whole] * len(shapes),
        scratch_shapes=[pltpu.VMEM((rows, LANES), jnp.float32) for rows in scratch] + list(more),
        compiler_params=pltpu.CompilerParams(vmem_limit_bytes=24 << 20),
        cost_estimate=pl.CostEstimate(flops=flops, bytes_accessed=4 * moved, transcendentals=0),
        name=name,
    )(*args)


def swap_edges(first, second, axis, levels):
    count = lax.axis_size(axis)
    odd, even = [], []
    for level in range(lax.axis_size("level")):
        at = level * count
        for i in range(count):
            if level in levels:
                odd.append((at + i, at + ((i + 1) % count if i % 2 else (i - 1) % count)))
                even.append((at + i, at + (i ^ 1)))
            else:
                odd.append((at + i, at + i))
                even.append((at + i, at + i))
    both = ("level", axis)
    return lax.ppermute(first, both, odd), lax.ppermute(second, both, even)


def shards(populations, solid_mask, recv_tiles, owner_gy, owner_tiles):
    peers = lax.axis_size("gy")
    count = owner_tiles.shape[-1]
    pops = populations.reshape(ROWS, LANES)
    solid = solid_mask.reshape(TILES, LANES)
    owners = owner_gy.reshape(1, count)
    wanted = owner_tiles.reshape(1, count)
    targets = recv_tiles.reshape(1, count)
    slots = peers * CAP
    (mom,) = call(moments_kernel, [MOMENTS * TILES], [pops], "moments")
    ask, pick = call(request_tables, [slots, TILES], [owners, wanted, targets], "requests")
    crossed = lax.ppermute(mom, "level", [(0, 1), (1, 0)])
    asked = lax.all_to_all(
        ask.reshape(peers, CAP, LANES), "gy", split_axis=0, concat_axis=0, tiled=True
    ).reshape(slots, LANES)
    (answer,) = call(pack_kernel, [slots * MOMENTS], [crossed, asked], "pack")
    reply = lax.all_to_all(
        answer.reshape(peers, CAP * MOMENTS, LANES), "gy", split_axis=0, concat_axis=0, tiled=True
    ).reshape(slots * MOMENTS, LANES)
    faces = [ROWS, FACE_ROWS, FACE_ROWS]
    own, xa, xb = call(
        rebuild_kernel,
        faces,
        [reply, pick, solid],
        "collide1",
        [MOMENTS * TILES, ROWS, ROWS] + [FACE_ROWS] * 2,
    )
    first, second = swap_edges(xa, xb, "gx", (0, 1))
    moved, ya, yb = call(
        functools.partial(shift_kernel, False),
        faces,
        [own, first, second],
        "shift1",
        [FACE_ROWS] * 4,
    )
    first, second = swap_edges(ya, yb, "gy", (0, 1))
    own, xa, xb = call(
        second_kernel,
        faces,
        [moved, first, second, solid],
        "collide2",
        [ROWS, ROWS] + [FACE_ROWS] * 2,
    )
    first, second = swap_edges(xa, xb, "gx", (1,))
    moved, ya, yb = call(
        functools.partial(shift_kernel, True),
        faces,
        [own, first, second],
        "shift2",
        [FACE_ROWS] * 4,
    )
    first, second = swap_edges(ya, yb, "gy", (1,))
    (out,) = call(
        last_kernel,
        [ROWS],
        [moved, first, second],
        "last",
        [ROWS] + [FACE_ROWS] * 2,
        far_outs=True,
        more=[pltpu.SemaphoreType.DMA((len(PIECES),))],
    )
    return out.reshape(populations.shape)


def solution(mesh):
    placed = (
        P("level", None, "gx", "gy", None),
        P("level", "gx", "gy", None),
        P("level", "gx", "gy", None),
        P("level", "gx", "gy", None, None),
        P("level", "gx", "gy", None),
    )
    return jax.shard_map(
        shards,
        mesh=mesh,
        in_specs=placed,
        out_specs=P("level", None, "gx", "gy", None),
        check_vma=False,
    )
```

```python
import functools
import jax
import jax.numpy as jnp
import numpy as np
from jax import lax
from jax.experimental import pallas as pl
from jax.experimental.pallas import tpu as pltpu
from jax.sharding import PartitionSpec as P


CAP = 2
FLOOR = 0.05
BETA_COARSE = 0.9
BETA_FINE = 0.8
SCALE_FINE = 0.5
SCALE_COARSE = 1.5
WIDTH = 4
TILES = 16
LANES = 128


def lattice():
    shells = [
        (0, 0, 0),
        (0, 0, 1),
        (0, 1, 1),
        (1, 1, 1),
        (0, 0, 2),
        (0, 2, 2),
        (2, 2, 2),
        (0, 0, 3),
        (0, 1, 2),
        (1, 1, 2),
    ]
    vectors = []
    for first in range(-3, 4):
        for second in range(-3, 4):
            for third in range(-3, 4):
                if tuple(sorted((abs(first), abs(second), abs(third)))) in shells:
                    vectors.append((first, second, third))
    offsets = np.array(vectors)
    speeds = offsets * 1.0
    raw = np.exp(-0.5 * np.sum(speeds * speeds, axis=1))
    total = np.sum(raw)
    weights = raw / total
    theta = float(np.sum(weights * speeds[:, 0] * speeds[:, 0]))
    return vectors, speeds, weights, theta, float(total)


VECTORS, SPEEDS, WEIGHTS, THETA, TOTAL = lattice()
Q = len(VECTORS)
ROWS = Q * TILES
INDEX = {v: i for i, v in enumerate(VECTORS)}
PAIRS = [(a, b) for a in range(3) for b in range(a, 3)]
TRIPLES = [(a, b, c) for a in range(3) for b in range(a, 3) for c in range(b, 3)]
MOMENTS = 1 + 3 + len(PAIRS) + len(TRIPLES)
GROUPS = {}
for _i, (_x, _y, _z) in enumerate(VECTORS):
    GROUPS.setdefault((_x, _y), []).append((_z, _i))


def norms():
    rows = [np.ones(Q)]
    for a in range(3):
        rows.append(SPEEDS[:, a])
    for a, b in PAIRS:
        rows.append(SPEEDS[:, a] * SPEEDS[:, b] - THETA * float(a == b))
    for a, b, c in TRIPLES:
        rows.append(
            SPEEDS[:, a] * SPEEDS[:, b] * SPEEDS[:, c]
            - THETA
            * (
                SPEEDS[:, a] * float(b == c)
                + SPEEDS[:, b] * float(a == c)
                + SPEEDS[:, c] * float(a == b)
            )
        )
    basis = np.stack(rows)
    return (basis * basis) @ WEIGHTS


NORMS = norms()


def face_layout(axis):
    sides = {}
    for sign in (1, -1):
        order = [i for n in (2, 1, 3) for i in range(Q) if VECTORS[i][axis] == sign * n]
        place, at = {}, 0
        for i in order:
            place[i] = at
            at += abs(VECTORS[i][axis])
        sides[sign] = (place, at)
    return sides


FACE_X = face_layout(0)
FACE_Y = face_layout(1)
FACE_ROWS = FACE_X[1][1] * WIDTH


def scaled(k, value):
    return value if k == 1 else value * float(k)


def combine(terms):
    total = None
    for k, value in terms:
        if k == 0:
            continue
        if total is None:
            total = scaled(k, value)
        elif k > 0:
            total = total + scaled(k, value)
        else:
            total = total - scaled(-k, value)
    return total


def tree(values):
    values = list(values)
    while len(values) > 1:
        values = [
            values[i] + values[i + 1] if i + 1 < len(values) else values[i]
            for i in range(0, len(values), 2)
        ]
    return values[0]


class Sums:
    def __init__(self, parts=4):
        self.parts = [None] * parts
        self.turn = 0

    def add(self, value):
        k = self.turn % len(self.parts)
        self.turn += 1
        self.parts[k] = value if self.parts[k] is None else self.parts[k] + value

    def total(self):
        return tree([p for p in self.parts if p is not None])


def half_rows(i, half):
    return pl.ds(pl.multiple_of(half * 8 + i * TILES, 8), 8)


def request_tables(owner_ref, wanted_ref, target_ref, ask_ref, pick_ref):
    own = owner_ref[...]
    count = own.shape[1]
    sub = lax.broadcasted_iota(jnp.int32, (count, count), 0)
    lane = lax.broadcasted_iota(jnp.int32, (count, count), 1)

    def down(row):
        return jnp.sum(
            jnp.where(sub == lane, jnp.broadcast_to(row, (count, count)), 0), axis=1, keepdims=True
        )

    same = jnp.where(
        jnp.logical_and(jnp.broadcast_to(own, (count, count)) == down(own), sub < lane), 1, 0
    )
    slot = own * CAP + jnp.sum(same, axis=0, keepdims=True)
    width = ask_ref.shape[0]
    by_slot = jnp.where(
        lax.broadcasted_iota(jnp.int32, (width, count), 0) == jnp.broadcast_to(slot, (width, count)),
        1.0,
        0.0,
    )
    wide = lax.broadcasted_iota(jnp.int32, (count, LANES), 1)
    tiles = jnp.where(wide == down(wanted_ref[...]), 1.0, 0.0)
    ask_ref[...] = jnp.dot(by_slot, tiles, preferred_element_type=jnp.float32)
    by_target = jnp.where(sub == jnp.broadcast_to(target_ref[...], (count, count)), 1.0, 0.0)
    slots = jnp.where(wide == down(slot), 1.0, 0.0)
    pick_ref[...] = jnp.dot(by_target, slots, preferred_element_type=jnp.float32)


def moments_kernel(pops_ref, mom_ref):
    def one(half, carry):
        raw = {}

        def put(key, k, value):
            if k == 0:
                return
            old = raw.get(key)
            term = scaled(abs(k), value)
            if old is None:
                raw[key] = term if k > 0 else -term
            else:
                raw[key] = old + term if k > 0 else old - term

        for x in range(-3, 4):
            inner = {}
            for y in range(-3, 4):
                if (x, y) not in GROUPS:
                    continue
                f = {z: pops_ref[half_rows(i, half), :] for z, i in GROUPS[(x, y)]}
                even = {k: f[k] + f[-k] for k in (1, 2, 3) if k in f}
                odd = {k: f[k] - f[-k] for k in (1, 2, 3) if k in f}
                sums = [
                    combine([(1, f[0])] + [(1, v) for v in even.values()]),
                    combine([(k, v) for k, v in odd.items()]),
                    combine([(k * k, v) for k, v in even.items()]),
                    combine([(k * k * k, v) for k, v in odd.items()]),
                ]
                for c in range(4):
                    if sums[c] is None:
                        continue
                    for b in range(4 - c):
                        k = y**b
                        if k:
                            inner.setdefault((b, c), []).append((k, sums[c]))
            for (b, c), terms in inner.items():
                terms.sort(key=lambda t: -t[0])
                value = combine(terms) if terms[0][0] > 0 else -combine([(-k, v) for k, v in terms])
                for a in range(4 - b - c):
                    put((a, b, c), x**a, value)
        out = [raw[(0, 0, 0)], raw[(1, 0, 0)], raw[(0, 1, 0)], raw[(0, 0, 1)]]

        def power(*axes):
            return tuple(sum(1 for a in axes if a == d) for d in range(3))

        for a, b in PAIRS:
            value = raw[power(a, b)]
            out.append(value - THETA * out[0] if a == b else value)
        for a, b, c in TRIPLES:
            value = raw[power(a, b, c)]
            if a == b == c:
                value = value - (3.0 * THETA) * out[1 + a]
            elif a == b:
                value = value - THETA * out[1 + c]
            elif b == c:
                value = value - THETA * out[1 + a]
            out.append(value)
        for n in range(MOMENTS):
            mom_ref[half_rows(n, half), :] = out[n]
        return carry

    lax.fori_loop(0, 2, one, 0)


def pack_kernel(mom_ref, ask_ref, reply_ref):
    ask = ask_ref[:, :TILES]
    width = ask_ref.shape[0]
    step = 4
    for first in range(0, MOMENTS, step):
        block = jnp.concatenate(
            [mom_ref[n * TILES : (n + 1) * TILES, :] for n in range(first, first + step)], axis=1
        )
        chosen = jnp.dot(
            ask, block, precision=lax.Precision.HIGHEST, preferred_element_type=jnp.float32
        )
        for k in range(step):
            reply_ref[pl.ds(first + k, width, stride=MOMENTS), :] = chosen[
                :, k * LANES : (k + 1) * LANES
            ]


def rebuild(col_ref, half, scale, f_ref):
    a = [col_ref[half_rows(n, half), :] for n in range(MOMENTS)]
    rho = a[0]
    inverse = 1.0 / rho
    flux = a[1:4]
    speed = [v * inverse for v in flux]
    b = [a[n] * (1.0 / NORMS[n]) for n in range(4)]
    n = 4
    names = {}
    for first, second in PAIRS:
        eq = flux[first] * speed[second]
        names[(first, second)] = (eq + scale * (a[n] - eq)) * (1.0 / NORMS[n])
        n += 1
    for first, second, third in TRIPLES:
        eq = flux[first] * speed[second] * speed[third]
        names[(first, second, third)] = (eq + scale * (a[n] - eq)) * (1.0 / NORMS[n])
        n += 1
    k0 = b[0] - THETA * (names[(0, 0)] + names[(1, 1)] + names[(2, 2)])
    lin = []
    for d in range(3):
        others = [names[tuple(sorted((d, e, e)))] for e in range(3) if e != d]
        lin.append(b[1 + d] - THETA * (3.0 * names[(d, d, d)] + (others[0] + others[1])))
    cubes = {k: names[(2, 2, 2)] * float(k**3) for k in (1, 2, 3)}

    def horner(k, parts):
        value = parts[-1]
        for part in parts[-2::-1]:
            if k == 0:
                value = part
            elif k == 1:
                value = part + value
            elif k == -1:
                value = part - value
            else:
                value = part + float(k) * value
        return value

    for x in range(-3, 4):
        q = [
            horner(x, [k0, lin[0], names[(0, 0)], names[(0, 0, 0)]]),
            horner(x, [lin[1], names[(0, 1)], names[(0, 0, 1)]]),
            horner(x, [names[(1, 1)], names[(0, 1, 1)]]),
            names[(1, 1, 1)],
        ]
        r = [
            horner(x, [lin[2], names[(0, 2)], names[(0, 0, 2)]]),
            horner(x, [names[(1, 2)], names[(0, 1, 2)]]),
            names[(1, 1, 2)],
        ]
        s = [horner(x, [names[(2, 2)], names[(0, 2, 2)]]), names[(1, 2, 2)]]
        for y in range(-3, 4):
            if (x, y) not in GROUPS:
                continue
            place = dict(GROUPS[(x, y)])
            p0, p1, p2 = horner(y, q), horner(y, r), horner(y, s)
            f_ref[half_rows(place[0], half), :] = p0
            for k in (1, 2, 3):
                if k in place:
                    even = p0 + scaled(k * k, p2)
                    odd = scaled(k, p1) + cubes[k]
                    f_ref[half_rows(place[k], half), :] = even + odd
                    f_ref[half_rows(place[-k], half), :] = even - odd


def collide(f_ref, d_ref, half, solid, beta, own_ref, weighted):
    w = [float(v) for v in WEIGHTS]

    def load(ref, i):
        return ref[half_rows(i, half), :]

    rho_s, flux_s = Sums(), [Sums(2) for _ in range(3)]
    rho_s.add(w[INDEX[(0, 0, 0)]] * load(f_ref, INDEX[(0, 0, 0)]))
    for i, v in enumerate(VECTORS):
        opposite = INDEX[tuple(-c for c in v)]
        if i >= opposite:
            continue
        plus, minus = load(f_ref, opposite), load(f_ref, i)
        rho_s.add(w[i] * (plus + minus))
        odd = w[i] * (plus - minus)
        for d in range(3):
            k = -v[d]
            if k:
                flux_s[d].add(odd if k == 1 else odd * float(k))
    rho = rho_s.total()
    inverse = 1.0 / rho
    powers, gauss = [], []
    for d in range(3):
        rate = flux_s[d].total() * inverse * (1.0 / THETA)
        up, down = jnp.exp(rate), jnp.exp(-rate)
        one = {0: None, 1: up, -1: down, 2: up * up, -2: down * down}
        one[3], one[-3] = one[2] * up, one[-2] * down
        powers.append(one)
        gauss.append({k: float(np.exp(-0.5 * k * k)) for k in range(-3, 4)})

    def pair_sum(d, k):
        return (powers[d][k] + powers[d][-k]) * gauss[d][k]

    zs = [pair_sum(2, k) for k in (1, 2, 3)]
    upto = {
        (0,): 1.0,
        (0, 1): 1.0 + zs[0],
        (0, 1, 2): 1.0 + zs[0] + zs[1],
        (0, 2): 1.0 + zs[1],
        (0, 1, 2, 3): 1.0 + zs[0] + zs[1] + zs[2],
    }
    xs = [1.0] + [pair_sum(0, k) for k in (1, 2, 3)]
    ys = [1.0] + [pair_sum(1, k) for k in (1, 2, 3)]
    rows = []
    for x in range(4):
        line = []
        for y in range(4):
            if (x, y) not in GROUPS:
                continue
            key = tuple(sorted(z for z, _ in GROUPS[(x, y)] if z >= 0))
            line.append(ys[y] * upto[key])
        rows.append(xs[x] * functools.reduce(lambda p, q: p + q, line))
    norm = functools.reduce(lambda p, q: p + q, rows)
    factor = rho * float(TOTAL) / norm

    least, curve, start = None, Sums(), Sums()
    for x in range(-3, 4):
        base = factor if x == 0 else factor * powers[0][x]
        for y in range(-3, 4):
            if (x, y) not in GROUPS:
                continue
            plane = base if y == 0 else base * powers[1][y]
            for z, i in GROUPS[(x, y)]:
                f = load(f_ref, i)
                equil = plane if z == 0 else plane * powers[2][z]
                delta = equil - f
                d_ref[half_rows(i, half), :] = delta
                floored = jnp.maximum(f, FLOOR)
                ratio = delta / floored
                least = ratio if least is None else jnp.minimum(least, ratio)
                curve.add(w[i] * (delta * ratio))
                start.add(w[i] * (floored * jnp.log(floored)))
    ceiling = 0.95 / jnp.maximum(-least, 0.2375)
    bound = 0.25 * (curve.total() + 1e-6)
    entropy = start.total()

    def newton(turn, alpha):
        value, slope = Sums(), Sums()
        for i in range(Q):
            delta = load(d_ref, i)
            path = jnp.maximum(load(f_ref, i) + alpha * delta, FLOOR)
            logs = w[i] * jnp.log(path)
            value.add(path * logs)
            slope.add(delta * logs)
        change = (value.total() - entropy) / jnp.maximum(slope.total(), bound)
        return jnp.minimum(jnp.maximum(alpha - change, 1.0), ceiling)

    alpha = lax.fori_loop(0, 3, newton, jnp.full(rho.shape, 2.0, jnp.float32))
    step = alpha * beta
    for i, v in enumerate(VECTORS):
        post = jnp.where(solid == 1, rho, load(f_ref, i) + step * load(d_ref, i))
        if weighted:
            post = post * w[i]
        if v[2]:
            post = pltpu.roll(post, v[2] % LANES, 1)
        own_ref[half_rows(i, half), :] = post


def route(axis, odd_ref, even_ref, one_ref, two_ref):
    odd = lax.axis_index(axis) % 2 == 1
    a, b = odd_ref[...], even_ref[...]
    one_ref[...] = jnp.where(odd, a, b)
    two_ref[...] = jnp.where(odd, b, a)


def send_x(own_ref, xa_ref, xb_ref, up_ref, down_ref):
    for sign, out_ref in ((1, up_ref), (-1, down_ref)):
        place, _ = FACE_X[sign]
        for i, at in place.items():
            n = abs(VECTORS[i][0]) * WIDTH
            first = i * TILES + (TILES - n if sign > 0 else 0)
            out_ref[at * WIDTH : at * WIDTH + n, :] = own_ref[first : first + n, :]
    route("gx", up_ref, down_ref, xa_ref, xb_ref)


def rebuild_kernel(
    reply_ref, pick_ref, solid_ref, own_ref, xa_ref, xb_ref, col_ref, f_ref, d_ref, up_ref, down_ref
):
    level = lax.axis_index("level")
    scale = jnp.where(level == 1, SCALE_FINE, SCALE_COARSE)
    beta = jnp.where(level == 1, BETA_FINE, BETA_COARSE)
    width = reply_ref.shape[0] // MOMENTS
    pick = pick_ref[:, :width]
    step = 4
    for first in range(0, MOMENTS, step):
        block = jnp.concatenate(
            [
                reply_ref[pl.ds(n, width, stride=MOMENTS), :]
                for n in range(first, first + step)
            ],
            axis=1,
        )
        chosen = jnp.dot(
            pick, block, precision=lax.Precision.HIGHEST, preferred_element_type=jnp.float32
        )
        for k in range(step):
            n = first + k
            col_ref[n * TILES : (n + 1) * TILES, :] = chosen[:, k * LANES : (k + 1) * LANES]

    def one(half, carry):
        rebuild(col_ref, half, scale, f_ref)
        solid = solid_ref[pl.ds(pl.multiple_of(half * 8, 8), 8), :]
        collide(f_ref, d_ref, half, solid, beta, own_ref, False)
        return carry

    lax.fori_loop(0, 2, one, 0)
    send_x(own_ref, xa_ref, xb_ref, up_ref, down_ref)


def shift_x(own_ref, xa_ref, xb_ref, x_ref, ya_ref, yb_ref, low_ref, high_ref, up_ref, down_ref):
    route("gx", xb_ref, xa_ref, low_ref, high_ref)
    for i, v in enumerate(VECTORS):
        n = abs(v[0]) * WIDTH
        base = i * TILES
        if n == 0:
            x_ref[base : base + TILES, :] = own_ref[base : base + TILES, :]
        elif v[0] > 0:
            at = FACE_X[1][0][i] * WIDTH
            x_ref[base + n : base + TILES, :] = own_ref[base : base + TILES - n, :]
            x_ref[base : base + n, :] = low_ref[at : at + n, :]
        else:
            at = FACE_X[-1][0][i] * WIDTH
            x_ref[base : base + TILES - n, :] = own_ref[base + n : base + TILES, :]
            x_ref[base + TILES - n : base + TILES, :] = high_ref[at : at + n, :]
    for sign, out_ref in ((1, up_ref), (-1, down_ref)):
        place, _ = FACE_Y[sign]
        for i, at in place.items():
            n = abs(VECTORS[i][1])
            for k in range(n):
                row = WIDTH - n + k if sign > 0 else k
                out_ref[(at + k) * WIDTH : (at + k + 1) * WIDTH, :] = x_ref[
                    pl.ds(i * TILES + row, WIDTH, stride=WIDTH), :
                ]
    route("gy", up_ref, down_ref, ya_ref, yb_ref)


def assemble(x_ref, low_ref, high_ref, out_ref, first=0, last=Q):
    for i in range(first, last):
        v = VECTORS[i]
        base = i * TILES
        out_ref[base : base + TILES, :] = x_ref[base - v[1] : base - v[1] + TILES, :]
        n = abs(v[1])
        for k in range(n):
            if v[1] > 0:
                src_ref, at, row = low_ref, FACE_Y[1][0][i] + k, k
            else:
                src_ref, at, row = high_ref, FACE_Y[-1][0][i] + k, WIDTH - n + k
            out_ref[pl.ds(base + row, WIDTH, stride=WIDTH), :] = src_ref[
                at * WIDTH : (at + 1) * WIDTH, :
            ]


def second_kernel(
    x_ref, ya_ref, yb_ref, solid_ref, own_ref, xa_ref, xb_ref, f_ref, d_ref, low_ref, high_ref
):
    route("gy", yb_ref, ya_ref, low_ref, high_ref)
    assemble(x_ref, low_ref, high_ref, f_ref)

    def one(half, carry):
        solid = solid_ref[pl.ds(pl.multiple_of(half * 8, 8), 8), :]
        collide(f_ref, d_ref, half, solid, BETA_FINE, own_ref, True)
        return carry

    lax.fori_loop(0, 2, one, 0)
    send_x(own_ref, xa_ref, xb_ref, low_ref, high_ref)


PIECES = [(Q * k // 4, Q * (k + 1) // 4) for k in range(4)]


def last_kernel(x_ref, ya_ref, yb_ref, out_ref, new_ref, low_ref, high_ref, sems):
    def piece(k):
        first, last = PIECES[k]
        rows = pl.ds(first * TILES, (last - first) * TILES)
        return pltpu.make_async_copy(new_ref.at[rows, :], out_ref.at[rows, :], sems.at[k])

    coarse = lax.axis_index("level") == 0
    route("gy", yb_ref, ya_ref, low_ref, high_ref)
    for k, (first, last) in enumerate(PIECES):
        assemble(x_ref, low_ref, high_ref, new_ref, first, last)

        @pl.when(coarse)
        def _():
            for i in range(first, last):
                rows = slice(i * TILES, (i + 1) * TILES)
                new_ref[rows, :] = new_ref[rows, :] * float(WEIGHTS[i])

        piece(k).start()
    for k in range(len(PIECES)):
        piece(k).wait()


def call(kernel, outs, args, name, scratch=(), flops=4_000_000, far_outs=False, more=()):
    whole = pl.BlockSpec(memory_space=pltpu.VMEM)
    far = pl.BlockSpec(memory_space=pltpu.HBM)
    shapes = [jax.ShapeDtypeStruct((rows, LANES), jnp.float32) for rows in outs]
    moved = sum(int(np.prod(s.shape)) for s in shapes) + sum(int(np.prod(a.shape)) for a in args)
    return pl.pallas_call(
        kernel,
        out_shape=shapes,
        in_specs=[whole] * len(args),
        out_specs=[far if far_outs else whole] * len(shapes),
        scratch_shapes=[pltpu.VMEM((rows, LANES), jnp.float32) for rows in scratch] + list(more),
        compiler_params=pltpu.CompilerParams(vmem_limit_bytes=24 << 20),
        cost_estimate=pl.CostEstimate(flops=flops, bytes_accessed=4 * moved, transcendentals=0),
        name=name,
    )(*args)


def swap_edges(first, second, axis):
    count = lax.axis_size(axis)
    odd = [(i, (i + 1) % count if i % 2 else (i - 1) % count) for i in range(count)]
    even = [(i, i ^ 1) for i in range(count)]
    return lax.ppermute(first, axis, odd), lax.ppermute(second, axis, even)


def shards(populations, solid_mask, recv_tiles, owner_gy, owner_tiles):
    peers = lax.axis_size("gy")
    count = owner_tiles.shape[-1]
    pops = populations.reshape(ROWS, LANES)
    solid = solid_mask.reshape(TILES, LANES)
    owners = owner_gy.reshape(1, count)
    wanted = owner_tiles.reshape(1, count)
    targets = recv_tiles.reshape(1, count)
    slots = peers * CAP
    (mom,) = call(moments_kernel, [MOMENTS * TILES], [pops], "moments")
    ask, pick = call(request_tables, [slots, TILES], [owners, wanted, targets], "requests")
    crossed = lax.ppermute(mom, "level", [(0, 1), (1, 0)])
    asked = lax.all_to_all(
        ask.reshape(peers, CAP, LANES), "gy", split_axis=0, concat_axis=0, tiled=True
    ).reshape(slots, LANES)
    (answer,) = call(pack_kernel, [slots * MOMENTS], [crossed, asked], "pack")
    reply = lax.all_to_all(
        answer.reshape(peers, CAP * MOMENTS, LANES), "gy", split_axis=0, concat_axis=0, tiled=True
    ).reshape(slots * MOMENTS, LANES)
    faces = [ROWS, FACE_ROWS, FACE_ROWS]
    own, xa, xb = call(
        rebuild_kernel,
        faces,
        [reply, pick, solid],
        "collide1",
        [MOMENTS * TILES, ROWS, ROWS] + [FACE_ROWS] * 2,
    )
    first, second = swap_edges(xa, xb, "gx")
    moved, ya, yb = call(
        shift_x,
        faces,
        [own, first, second],
        "shift1",
        [FACE_ROWS] * 4,
    )
    first, second = swap_edges(ya, yb, "gy")
    def fine_end(moved, first, second, solid):
        own, xa, xb = call(
            second_kernel,
            faces,
            [moved, first, second, solid],
            "collide2",
            [ROWS, ROWS] + [FACE_ROWS] * 2,
        )
        first, second = swap_edges(xa, xb, "gx")
        moved, ya, yb = call(shift_x, faces, [own, first, second], "shift2", [FACE_ROWS] * 4)
        first, second = swap_edges(ya, yb, "gy")
        return moved, first, second

    def coarse_end(moved, first, second, solid):
        return moved, first, second

    moved, first, second = lax.cond(
        lax.axis_index("level") == 1, fine_end, coarse_end, moved, first, second, solid
    )
    (out,) = call(
        last_kernel,
        [ROWS],
        [moved, first, second],
        "last",
        [ROWS] + [FACE_ROWS] * 2,
        far_outs=True,
        more=[pltpu.SemaphoreType.DMA((len(PIECES),))],
    )
    return out.reshape(populations.shape)


def solution(mesh):
    placed = (
        P("level", None, "gx", "gy", None),
        P("level", "gx", "gy", None),
        P("level", "gx", "gy", None),
        P("level", "gx", "gy", None, None),
        P("level", "gx", "gy", None),
    )
    return jax.shard_map(
        shards,
        mesh=mesh,
        in_specs=placed,
        out_specs=P("level", None, "gx", "gy", None),
        check_vma=False,
    )
```

```python
import functools
import jax
import jax.numpy as jnp
import numpy as np
from jax import lax
from jax.experimental import pallas as pl
from jax.experimental.pallas import tpu as pltpu
from jax.sharding import PartitionSpec as P


CAP = 2
FLOOR = 0.05
BETA_COARSE = 0.9
BETA_FINE = 0.8
SCALE_FINE = 0.5
SCALE_COARSE = 1.5
WIDTH = 4
TILES = 16
LANES = 128


def lattice():
    shells = [
        (0, 0, 0),
        (0, 0, 1),
        (0, 1, 1),
        (1, 1, 1),
        (0, 0, 2),
        (0, 2, 2),
        (2, 2, 2),
        (0, 0, 3),
        (0, 1, 2),
        (1, 1, 2),
    ]
    vectors = []
    for first in range(-3, 4):
        for second in range(-3, 4):
            for third in range(-3, 4):
                if tuple(sorted((abs(first), abs(second), abs(third)))) in shells:
                    vectors.append((first, second, third))
    offsets = np.array(vectors)
    speeds = offsets * 1.0
    raw = np.exp(-0.5 * np.sum(speeds * speeds, axis=1))
    total = np.sum(raw)
    weights = raw / total
    theta = float(np.sum(weights * speeds[:, 0] * speeds[:, 0]))
    return vectors, speeds, weights, theta, float(total)


VECTORS, SPEEDS, WEIGHTS, THETA, TOTAL = lattice()
Q = len(VECTORS)
ROWS = Q * TILES
INDEX = {v: i for i, v in enumerate(VECTORS)}
PAIRS = [(a, b) for a in range(3) for b in range(a, 3)]
TRIPLES = [(a, b, c) for a in range(3) for b in range(a, 3) for c in range(b, 3)]
MOMENTS = 1 + 3 + len(PAIRS) + len(TRIPLES)
GROUPS = {}
for _i, (_x, _y, _z) in enumerate(VECTORS):
    GROUPS.setdefault((_x, _y), []).append((_z, _i))


def norms():
    rows = [np.ones(Q)]
    for a in range(3):
        rows.append(SPEEDS[:, a])
    for a, b in PAIRS:
        rows.append(SPEEDS[:, a] * SPEEDS[:, b] - THETA * float(a == b))
    for a, b, c in TRIPLES:
        rows.append(
            SPEEDS[:, a] * SPEEDS[:, b] * SPEEDS[:, c]
            - THETA
            * (
                SPEEDS[:, a] * float(b == c)
                + SPEEDS[:, b] * float(a == c)
                + SPEEDS[:, c] * float(a == b)
            )
        )
    basis = np.stack(rows)
    return (basis * basis) @ WEIGHTS


NORMS = norms()


def face_layout(axis):
    sides = {}
    for sign in (1, -1):
        order = [i for n in (2, 1, 3) for i in range(Q) if VECTORS[i][axis] == sign * n]
        place, at = {}, 0
        for i in order:
            place[i] = at
            at += abs(VECTORS[i][axis])
        sides[sign] = (place, at)
    return sides


FACE_X = face_layout(0)
FACE_Y = face_layout(1)
FACE_ROWS = FACE_X[1][1] * WIDTH


def scaled(k, value):
    return value if k == 1 else value * float(k)


def combine(terms):
    total = None
    for k, value in terms:
        if k == 0:
            continue
        if total is None:
            total = scaled(k, value)
        elif k > 0:
            total = total + scaled(k, value)
        else:
            total = total - scaled(-k, value)
    return total


def tree(values):
    values = list(values)
    while len(values) > 1:
        values = [
            values[i] + values[i + 1] if i + 1 < len(values) else values[i]
            for i in range(0, len(values), 2)
        ]
    return values[0]


class Sums:
    def __init__(self, parts=4):
        self.parts = [None] * parts
        self.turn = 0

    def add(self, value):
        k = self.turn % len(self.parts)
        self.turn += 1
        self.parts[k] = value if self.parts[k] is None else self.parts[k] + value

    def total(self):
        return tree([p for p in self.parts if p is not None])


def half_rows(i, half):
    return pl.ds(pl.multiple_of(half * 8 + i * TILES, 8), 8)


def request_tables(owner_ref, wanted_ref, target_ref, ask_ref, pick_ref):
    own = owner_ref[...]
    count = own.shape[1]
    sub = lax.broadcasted_iota(jnp.int32, (count, count), 0)
    lane = lax.broadcasted_iota(jnp.int32, (count, count), 1)

    def down(row):
        return jnp.sum(
            jnp.where(sub == lane, jnp.broadcast_to(row, (count, count)), 0), axis=1, keepdims=True
        )

    same = jnp.where(
        jnp.logical_and(jnp.broadcast_to(own, (count, count)) == down(own), sub < lane), 1, 0
    )
    slot = own * CAP + jnp.sum(same, axis=0, keepdims=True)
    width = ask_ref.shape[0]
    by_slot = jnp.where(
        lax.broadcasted_iota(jnp.int32, (width, count), 0) == jnp.broadcast_to(slot, (width, count)),
        1.0,
        0.0,
    )
    wide = lax.broadcasted_iota(jnp.int32, (count, LANES), 1)
    tiles = jnp.where(wide == down(wanted_ref[...]), 1.0, 0.0)
    ask_ref[...] = jnp.dot(by_slot, tiles, preferred_element_type=jnp.float32)
    by_target = jnp.where(sub == jnp.broadcast_to(target_ref[...], (count, count)), 1.0, 0.0)
    slots = jnp.where(wide == down(slot), 1.0, 0.0)
    pick_ref[...] = jnp.dot(by_target, slots, preferred_element_type=jnp.float32)


def moments_kernel(pops_ref, mom_ref):
    def one(half, carry):
        raw = {}

        def put(key, k, value):
            if k == 0:
                return
            old = raw.get(key)
            term = scaled(abs(k), value)
            if old is None:
                raw[key] = term if k > 0 else -term
            else:
                raw[key] = old + term if k > 0 else old - term

        for x in range(-3, 4):
            inner = {}
            for y in range(-3, 4):
                if (x, y) not in GROUPS:
                    continue
                f = {z: pops_ref[half_rows(i, half), :] for z, i in GROUPS[(x, y)]}
                even = {k: f[k] + f[-k] for k in (1, 2, 3) if k in f}
                odd = {k: f[k] - f[-k] for k in (1, 2, 3) if k in f}
                sums = [
                    combine([(1, f[0])] + [(1, v) for v in even.values()]),
                    combine([(k, v) for k, v in odd.items()]),
                    combine([(k * k, v) for k, v in even.items()]),
                    combine([(k * k * k, v) for k, v in odd.items()]),
                ]
                for c in range(4):
                    if sums[c] is None:
                        continue
                    for b in range(4 - c):
                        k = y**b
                        if k:
                            inner.setdefault((b, c), []).append((k, sums[c]))
            for (b, c), terms in inner.items():
                terms.sort(key=lambda t: -t[0])
                value = combine(terms) if terms[0][0] > 0 else -combine([(-k, v) for k, v in terms])
                for a in range(4 - b - c):
                    put((a, b, c), x**a, value)
        out = [raw[(0, 0, 0)], raw[(1, 0, 0)], raw[(0, 1, 0)], raw[(0, 0, 1)]]

        def power(*axes):
            return tuple(sum(1 for a in axes if a == d) for d in range(3))

        for a, b in PAIRS:
            value = raw[power(a, b)]
            out.append(value - THETA * out[0] if a == b else value)
        for a, b, c in TRIPLES:
            value = raw[power(a, b, c)]
            if a == b == c:
                value = value - (3.0 * THETA) * out[1 + a]
            elif a == b:
                value = value - THETA * out[1 + c]
            elif b == c:
                value = value - THETA * out[1 + a]
            out.append(value)
        for n in range(MOMENTS):
            mom_ref[half_rows(n, half), :] = out[n]
        return carry

    lax.fori_loop(0, 2, one, 0)


def pack_kernel(mom_ref, ask_ref, reply_ref):
    ask = ask_ref[:, :TILES]
    width = ask_ref.shape[0]
    step = 4
    for first in range(0, MOMENTS, step):
        block = jnp.concatenate(
            [mom_ref[n * TILES : (n + 1) * TILES, :] for n in range(first, first + step)], axis=1
        )
        chosen = jnp.dot(
            ask, block, precision=lax.Precision.HIGHEST, preferred_element_type=jnp.float32
        )
        for k in range(step):
            reply_ref[pl.ds(first + k, width, stride=MOMENTS), :] = chosen[
                :, k * LANES : (k + 1) * LANES
            ]


def rebuild(col_ref, half, scale, f_ref):
    a = [col_ref[half_rows(n, half), :] for n in range(MOMENTS)]
    rho = a[0]
    inverse = 1.0 / rho
    flux = a[1:4]
    speed = [v * inverse for v in flux]
    b = [a[n] * (1.0 / NORMS[n]) for n in range(4)]
    n = 4
    names = {}
    for first, second in PAIRS:
        eq = flux[first] * speed[second]
        names[(first, second)] = (eq + scale * (a[n] - eq)) * (1.0 / NORMS[n])
        n += 1
    for first, second, third in TRIPLES:
        eq = flux[first] * speed[second] * speed[third]
        names[(first, second, third)] = (eq + scale * (a[n] - eq)) * (1.0 / NORMS[n])
        n += 1
    k0 = b[0] - THETA * (names[(0, 0)] + names[(1, 1)] + names[(2, 2)])
    lin = []
    for d in range(3):
        others = [names[tuple(sorted((d, e, e)))] for e in range(3) if e != d]
        lin.append(b[1 + d] - THETA * (3.0 * names[(d, d, d)] + (others[0] + others[1])))
    cubes = {k: names[(2, 2, 2)] * float(k**3) for k in (1, 2, 3)}

    def horner(k, parts):
        value = parts[-1]
        for part in parts[-2::-1]:
            if k == 0:
                value = part
            elif k == 1:
                value = part + value
            elif k == -1:
                value = part - value
            else:
                value = part + float(k) * value
        return value

    for x in range(-3, 4):
        q = [
            horner(x, [k0, lin[0], names[(0, 0)], names[(0, 0, 0)]]),
            horner(x, [lin[1], names[(0, 1)], names[(0, 0, 1)]]),
            horner(x, [names[(1, 1)], names[(0, 1, 1)]]),
            names[(1, 1, 1)],
        ]
        r = [
            horner(x, [lin[2], names[(0, 2)], names[(0, 0, 2)]]),
            horner(x, [names[(1, 2)], names[(0, 1, 2)]]),
            names[(1, 1, 2)],
        ]
        s = [horner(x, [names[(2, 2)], names[(0, 2, 2)]]), names[(1, 2, 2)]]
        for y in range(-3, 4):
            if (x, y) not in GROUPS:
                continue
            place = dict(GROUPS[(x, y)])
            p0, p1, p2 = horner(y, q), horner(y, r), horner(y, s)
            f_ref[half_rows(place[0], half), :] = p0
            for k in (1, 2, 3):
                if k in place:
                    even = p0 + scaled(k * k, p2)
                    odd = scaled(k, p1) + cubes[k]
                    f_ref[half_rows(place[k], half), :] = even + odd
                    f_ref[half_rows(place[-k], half), :] = even - odd


def collide(f_ref, d_ref, half, solid, beta, own_ref, weighted):
    w = [float(v) for v in WEIGHTS]

    def load(ref, i):
        return ref[half_rows(i, half), :]

    rho_s, flux_s = Sums(), [Sums(2) for _ in range(3)]
    rho_s.add(w[INDEX[(0, 0, 0)]] * load(f_ref, INDEX[(0, 0, 0)]))
    for i, v in enumerate(VECTORS):
        opposite = INDEX[tuple(-c for c in v)]
        if i >= opposite:
            continue
        plus, minus = load(f_ref, opposite), load(f_ref, i)
        rho_s.add(w[i] * (plus + minus))
        odd = w[i] * (plus - minus)
        for d in range(3):
            k = -v[d]
            if k:
                flux_s[d].add(odd if k == 1 else odd * float(k))
    rho = rho_s.total()
    inverse = 1.0 / rho
    powers, gauss = [], []
    for d in range(3):
        rate = flux_s[d].total() * inverse * (1.0 / THETA)
        up, down = jnp.exp(rate), jnp.exp(-rate)
        one = {0: None, 1: up, -1: down, 2: up * up, -2: down * down}
        one[3], one[-3] = one[2] * up, one[-2] * down
        powers.append(one)
        gauss.append({k: float(np.exp(-0.5 * k * k)) for k in range(-3, 4)})

    def pair_sum(d, k):
        return (powers[d][k] + powers[d][-k]) * gauss[d][k]

    zs = [pair_sum(2, k) for k in (1, 2, 3)]
    upto = {
        (0,): 1.0,
        (0, 1): 1.0 + zs[0],
        (0, 1, 2): 1.0 + zs[0] + zs[1],
        (0, 2): 1.0 + zs[1],
        (0, 1, 2, 3): 1.0 + zs[0] + zs[1] + zs[2],
    }
    xs = [1.0] + [pair_sum(0, k) for k in (1, 2, 3)]
    ys = [1.0] + [pair_sum(1, k) for k in (1, 2, 3)]
    rows = []
    for x in range(4):
        line = []
        for y in range(4):
            if (x, y) not in GROUPS:
                continue
            key = tuple(sorted(z for z, _ in GROUPS[(x, y)] if z >= 0))
            line.append(ys[y] * upto[key])
        rows.append(xs[x] * functools.reduce(lambda p, q: p + q, line))
    norm = functools.reduce(lambda p, q: p + q, rows)
    factor = rho * float(TOTAL) / norm

    least, curve, start = None, Sums(), Sums()
    for x in range(-3, 4):
        base = factor if x == 0 else factor * powers[0][x]
        for y in range(-3, 4):
            if (x, y) not in GROUPS:
                continue
            plane = base if y == 0 else base * powers[1][y]
            for z, i in GROUPS[(x, y)]:
                f = load(f_ref, i)
                equil = plane if z == 0 else plane * powers[2][z]
                delta = equil - f
                d_ref[half_rows(i, half), :] = delta
                floored = jnp.maximum(f, FLOOR)
                ratio = delta / floored
                least = ratio if least is None else jnp.minimum(least, ratio)
                curve.add(w[i] * (delta * ratio))
                start.add(w[i] * (floored * jnp.log(floored)))
    ceiling = 0.95 / jnp.maximum(-least, 0.2375)
    bound = 0.25 * (curve.total() + 1e-6)
    entropy = start.total()

    def newton(turn, alpha):
        value, slope = Sums(), Sums()
        for i in range(Q):
            delta = load(d_ref, i)
            path = jnp.maximum(load(f_ref, i) + alpha * delta, FLOOR)
            logs = w[i] * jnp.log(path)
            value.add(path * logs)
            slope.add(delta * logs)
        change = (value.total() - entropy) / jnp.maximum(slope.total(), bound)
        return jnp.minimum(jnp.maximum(alpha - change, 1.0), ceiling)

    alpha = lax.fori_loop(0, 3, newton, jnp.full(rho.shape, 2.0, jnp.float32))
    step = alpha * beta
    for i, v in enumerate(VECTORS):
        post = jnp.where(solid == 1, rho, load(f_ref, i) + step * load(d_ref, i))
        if weighted:
            post = post * w[i]
        if v[2]:
            post = pltpu.roll(post, v[2] % LANES, 1)
        own_ref[half_rows(i, half), :] = post


def route(axis, odd_ref, even_ref, one_ref, two_ref):
    odd = lax.axis_index(axis) % 2 == 1
    a, b = odd_ref[...], even_ref[...]
    one_ref[...] = jnp.where(odd, a, b)
    two_ref[...] = jnp.where(odd, b, a)


def send_x(own_ref, xa_ref, xb_ref, up_ref, down_ref):
    for sign, out_ref in ((1, up_ref), (-1, down_ref)):
        place, _ = FACE_X[sign]
        for i, at in place.items():
            n = abs(VECTORS[i][0]) * WIDTH
            first = i * TILES + (TILES - n if sign > 0 else 0)
            out_ref[at * WIDTH : at * WIDTH + n, :] = own_ref[first : first + n, :]
    route("gx", up_ref, down_ref, xa_ref, xb_ref)


def rebuild_kernel(
    reply_ref, pick_ref, solid_ref, own_ref, xa_ref, xb_ref, col_ref, f_ref, d_ref, up_ref, down_ref
):
    level = lax.axis_index("level")
    scale = jnp.where(level == 1, SCALE_FINE, SCALE_COARSE)
    beta = jnp.where(level == 1, BETA_FINE, BETA_COARSE)
    width = reply_ref.shape[0] // MOMENTS
    pick = pick_ref[:, :width]
    step = 4
    for first in range(0, MOMENTS, step):
        block = jnp.concatenate(
            [
                reply_ref[pl.ds(n, width, stride=MOMENTS), :]
                for n in range(first, first + step)
            ],
            axis=1,
        )
        chosen = jnp.dot(
            pick, block, precision=lax.Precision.HIGHEST, preferred_element_type=jnp.float32
        )
        for k in range(step):
            n = first + k
            col_ref[n * TILES : (n + 1) * TILES, :] = chosen[:, k * LANES : (k + 1) * LANES]

    def one(half, carry):
        rebuild(col_ref, half, scale, f_ref)
        solid = solid_ref[pl.ds(pl.multiple_of(half * 8, 8), 8), :]
        collide(f_ref, d_ref, half, solid, beta, own_ref, False)
        return carry

    lax.fori_loop(0, 2, one, 0)
    send_x(own_ref, xa_ref, xb_ref, up_ref, down_ref)


def shift_x(own_ref, xa_ref, xb_ref, x_ref, ya_ref, yb_ref, low_ref, high_ref, up_ref, down_ref):
    route("gx", xb_ref, xa_ref, low_ref, high_ref)
    for i, v in enumerate(VECTORS):
        n = abs(v[0]) * WIDTH
        base = i * TILES
        if n == 0:
            x_ref[base : base + TILES, :] = own_ref[base : base + TILES, :]
        elif v[0] > 0:
            at = FACE_X[1][0][i] * WIDTH
            x_ref[base + n : base + TILES, :] = own_ref[base : base + TILES - n, :]
            x_ref[base : base + n, :] = low_ref[at : at + n, :]
        else:
            at = FACE_X[-1][0][i] * WIDTH
            x_ref[base : base + TILES - n, :] = own_ref[base + n : base + TILES, :]
            x_ref[base + TILES - n : base + TILES, :] = high_ref[at : at + n, :]
    for sign, out_ref in ((1, up_ref), (-1, down_ref)):
        place, _ = FACE_Y[sign]
        for i, at in place.items():
            n = abs(VECTORS[i][1])
            for k in range(n):
                row = WIDTH - n + k if sign > 0 else k
                out_ref[(at + k) * WIDTH : (at + k + 1) * WIDTH, :] = x_ref[
                    pl.ds(i * TILES + row, WIDTH, stride=WIDTH), :
                ]
    route("gy", up_ref, down_ref, ya_ref, yb_ref)


def assemble(x_ref, low_ref, high_ref, out_ref, first=0, last=Q):
    for i in range(first, last):
        v = VECTORS[i]
        base = i * TILES
        out_ref[base : base + TILES, :] = x_ref[base - v[1] : base - v[1] + TILES, :]
        n = abs(v[1])
        for k in range(n):
            if v[1] > 0:
                src_ref, at, row = low_ref, FACE_Y[1][0][i] + k, k
            else:
                src_ref, at, row = high_ref, FACE_Y[-1][0][i] + k, WIDTH - n + k
            out_ref[pl.ds(base + row, WIDTH, stride=WIDTH), :] = src_ref[
                at * WIDTH : (at + 1) * WIDTH, :
            ]


def second_kernel(
    x_ref, ya_ref, yb_ref, solid_ref, own_ref, xa_ref, xb_ref, f_ref, d_ref, low_ref, high_ref
):
    route("gy", yb_ref, ya_ref, low_ref, high_ref)
    assemble(x_ref, low_ref, high_ref, f_ref)

    def one(half, carry):
        solid = solid_ref[pl.ds(pl.multiple_of(half * 8, 8), 8), :]
        collide(f_ref, d_ref, half, solid, BETA_FINE, own_ref, True)
        return carry

    lax.fori_loop(0, 2, one, 0)
    send_x(own_ref, xa_ref, xb_ref, low_ref, high_ref)


PIECES = [(Q * k // 4, Q * (k + 1) // 4) for k in range(4)]


def last_kernel(weighted, x_ref, ya_ref, yb_ref, out_ref, new_ref, low_ref, high_ref, sems):
    def piece(k):
        first, last = PIECES[k]
        rows = pl.ds(first * TILES, (last - first) * TILES)
        return pltpu.make_async_copy(new_ref.at[rows, :], out_ref.at[rows, :], sems.at[k])

    route("gy", yb_ref, ya_ref, low_ref, high_ref)
    for k, (first, last) in enumerate(PIECES):
        assemble(x_ref, low_ref, high_ref, new_ref, first, last)
        if not weighted:
            for i in range(first, last):
                rows = slice(i * TILES, (i + 1) * TILES)
                new_ref[rows, :] = new_ref[rows, :] * float(WEIGHTS[i])
        piece(k).start()
    for k in range(len(PIECES)):
        piece(k).wait()


def call(kernel, outs, args, name, scratch=(), flops=4_000_000, far_outs=False, more=()):
    whole = pl.BlockSpec(memory_space=pltpu.VMEM)
    far = pl.BlockSpec(memory_space=pltpu.HBM)
    kind = pltpu.HBM if far_outs else jax.ShapeDtypeStruct
    shapes = [kind((rows, LANES), jnp.float32) for rows in outs]
    moved = sum(int(rows) * LANES for rows in outs) + sum(int(np.prod(a.shape)) for a in args)
    return pl.pallas_call(
        kernel,
        out_shape=shapes,
        in_specs=[whole] * len(args),
        out_specs=[far if far_outs else whole] * len(shapes),
        scratch_shapes=[pltpu.VMEM((rows, LANES), jnp.float32) for rows in scratch] + list(more),
        compiler_params=pltpu.CompilerParams(vmem_limit_bytes=24 << 20),
        cost_estimate=pl.CostEstimate(flops=flops, bytes_accessed=4 * moved, transcendentals=0),
        name=name,
    )(*args)


def swap_edges(first, second, axis):
    count = lax.axis_size(axis)
    odd = [(i, (i + 1) % count if i % 2 else (i - 1) % count) for i in range(count)]
    even = [(i, i ^ 1) for i in range(count)]
    return lax.ppermute(first, axis, odd), lax.ppermute(second, axis, even)


def shards(populations, solid_mask, recv_tiles, owner_gy, owner_tiles):
    peers = lax.axis_size("gy")
    count = owner_tiles.shape[-1]
    pops = populations.reshape(ROWS, LANES)
    solid = solid_mask.reshape(TILES, LANES)
    owners = owner_gy.reshape(1, count)
    wanted = owner_tiles.reshape(1, count)
    targets = recv_tiles.reshape(1, count)
    slots = peers * CAP
    (mom,) = call(moments_kernel, [MOMENTS * TILES], [pops], "moments")
    ask, pick = call(request_tables, [slots, TILES], [owners, wanted, targets], "requests")
    crossed = lax.ppermute(mom, "level", [(0, 1), (1, 0)])
    asked = lax.all_to_all(
        ask.reshape(peers, CAP, LANES), "gy", split_axis=0, concat_axis=0, tiled=True
    ).reshape(slots, LANES)
    (answer,) = call(pack_kernel, [slots * MOMENTS], [crossed, asked], "pack")
    reply = lax.all_to_all(
        answer.reshape(peers, CAP * MOMENTS, LANES), "gy", split_axis=0, concat_axis=0, tiled=True
    ).reshape(slots * MOMENTS, LANES)
    faces = [ROWS, FACE_ROWS, FACE_ROWS]
    own, xa, xb = call(
        rebuild_kernel,
        faces,
        [reply, pick, solid],
        "collide1",
        [MOMENTS * TILES, ROWS, ROWS] + [FACE_ROWS] * 2,
    )
    first, second = swap_edges(xa, xb, "gx")
    moved, ya, yb = call(
        shift_x,
        faces,
        [own, first, second],
        "shift1",
        [FACE_ROWS] * 4,
    )
    first, second = swap_edges(ya, yb, "gy")
    def last(weighted, moved, first, second):
        (out,) = call(
            functools.partial(last_kernel, weighted),
            [ROWS],
            [moved, first, second],
            "last",
            [ROWS] + [FACE_ROWS] * 2,
            far_outs=True,
            more=[pltpu.SemaphoreType.DMA((len(PIECES),))],
        )
        return out

    def fine_end(moved, first, second, solid):
        own, xa, xb = call(
            second_kernel,
            faces,
            [moved, first, second, solid],
            "collide2",
            [ROWS, ROWS] + [FACE_ROWS] * 2,
        )
        first, second = swap_edges(xa, xb, "gx")
        moved, ya, yb = call(shift_x, faces, [own, first, second], "shift2", [FACE_ROWS] * 4)
        first, second = swap_edges(ya, yb, "gy")
        return last(True, moved, first, second)

    def coarse_end(moved, first, second, solid):
        return last(False, moved, first, second)

    out = lax.cond(
        lax.axis_index("level") == 1, fine_end, coarse_end, moved, first, second, solid
    )
    return out.reshape(populations.shape)


def solution(mesh):
    placed = (
        P("level", None, "gx", "gy", None),
        P("level", "gx", "gy", None),
        P("level", "gx", "gy", None),
        P("level", "gx", "gy", None, None),
        P("level", "gx", "gy", None),
    )
    return jax.shard_map(
        shards,
        mesh=mesh,
        in_specs=placed,
        out_specs=P("level", None, "gx", "gy", None),
        check_vma=False,
    )
```

```python
import functools
import jax
import jax.numpy as jnp
import numpy as np
from jax import lax
from jax.experimental import pallas as pl
from jax.experimental.pallas import tpu as pltpu
from jax.sharding import PartitionSpec as P


CAP = 2
FLOOR = 0.05
BETA_COARSE = 0.9
BETA_FINE = 0.8
SCALE_FINE = 0.5
SCALE_COARSE = 1.5
WIDTH = 4
TILES = 16
LANES = 128
MIRROR = 3


def lattice():
    shells = [
        (0, 0, 0),
        (0, 0, 1),
        (0, 1, 1),
        (1, 1, 1),
        (0, 0, 2),
        (0, 2, 2),
        (2, 2, 2),
        (0, 0, 3),
        (0, 1, 2),
        (1, 1, 2),
    ]
    vectors = []
    for first in range(-3, 4):
        for second in range(-3, 4):
            for third in range(-3, 4):
                if tuple(sorted((abs(first), abs(second), abs(third)))) in shells:
                    vectors.append((first, second, third))
    offsets = np.array(vectors)
    speeds = offsets * 1.0
    raw = np.exp(-0.5 * np.sum(speeds * speeds, axis=1))
    total = np.sum(raw)
    weights = raw / total
    theta = float(np.sum(weights * speeds[:, 0] * speeds[:, 0]))
    return vectors, speeds, weights, theta, float(total)


VECTORS, SPEEDS, WEIGHTS, THETA, TOTAL = lattice()
Q = len(VECTORS)
ROWS = Q * TILES
INDEX = {v: i for i, v in enumerate(VECTORS)}
PAIRS = [(a, b) for a in range(3) for b in range(a, 3)]
TRIPLES = [(a, b, c) for a in range(3) for b in range(a, 3) for c in range(b, 3)]
MOMENTS = 1 + 3 + len(PAIRS) + len(TRIPLES)
GROUPS = {}
for _i, (_x, _y, _z) in enumerate(VECTORS):
    GROUPS.setdefault((_x, _y), []).append((_z, _i))


def norms():
    rows = [np.ones(Q)]
    for a in range(3):
        rows.append(SPEEDS[:, a])
    for a, b in PAIRS:
        rows.append(SPEEDS[:, a] * SPEEDS[:, b] - THETA * float(a == b))
    for a, b, c in TRIPLES:
        rows.append(
            SPEEDS[:, a] * SPEEDS[:, b] * SPEEDS[:, c]
            - THETA
            * (
                SPEEDS[:, a] * float(b == c)
                + SPEEDS[:, b] * float(a == c)
                + SPEEDS[:, c] * float(a == b)
            )
        )
    basis = np.stack(rows)
    return (basis * basis) @ WEIGHTS


NORMS = norms()


def face_layout(axis):
    sides = {}
    for sign in (1, -1):
        order = [i for n in (2, 1, 3) for i in range(Q) if VECTORS[i][axis] == sign * n]
        place, at = {}, 0
        for i in order:
            place[i] = at
            at += abs(VECTORS[i][axis])
        sides[sign] = (place, at)
    return sides


FACE_X = face_layout(0)
FACE_Y = face_layout(1)
FACE_ROWS = FACE_X[1][1] * WIDTH


def scaled(k, value):
    return value if k == 1 else value * float(k)


def combine(terms):
    total = None
    for k, value in terms:
        if k == 0:
            continue
        if total is None:
            total = scaled(k, value)
        elif k > 0:
            total = total + scaled(k, value)
        else:
            total = total - scaled(-k, value)
    return total


def tree(values):
    values = list(values)
    while len(values) > 1:
        values = [
            values[i] + values[i + 1] if i + 1 < len(values) else values[i]
            for i in range(0, len(values), 2)
        ]
    return values[0]


class Sums:
    def __init__(self, parts=4):
        self.parts = [None] * parts
        self.turn = 0

    def add(self, value):
        k = self.turn % len(self.parts)
        self.turn += 1
        self.parts[k] = value if self.parts[k] is None else self.parts[k] + value

    def total(self):
        return tree([p for p in self.parts if p is not None])


def half_rows(i, half):
    return pl.ds(pl.multiple_of(half * 8 + i * TILES, 8), 8)


def request_tables(owner_ref, wanted_ref, target_ref, ask_ref, pick_ref):
    own = owner_ref[...] ^ MIRROR
    count = own.shape[1]
    sub = lax.broadcasted_iota(jnp.int32, (count, count), 0)
    lane = lax.broadcasted_iota(jnp.int32, (count, count), 1)

    def down(row):
        return jnp.sum(
            jnp.where(sub == lane, jnp.broadcast_to(row, (count, count)), 0), axis=1, keepdims=True
        )

    same = jnp.where(
        jnp.logical_and(jnp.broadcast_to(own, (count, count)) == down(own), sub < lane), 1, 0
    )
    slot = own * CAP + jnp.sum(same, axis=0, keepdims=True)
    width = ask_ref.shape[0]
    by_slot = jnp.where(
        lax.broadcasted_iota(jnp.int32, (width, count), 0) == jnp.broadcast_to(slot, (width, count)),
        1.0,
        0.0,
    )
    wide = lax.broadcasted_iota(jnp.int32, (count, LANES), 1)
    tiles = jnp.where(wide == down(wanted_ref[...]), 1.0, 0.0)
    ask_ref[...] = jnp.dot(by_slot, tiles, preferred_element_type=jnp.float32)
    by_target = jnp.where(sub == jnp.broadcast_to(target_ref[...], (count, count)), 1.0, 0.0)
    slots = jnp.where(wide == down(slot), 1.0, 0.0)
    pick_ref[...] = jnp.dot(by_target, slots, preferred_element_type=jnp.float32)


def moments_kernel(
    pops_hbm,
    owner_hbm,
    wanted_hbm,
    target_hbm,
    mom_ref,
    ask_ref,
    pick_ref,
    pops_ref,
    owner_ref,
    wanted_ref,
    target_ref,
    sems,
):
    pairs = [
        (owner_hbm, owner_ref),
        (wanted_hbm, wanted_ref),
        (target_hbm, target_ref),
        (pops_hbm, pops_ref),
    ]
    copies = [pltpu.make_async_copy(a, b, sems.at[k]) for k, (a, b) in enumerate(pairs)]
    for copy in copies:
        copy.start()
    for copy in copies[:3]:
        copy.wait()
    request_tables(owner_ref, wanted_ref, target_ref, ask_ref, pick_ref)
    copies[3].wait()
    def one(half, carry):
        raw = {}

        def put(key, k, value):
            if k == 0:
                return
            old = raw.get(key)
            term = scaled(abs(k), value)
            if old is None:
                raw[key] = term if k > 0 else -term
            else:
                raw[key] = old + term if k > 0 else old - term

        for x in range(-3, 4):
            inner = {}
            for y in range(-3, 4):
                if (x, y) not in GROUPS:
                    continue
                f = {z: pops_ref[half_rows(i, half), :] for z, i in GROUPS[(x, y)]}
                even = {k: f[k] + f[-k] for k in (1, 2, 3) if k in f}
                odd = {k: f[k] - f[-k] for k in (1, 2, 3) if k in f}
                sums = [
                    combine([(1, f[0])] + [(1, v) for v in even.values()]),
                    combine([(k, v) for k, v in odd.items()]),
                    combine([(k * k, v) for k, v in even.items()]),
                    combine([(k * k * k, v) for k, v in odd.items()]),
                ]
                for c in range(4):
                    if sums[c] is None:
                        continue
                    for b in range(4 - c):
                        k = y**b
                        if k:
                            inner.setdefault((b, c), []).append((k, sums[c]))
            for (b, c), terms in inner.items():
                terms.sort(key=lambda t: -t[0])
                value = combine(terms) if terms[0][0] > 0 else -combine([(-k, v) for k, v in terms])
                for a in range(4 - b - c):
                    put((a, b, c), x**a, value)
        out = [raw[(0, 0, 0)], raw[(1, 0, 0)], raw[(0, 1, 0)], raw[(0, 0, 1)]]

        def power(*axes):
            return tuple(sum(1 for a in axes if a == d) for d in range(3))

        for a, b in PAIRS:
            value = raw[power(a, b)]
            out.append(value - THETA * out[0] if a == b else value)
        for a, b, c in TRIPLES:
            value = raw[power(a, b, c)]
            if a == b == c:
                value = value - (3.0 * THETA) * out[1 + a]
            elif a == b:
                value = value - THETA * out[1 + c]
            elif b == c:
                value = value - THETA * out[1 + a]
            out.append(value)
        for n in range(MOMENTS):
            mom_ref[half_rows(n, half), :] = out[n]
        return carry

    lax.fori_loop(0, 2, one, 0)


def pack_kernel(mom_ref, ask_ref, reply_ref):
    ask = ask_ref[:, :TILES]
    width = ask_ref.shape[0]
    step = 4
    for first in range(0, MOMENTS, step):
        block = jnp.concatenate(
            [mom_ref[n * TILES : (n + 1) * TILES, :] for n in range(first, first + step)], axis=1
        )
        chosen = jnp.dot(
            ask, block, precision=lax.Precision.HIGHEST, preferred_element_type=jnp.float32
        )
        for k in range(step):
            reply_ref[pl.ds(first + k, width, stride=MOMENTS), :] = chosen[
                :, k * LANES : (k + 1) * LANES
            ]


def rebuild(col_ref, half, scale, f_ref):
    a = [col_ref[half_rows(n, half), :] for n in range(MOMENTS)]
    rho = a[0]
    inverse = 1.0 / rho
    flux = a[1:4]
    speed = [v * inverse for v in flux]
    b = [a[n] * (1.0 / NORMS[n]) for n in range(4)]
    n = 4
    names = {}
    for first, second in PAIRS:
        eq = flux[first] * speed[second]
        names[(first, second)] = (eq + scale * (a[n] - eq)) * (1.0 / NORMS[n])
        n += 1
    for first, second, third in TRIPLES:
        eq = flux[first] * speed[second] * speed[third]
        names[(first, second, third)] = (eq + scale * (a[n] - eq)) * (1.0 / NORMS[n])
        n += 1
    k0 = b[0] - THETA * (names[(0, 0)] + names[(1, 1)] + names[(2, 2)])
    lin = []
    for d in range(3):
        others = [names[tuple(sorted((d, e, e)))] for e in range(3) if e != d]
        lin.append(b[1 + d] - THETA * (3.0 * names[(d, d, d)] + (others[0] + others[1])))
    cubes = {k: names[(2, 2, 2)] * float(k**3) for k in (1, 2, 3)}

    def horner(k, parts):
        value = parts[-1]
        for part in parts[-2::-1]:
            if k == 0:
                value = part
            elif k == 1:
                value = part + value
            elif k == -1:
                value = part - value
            else:
                value = part + float(k) * value
        return value

    for x in range(-3, 4):
        q = [
            horner(x, [k0, lin[0], names[(0, 0)], names[(0, 0, 0)]]),
            horner(x, [lin[1], names[(0, 1)], names[(0, 0, 1)]]),
            horner(x, [names[(1, 1)], names[(0, 1, 1)]]),
            names[(1, 1, 1)],
        ]
        r = [
            horner(x, [lin[2], names[(0, 2)], names[(0, 0, 2)]]),
            horner(x, [names[(1, 2)], names[(0, 1, 2)]]),
            names[(1, 1, 2)],
        ]
        s = [horner(x, [names[(2, 2)], names[(0, 2, 2)]]), names[(1, 2, 2)]]
        for y in range(-3, 4):
            if (x, y) not in GROUPS:
                continue
            place = dict(GROUPS[(x, y)])
            p0, p1, p2 = horner(y, q), horner(y, r), horner(y, s)
            f_ref[half_rows(place[0], half), :] = p0
            for k in (1, 2, 3):
                if k in place:
                    even = p0 + scaled(k * k, p2)
                    odd = scaled(k, p1) + cubes[k]
                    f_ref[half_rows(place[k], half), :] = even + odd
                    f_ref[half_rows(place[-k], half), :] = even - odd


def collide(f_ref, d_ref, half, solid, beta, own_ref, weighted):
    w = [float(v) for v in WEIGHTS]

    def load(ref, i):
        return ref[half_rows(i, half), :]

    rho_s, flux_s = Sums(), [Sums(2) for _ in range(3)]
    rho_s.add(w[INDEX[(0, 0, 0)]] * load(f_ref, INDEX[(0, 0, 0)]))
    for i, v in enumerate(VECTORS):
        opposite = INDEX[tuple(-c for c in v)]
        if i >= opposite:
            continue
        plus, minus = load(f_ref, opposite), load(f_ref, i)
        rho_s.add(w[i] * (plus + minus))
        odd = w[i] * (plus - minus)
        for d in range(3):
            k = -v[d]
            if k:
                flux_s[d].add(odd if k == 1 else odd * float(k))
    rho = rho_s.total()
    inverse = 1.0 / rho
    powers, gauss = [], []
    for d in range(3):
        rate = flux_s[d].total() * inverse * (1.0 / THETA)
        up, down = jnp.exp(rate), jnp.exp(-rate)
        one = {0: None, 1: up, -1: down, 2: up * up, -2: down * down}
        one[3], one[-3] = one[2] * up, one[-2] * down
        powers.append(one)
        gauss.append({k: float(np.exp(-0.5 * k * k)) for k in range(-3, 4)})

    def pair_sum(d, k):
        return (powers[d][k] + powers[d][-k]) * gauss[d][k]

    zs = [pair_sum(2, k) for k in (1, 2, 3)]
    upto = {
        (0,): 1.0,
        (0, 1): 1.0 + zs[0],
        (0, 1, 2): 1.0 + zs[0] + zs[1],
        (0, 2): 1.0 + zs[1],
        (0, 1, 2, 3): 1.0 + zs[0] + zs[1] + zs[2],
    }
    xs = [1.0] + [pair_sum(0, k) for k in (1, 2, 3)]
    ys = [1.0] + [pair_sum(1, k) for k in (1, 2, 3)]
    rows = []
    for x in range(4):
        line = []
        for y in range(4):
            if (x, y) not in GROUPS:
                continue
            key = tuple(sorted(z for z, _ in GROUPS[(x, y)] if z >= 0))
            line.append(ys[y] * upto[key])
        rows.append(xs[x] * functools.reduce(lambda p, q: p + q, line))
    norm = functools.reduce(lambda p, q: p + q, rows)
    factor = rho * float(TOTAL) / norm

    least, curve, start = None, Sums(), Sums()
    for x in range(-3, 4):
        base = factor if x == 0 else factor * powers[0][x]
        for y in range(-3, 4):
            if (x, y) not in GROUPS:
                continue
            plane = base if y == 0 else base * powers[1][y]
            for z, i in GROUPS[(x, y)]:
                f = load(f_ref, i)
                equil = plane if z == 0 else plane * powers[2][z]
                delta = equil - f
                d_ref[half_rows(i, half), :] = delta
                floored = jnp.maximum(f, FLOOR)
                ratio = delta / floored
                least = ratio if least is None else jnp.minimum(least, ratio)
                curve.add(w[i] * (delta * ratio))
                start.add(w[i] * (floored * jnp.log(floored)))
    ceiling = 0.95 / jnp.maximum(-least, 0.2375)
    bound = 0.25 * (curve.total() + 1e-6)
    entropy = start.total()

    def newton(turn, alpha):
        value, slope = Sums(), Sums()
        for i in range(Q):
            delta = load(d_ref, i)
            path = jnp.maximum(load(f_ref, i) + alpha * delta, FLOOR)
            logs = w[i] * jnp.log(path)
            value.add(path * logs)
            slope.add(delta * logs)
        change = (value.total() - entropy) / jnp.maximum(slope.total(), bound)
        return jnp.minimum(jnp.maximum(alpha - change, 1.0), ceiling)

    alpha = lax.fori_loop(0, 3, newton, jnp.full(rho.shape, 2.0, jnp.float32))
    step = alpha * beta
    for i, v in enumerate(VECTORS):
        post = jnp.where(solid == 1, rho, load(f_ref, i) + step * load(d_ref, i))
        if weighted:
            post = post * w[i]
        if v[2]:
            post = pltpu.roll(post, v[2] % LANES, 1)
        own_ref[half_rows(i, half), :] = post


def route(axis, odd_ref, even_ref, one_ref, two_ref):
    odd = lax.axis_index(axis) % 2 == 1
    a, b = odd_ref[...], even_ref[...]
    one_ref[...] = jnp.where(odd, a, b)
    two_ref[...] = jnp.where(odd, b, a)


def send_x(own_ref, xa_ref, xb_ref, up_ref, down_ref):
    for sign, out_ref in ((1, up_ref), (-1, down_ref)):
        place, _ = FACE_X[sign]
        for i, at in place.items():
            n = abs(VECTORS[i][0]) * WIDTH
            first = i * TILES + (TILES - n if sign > 0 else 0)
            out_ref[at * WIDTH : at * WIDTH + n, :] = own_ref[first : first + n, :]
    route("gx", up_ref, down_ref, xa_ref, xb_ref)


def rebuild_kernel(
    reply_ref, pick_ref, solid_ref, own_ref, xa_ref, xb_ref, col_ref, f_ref, d_ref, up_ref, down_ref
):
    level = lax.axis_index("level")
    scale = jnp.where(level == 1, SCALE_FINE, SCALE_COARSE)
    beta = jnp.where(level == 1, BETA_FINE, BETA_COARSE)
    width = reply_ref.shape[0] // MOMENTS
    pick = pick_ref[:, :width]
    step = 4
    for first in range(0, MOMENTS, step):
        block = jnp.concatenate(
            [
                reply_ref[pl.ds(n, width, stride=MOMENTS), :]
                for n in range(first, first + step)
            ],
            axis=1,
        )
        chosen = jnp.dot(
            pick, block, precision=lax.Precision.HIGHEST, preferred_element_type=jnp.float32
        )
        for k in range(step):
            n = first + k
            col_ref[n * TILES : (n + 1) * TILES, :] = chosen[:, k * LANES : (k + 1) * LANES]

    def one(half, carry):
        rebuild(col_ref, half, scale, f_ref)
        solid = solid_ref[pl.ds(pl.multiple_of(half * 8, 8), 8), :]
        collide(f_ref, d_ref, half, solid, beta, own_ref, False)
        return carry

    lax.fori_loop(0, 2, one, 0)
    send_x(own_ref, xa_ref, xb_ref, up_ref, down_ref)


def shift_x(own_ref, xa_ref, xb_ref, x_ref, ya_ref, yb_ref, low_ref, high_ref, up_ref, down_ref):
    route("gx", xb_ref, xa_ref, low_ref, high_ref)
    for i, v in enumerate(VECTORS):
        n = abs(v[0]) * WIDTH
        base = i * TILES
        if n == 0:
            x_ref[base : base + TILES, :] = own_ref[base : base + TILES, :]
        elif v[0] > 0:
            at = FACE_X[1][0][i] * WIDTH
            x_ref[base + n : base + TILES, :] = own_ref[base : base + TILES - n, :]
            x_ref[base : base + n, :] = low_ref[at : at + n, :]
        else:
            at = FACE_X[-1][0][i] * WIDTH
            x_ref[base : base + TILES - n, :] = own_ref[base + n : base + TILES, :]
            x_ref[base + TILES - n : base + TILES, :] = high_ref[at : at + n, :]
    for sign, out_ref in ((1, up_ref), (-1, down_ref)):
        place, _ = FACE_Y[sign]
        for i, at in place.items():
            n = abs(VECTORS[i][1])
            for k in range(n):
                row = WIDTH - n + k if sign > 0 else k
                out_ref[(at + k) * WIDTH : (at + k + 1) * WIDTH, :] = x_ref[
                    pl.ds(i * TILES + row, WIDTH, stride=WIDTH), :
                ]
    route("gy", up_ref, down_ref, ya_ref, yb_ref)


def assemble(x_ref, low_ref, high_ref, out_ref, first=0, last=Q):
    for i in range(first, last):
        v = VECTORS[i]
        base = i * TILES
        out_ref[base : base + TILES, :] = x_ref[base - v[1] : base - v[1] + TILES, :]
        n = abs(v[1])
        for k in range(n):
            if v[1] > 0:
                src_ref, at, row = low_ref, FACE_Y[1][0][i] + k, k
            else:
                src_ref, at, row = high_ref, FACE_Y[-1][0][i] + k, WIDTH - n + k
            out_ref[pl.ds(base + row, WIDTH, stride=WIDTH), :] = src_ref[
                at * WIDTH : (at + 1) * WIDTH, :
            ]


def second_kernel(
    x_ref, ya_ref, yb_ref, solid_ref, own_ref, xa_ref, xb_ref, f_ref, d_ref, low_ref, high_ref
):
    route("gy", yb_ref, ya_ref, low_ref, high_ref)
    assemble(x_ref, low_ref, high_ref, f_ref)

    def one(half, carry):
        solid = solid_ref[pl.ds(pl.multiple_of(half * 8, 8), 8), :]
        collide(f_ref, d_ref, half, solid, BETA_FINE, own_ref, True)
        return carry

    lax.fori_loop(0, 2, one, 0)
    send_x(own_ref, xa_ref, xb_ref, low_ref, high_ref)


PIECES = [(Q * k // 4, Q * (k + 1) // 4) for k in range(4)]


def last_kernel(weighted, x_ref, ya_ref, yb_ref, out_ref, new_ref, low_ref, high_ref, sems):
    def piece(k):
        first, last = PIECES[k]
        rows = pl.ds(first * TILES, (last - first) * TILES)
        return pltpu.make_async_copy(new_ref.at[rows, :], out_ref.at[rows, :], sems.at[k])

    route("gy", yb_ref, ya_ref, low_ref, high_ref)
    for k, (first, last) in enumerate(PIECES):
        assemble(x_ref, low_ref, high_ref, new_ref, first, last)
        if not weighted:
            for i in range(first, last):
                rows = slice(i * TILES, (i + 1) * TILES)
                new_ref[rows, :] = new_ref[rows, :] * float(WEIGHTS[i])
        piece(k).start()
    for k in range(len(PIECES)):
        piece(k).wait()


def call(kernel, outs, args, name, scratch=(), flops=4_000_000, far_args=0, far_outs=False, more=()):
    whole = pl.BlockSpec(memory_space=pltpu.VMEM)
    far = pl.BlockSpec(memory_space=pltpu.HBM)
    kind = pltpu.HBM if far_outs else jax.ShapeDtypeStruct
    shapes = [kind((rows, LANES), jnp.float32) for rows in outs]
    moved = sum(int(rows) * LANES for rows in outs) + sum(int(np.prod(a.shape)) for a in args)
    return pl.pallas_call(
        kernel,
        out_shape=shapes,
        in_specs=[far] * far_args + [whole] * (len(args) - far_args),
        out_specs=[far if far_outs else whole] * len(shapes),
        scratch_shapes=[pltpu.VMEM((rows, LANES), jnp.float32) for rows in scratch] + list(more),
        compiler_params=pltpu.CompilerParams(vmem_limit_bytes=24 << 20),
        cost_estimate=pl.CostEstimate(flops=flops, bytes_accessed=4 * moved, transcendentals=0),
        name=name,
    )(*args)


def swap_edges(first, second, axis):
    count = lax.axis_size(axis)
    odd = [(i, (i + 1) % count if i % 2 else (i - 1) % count) for i in range(count)]
    even = [(i, i ^ 1) for i in range(count)]
    return lax.ppermute(first, axis, odd), lax.ppermute(second, axis, even)


def shards(populations, solid_mask, recv_tiles, owner_gy, owner_tiles):
    peers = lax.axis_size("gy")
    count = owner_tiles.shape[-1]
    pops = populations.reshape(ROWS, LANES)
    solid = solid_mask.reshape(TILES, LANES)
    owners = owner_gy.reshape(1, count)
    wanted = owner_tiles.reshape(1, count)
    targets = recv_tiles.reshape(1, count)
    slots = peers * CAP
    tables = [owners, wanted, targets]
    mom, ask, pick = call(
        moments_kernel,
        [MOMENTS * TILES, slots, TILES],
        [pltpu.with_memory_space_constraint(a, pltpu.HBM) for a in [pops] + tables],
        "moments",
        [ROWS],
        far_args=4,
        more=[pltpu.VMEM((1, count), jnp.int32)] * 3 + [pltpu.SemaphoreType.DMA((4,))],
    )
    across = [
        (level * peers + g, (1 - level) * peers + (g ^ MIRROR))
        for level in range(lax.axis_size("level"))
        for g in range(peers)
    ]
    crossed = lax.ppermute(mom, ("level", "gy"), across)
    asked = lax.all_to_all(
        ask.reshape(peers, CAP, LANES), "gy", split_axis=0, concat_axis=0, tiled=True
    ).reshape(slots, LANES)
    (answer,) = call(pack_kernel, [slots * MOMENTS], [crossed, asked], "pack")
    reply = lax.all_to_all(
        answer.reshape(peers, CAP * MOMENTS, LANES), "gy", split_axis=0, concat_axis=0, tiled=True
    ).reshape(slots * MOMENTS, LANES)
    faces = [ROWS, FACE_ROWS, FACE_ROWS]
    own, xa, xb = call(
        rebuild_kernel,
        faces,
        [reply, pick, solid],
        "collide1",
        [MOMENTS * TILES, ROWS, ROWS] + [FACE_ROWS] * 2,
    )
    first, second = swap_edges(xa, xb, "gx")
    moved, ya, yb = call(
        shift_x,
        faces,
        [own, first, second],
        "shift1",
        [FACE_ROWS] * 4,
    )
    first, second = swap_edges(ya, yb, "gy")
    def last(weighted, moved, first, second):
        (out,) = call(
            functools.partial(last_kernel, weighted),
            [ROWS],
            [moved, first, second],
            "last",
            [ROWS] + [FACE_ROWS] * 2,
            far_outs=True,
            more=[pltpu.SemaphoreType.DMA((len(PIECES),))],
        )
        return out

    def fine_end(moved, first, second, solid):
        own, xa, xb = call(
            second_kernel,
            faces,
            [moved, first, second, solid],
            "collide2",
            [ROWS, ROWS] + [FACE_ROWS] * 2,
        )
        first, second = swap_edges(xa, xb, "gx")
        moved, ya, yb = call(shift_x, faces, [own, first, second], "shift2", [FACE_ROWS] * 4)
        first, second = swap_edges(ya, yb, "gy")
        return last(True, moved, first, second)

    def coarse_end(moved, first, second, solid):
        return last(False, moved, first, second)

    out = lax.cond(
        lax.axis_index("level") == 1, fine_end, coarse_end, moved, first, second, solid
    )
    return out.reshape(populations.shape)


def solution(mesh):
    placed = (
        P("level", None, "gx", "gy", None),
        P("level", "gx", "gy", None),
        P("level", "gx", "gy", None),
        P("level", "gx", "gy", None, None),
        P("level", "gx", "gy", None),
    )
    return jax.shard_map(
        shards,
        mesh=mesh,
        in_specs=placed,
        out_specs=P("level", None, "gx", "gy", None),
        check_vma=False,
    )
```

```python
import functools
import jax
import jax.numpy as jnp
import numpy as np
from jax import lax
from jax.experimental import pallas as pl
from jax.experimental.pallas import tpu as pltpu
from jax.sharding import PartitionSpec as P


CAP = 2
FLOOR = 0.05
BETA_COARSE = 0.9
BETA_FINE = 0.8
SCALE_FINE = 0.5
SCALE_COARSE = 1.5
WIDTH = 4
TILES = 16
LANES = 128
MIRROR = 3


def lattice():
    shells = [
        (0, 0, 0),
        (0, 0, 1),
        (0, 1, 1),
        (1, 1, 1),
        (0, 0, 2),
        (0, 2, 2),
        (2, 2, 2),
        (0, 0, 3),
        (0, 1, 2),
        (1, 1, 2),
    ]
    vectors = []
    for first in range(-3, 4):
        for second in range(-3, 4):
            for third in range(-3, 4):
                if tuple(sorted((abs(first), abs(second), abs(third)))) in shells:
                    vectors.append((first, second, third))
    offsets = np.array(vectors)
    speeds = offsets * 1.0
    raw = np.exp(-0.5 * np.sum(speeds * speeds, axis=1))
    total = np.sum(raw)
    weights = raw / total
    theta = float(np.sum(weights * speeds[:, 0] * speeds[:, 0]))
    return vectors, speeds, weights, theta, float(total)


VECTORS, SPEEDS, WEIGHTS, THETA, TOTAL = lattice()
Q = len(VECTORS)
ROWS = Q * TILES
INDEX = {v: i for i, v in enumerate(VECTORS)}
PAIRS = [(a, b) for a in range(3) for b in range(a, 3)]
TRIPLES = [(a, b, c) for a in range(3) for b in range(a, 3) for c in range(b, 3)]
MOMENTS = 1 + 3 + len(PAIRS) + len(TRIPLES)
GROUPS = {}
for _i, (_x, _y, _z) in enumerate(VECTORS):
    GROUPS.setdefault((_x, _y), []).append((_z, _i))


def norms():
    rows = [np.ones(Q)]
    for a in range(3):
        rows.append(SPEEDS[:, a])
    for a, b in PAIRS:
        rows.append(SPEEDS[:, a] * SPEEDS[:, b] - THETA * float(a == b))
    for a, b, c in TRIPLES:
        rows.append(
            SPEEDS[:, a] * SPEEDS[:, b] * SPEEDS[:, c]
            - THETA
            * (
                SPEEDS[:, a] * float(b == c)
                + SPEEDS[:, b] * float(a == c)
                + SPEEDS[:, c] * float(a == b)
            )
        )
    basis = np.stack(rows)
    return (basis * basis) @ WEIGHTS


NORMS = norms()


def face_layout(axis):
    sides = {}
    for sign in (1, -1):
        order = [i for n in (2, 1, 3) for i in range(Q) if VECTORS[i][axis] == sign * n]
        place, at = {}, 0
        for i in order:
            place[i] = at
            at += abs(VECTORS[i][axis])
        sides[sign] = (place, at)
    return sides


FACE_X = face_layout(0)
FACE_Y = face_layout(1)
FACE_ROWS = FACE_X[1][1] * WIDTH


SHELLS = {}
for _i, _v in enumerate(VECTORS):
    SHELLS.setdefault(sum(c * c for c in _v), []).append(_i)


def scaled(k, value):
    return value if k == 1 else value * float(k)


def combine(terms):
    total = None
    for k, value in terms:
        if k == 0:
            continue
        if total is None:
            total = scaled(k, value)
        elif k > 0:
            total = total + scaled(k, value)
        else:
            total = total - scaled(-k, value)
    return total


def tree(values):
    values = list(values)
    while len(values) > 1:
        values = [
            values[i] + values[i + 1] if i + 1 < len(values) else values[i]
            for i in range(0, len(values), 2)
        ]
    return values[0]


class Sums:
    def __init__(self, parts=4):
        self.parts = [None] * parts
        self.turn = 0

    def add(self, value):
        k = self.turn % len(self.parts)
        self.turn += 1
        self.parts[k] = value if self.parts[k] is None else self.parts[k] + value

    def total(self):
        return tree([p for p in self.parts if p is not None])


def half_rows(i, half):
    return pl.ds(pl.multiple_of(half * 8 + i * TILES, 8), 8)


def request_tables(owner_ref, wanted_ref, target_ref, ask_ref, pick_ref):
    own = owner_ref[...] ^ MIRROR
    count = own.shape[1]
    sub = lax.broadcasted_iota(jnp.int32, (count, count), 0)
    lane = lax.broadcasted_iota(jnp.int32, (count, count), 1)

    def down(row):
        return jnp.sum(
            jnp.where(sub == lane, jnp.broadcast_to(row, (count, count)), 0), axis=1, keepdims=True
        )

    same = jnp.where(
        jnp.logical_and(jnp.broadcast_to(own, (count, count)) == down(own), sub < lane), 1, 0
    )
    slot = own * CAP + jnp.sum(same, axis=0, keepdims=True)
    width = ask_ref.shape[0]
    by_slot = jnp.where(
        lax.broadcasted_iota(jnp.int32, (width, count), 0) == jnp.broadcast_to(slot, (width, count)),
        1.0,
        0.0,
    )
    wide = lax.broadcasted_iota(jnp.int32, (count, LANES), 1)
    tiles = jnp.where(wide == down(wanted_ref[...]), 1.0, 0.0)
    ask_ref[...] = jnp.dot(by_slot, tiles, preferred_element_type=jnp.float32)
    by_target = jnp.where(sub == jnp.broadcast_to(target_ref[...], (count, count)), 1.0, 0.0)
    slots = jnp.where(wide == down(slot), 1.0, 0.0)
    pick_ref[...] = jnp.dot(by_target, slots, preferred_element_type=jnp.float32)


def moments_kernel(
    pops_hbm,
    owner_hbm,
    wanted_hbm,
    target_hbm,
    mom_ref,
    ask_ref,
    pick_ref,
    pops_ref,
    owner_ref,
    wanted_ref,
    target_ref,
    sems,
):
    pairs = [
        (owner_hbm, owner_ref),
        (wanted_hbm, wanted_ref),
        (target_hbm, target_ref),
        (pops_hbm, pops_ref),
    ]
    copies = [pltpu.make_async_copy(a, b, sems.at[k]) for k, (a, b) in enumerate(pairs)]
    for copy in copies:
        copy.start()
    for copy in copies[:3]:
        copy.wait()
    request_tables(owner_ref, wanted_ref, target_ref, ask_ref, pick_ref)
    copies[3].wait()
    def one(half, carry):
        raw = {}

        def put(key, k, value):
            if k == 0:
                return
            old = raw.get(key)
            term = scaled(abs(k), value)
            if old is None:
                raw[key] = term if k > 0 else -term
            else:
                raw[key] = old + term if k > 0 else old - term

        for x in range(-3, 4):
            inner = {}
            for y in range(-3, 4):
                if (x, y) not in GROUPS:
                    continue
                f = {z: pops_ref[half_rows(i, half), :] for z, i in GROUPS[(x, y)]}
                even = {k: f[k] + f[-k] for k in (1, 2, 3) if k in f}
                odd = {k: f[k] - f[-k] for k in (1, 2, 3) if k in f}
                sums = [
                    combine([(1, f[0])] + [(1, v) for v in even.values()]),
                    combine([(k, v) for k, v in odd.items()]),
                    combine([(k * k, v) for k, v in even.items()]),
                    combine([(k * k * k, v) for k, v in odd.items()]),
                ]
                for c in range(4):
                    if sums[c] is None:
                        continue
                    for b in range(4 - c):
                        k = y**b
                        if k:
                            inner.setdefault((b, c), []).append((k, sums[c]))
            for (b, c), terms in inner.items():
                terms.sort(key=lambda t: -t[0])
                value = combine(terms) if terms[0][0] > 0 else -combine([(-k, v) for k, v in terms])
                for a in range(4 - b - c):
                    put((a, b, c), x**a, value)
        out = [raw[(0, 0, 0)], raw[(1, 0, 0)], raw[(0, 1, 0)], raw[(0, 0, 1)]]

        def power(*axes):
            return tuple(sum(1 for a in axes if a == d) for d in range(3))

        for a, b in PAIRS:
            value = raw[power(a, b)]
            out.append(value - THETA * out[0] if a == b else value)
        for a, b, c in TRIPLES:
            value = raw[power(a, b, c)]
            if a == b == c:
                value = value - (3.0 * THETA) * out[1 + a]
            elif a == b:
                value = value - THETA * out[1 + c]
            elif b == c:
                value = value - THETA * out[1 + a]
            out.append(value)
        for n in range(MOMENTS):
            mom_ref[half_rows(n, half), :] = out[n]
        return carry

    lax.fori_loop(0, 2, one, 0)


def pack_kernel(mom_ref, ask_ref, reply_ref):
    ask = ask_ref[:, :TILES]
    width = ask_ref.shape[0]
    step = 4
    for first in range(0, MOMENTS, step):
        block = jnp.concatenate(
            [mom_ref[n * TILES : (n + 1) * TILES, :] for n in range(first, first + step)], axis=1
        )
        chosen = jnp.dot(
            ask, block, precision=lax.Precision.HIGHEST, preferred_element_type=jnp.float32
        )
        for k in range(step):
            reply_ref[pl.ds(first + k, width, stride=MOMENTS), :] = chosen[
                :, k * LANES : (k + 1) * LANES
            ]


def rebuild(col_ref, half, scale, f_ref):
    a = [col_ref[half_rows(n, half), :] for n in range(MOMENTS)]
    rho = a[0]
    inverse = 1.0 / rho
    flux = a[1:4]
    speed = [v * inverse for v in flux]
    b = [a[n] * (1.0 / NORMS[n]) for n in range(4)]
    n = 4
    names = {}
    for first, second in PAIRS:
        eq = flux[first] * speed[second]
        names[(first, second)] = (eq + scale * (a[n] - eq)) * (1.0 / NORMS[n])
        n += 1
    for first, second, third in TRIPLES:
        eq = flux[first] * speed[second] * speed[third]
        names[(first, second, third)] = (eq + scale * (a[n] - eq)) * (1.0 / NORMS[n])
        n += 1
    k0 = b[0] - THETA * (names[(0, 0)] + names[(1, 1)] + names[(2, 2)])
    lin = []
    for d in range(3):
        others = [names[tuple(sorted((d, e, e)))] for e in range(3) if e != d]
        lin.append(b[1 + d] - THETA * (3.0 * names[(d, d, d)] + (others[0] + others[1])))
    cubes = {k: names[(2, 2, 2)] * float(k**3) for k in (1, 2, 3)}

    def horner(k, parts):
        value = parts[-1]
        for part in parts[-2::-1]:
            if k == 0:
                value = part
            elif k == 1:
                value = part + value
            elif k == -1:
                value = part - value
            else:
                value = part + float(k) * value
        return value

    for x in range(-3, 4):
        q = [
            horner(x, [k0, lin[0], names[(0, 0)], names[(0, 0, 0)]]),
            horner(x, [lin[1], names[(0, 1)], names[(0, 0, 1)]]),
            horner(x, [names[(1, 1)], names[(0, 1, 1)]]),
            names[(1, 1, 1)],
        ]
        r = [
            horner(x, [lin[2], names[(0, 2)], names[(0, 0, 2)]]),
            horner(x, [names[(1, 2)], names[(0, 1, 2)]]),
            names[(1, 1, 2)],
        ]
        s = [horner(x, [names[(2, 2)], names[(0, 2, 2)]]), names[(1, 2, 2)]]
        for y in range(-3, 4):
            if (x, y) not in GROUPS:
                continue
            place = dict(GROUPS[(x, y)])
            p0, p1, p2 = horner(y, q), horner(y, r), horner(y, s)
            f_ref[half_rows(place[0], half), :] = p0
            for k in (1, 2, 3):
                if k in place:
                    even = p0 + scaled(k * k, p2)
                    odd = scaled(k, p1) + cubes[k]
                    f_ref[half_rows(place[k], half), :] = even + odd
                    f_ref[half_rows(place[-k], half), :] = even - odd


def collide(f_ref, d_ref, half, solid, beta, own_ref, weighted):
    w = [float(v) for v in WEIGHTS]

    def load(ref, i):
        return ref[half_rows(i, half), :]

    rho_s, flux_s = Sums(), [Sums(2) for _ in range(3)]
    rho_s.add(w[INDEX[(0, 0, 0)]] * load(f_ref, INDEX[(0, 0, 0)]))
    for i, v in enumerate(VECTORS):
        opposite = INDEX[tuple(-c for c in v)]
        if i >= opposite:
            continue
        plus, minus = load(f_ref, opposite), load(f_ref, i)
        rho_s.add(w[i] * (plus + minus))
        odd = w[i] * (plus - minus)
        for d in range(3):
            k = -v[d]
            if k:
                flux_s[d].add(odd if k == 1 else odd * float(k))
    rho = rho_s.total()
    inverse = 1.0 / rho
    powers, gauss = [], []
    for d in range(3):
        rate = flux_s[d].total() * inverse * (1.0 / THETA)
        up, down = jnp.exp(rate), jnp.exp(-rate)
        one = {0: None, 1: up, -1: down, 2: up * up, -2: down * down}
        one[3], one[-3] = one[2] * up, one[-2] * down
        powers.append(one)
        gauss.append({k: float(np.exp(-0.5 * k * k)) for k in range(-3, 4)})

    def pair_sum(d, k):
        return (powers[d][k] + powers[d][-k]) * gauss[d][k]

    zs = [pair_sum(2, k) for k in (1, 2, 3)]
    upto = {
        (0,): 1.0,
        (0, 1): 1.0 + zs[0],
        (0, 1, 2): 1.0 + zs[0] + zs[1],
        (0, 2): 1.0 + zs[1],
        (0, 1, 2, 3): 1.0 + zs[0] + zs[1] + zs[2],
    }
    xs = [1.0] + [pair_sum(0, k) for k in (1, 2, 3)]
    ys = [1.0] + [pair_sum(1, k) for k in (1, 2, 3)]
    rows = []
    for x in range(4):
        line = []
        for y in range(4):
            if (x, y) not in GROUPS:
                continue
            key = tuple(sorted(z for z, _ in GROUPS[(x, y)] if z >= 0))
            line.append(ys[y] * upto[key])
        rows.append(xs[x] * functools.reduce(lambda p, q: p + q, line))
    norm = functools.reduce(lambda p, q: p + q, rows)
    factor = rho * float(TOTAL) / norm

    least = None
    curves = {n: Sums(2) for n in SHELLS}
    starts = {n: Sums(2) for n in SHELLS}
    for x in range(-3, 4):
        base = factor if x == 0 else factor * powers[0][x]
        for y in range(-3, 4):
            if (x, y) not in GROUPS:
                continue
            plane = base if y == 0 else base * powers[1][y]
            for z, i in GROUPS[(x, y)]:
                f = load(f_ref, i)
                equil = plane if z == 0 else plane * powers[2][z]
                delta = equil - f
                d_ref[half_rows(i, half), :] = delta
                floored = jnp.maximum(f, FLOOR)
                ratio = delta / floored
                least = ratio if least is None else jnp.minimum(least, ratio)
                shell = x * x + y * y + z * z
                curves[shell].add(delta * ratio)
                starts[shell].add(floored * jnp.log(floored))
    ceiling = 0.95 / jnp.maximum(-least, 0.2375)
    of_shell = {n: w[members[0]] for n, members in SHELLS.items()}
    bound = 0.25 * (tree(of_shell[n] * curves[n].total() for n in SHELLS) + 1e-6)
    entropy = tree(of_shell[n] * starts[n].total() for n in SHELLS)

    def newton(turn, alpha):
        value, slope = Sums(), Sums()
        for members in SHELLS.values():
            of_value, of_slope = Sums(), Sums()
            for i in members:
                delta = load(d_ref, i)
                path = jnp.maximum(load(f_ref, i) + alpha * delta, FLOOR)
                logs = jnp.log(path)
                of_value.add(path * logs)
                of_slope.add(delta * logs)
            value.add(w[members[0]] * of_value.total())
            slope.add(w[members[0]] * of_slope.total())
        change = (value.total() - entropy) / jnp.maximum(slope.total(), bound)
        return jnp.minimum(jnp.maximum(alpha - change, 1.0), ceiling)

    alpha = lax.fori_loop(0, 3, newton, jnp.full(rho.shape, 2.0, jnp.float32))
    step = alpha * beta
    for i, v in enumerate(VECTORS):
        post = jnp.where(solid == 1, rho, load(f_ref, i) + step * load(d_ref, i))
        if weighted:
            post = post * w[i]
        if v[2]:
            post = pltpu.roll(post, v[2] % LANES, 1)
        own_ref[half_rows(i, half), :] = post


def route(axis, odd_ref, even_ref, one_ref, two_ref):
    odd = lax.axis_index(axis) % 2 == 1
    a, b = odd_ref[...], even_ref[...]
    one_ref[...] = jnp.where(odd, a, b)
    two_ref[...] = jnp.where(odd, b, a)


def send_x(own_ref, xa_ref, xb_ref, up_ref, down_ref):
    for sign, out_ref in ((1, up_ref), (-1, down_ref)):
        place, _ = FACE_X[sign]
        for i, at in place.items():
            n = abs(VECTORS[i][0]) * WIDTH
            first = i * TILES + (TILES - n if sign > 0 else 0)
            out_ref[at * WIDTH : at * WIDTH + n, :] = own_ref[first : first + n, :]
    route("gx", up_ref, down_ref, xa_ref, xb_ref)


def rebuild_kernel(
    reply_ref, pick_ref, solid_ref, own_ref, xa_ref, xb_ref, col_ref, f_ref, d_ref, up_ref, down_ref
):
    level = lax.axis_index("level")
    scale = jnp.where(level == 1, SCALE_FINE, SCALE_COARSE)
    beta = jnp.where(level == 1, BETA_FINE, BETA_COARSE)
    width = reply_ref.shape[0] // MOMENTS
    pick = pick_ref[:, :width]
    step = 4
    for first in range(0, MOMENTS, step):
        block = jnp.concatenate(
            [
                reply_ref[pl.ds(n, width, stride=MOMENTS), :]
                for n in range(first, first + step)
            ],
            axis=1,
        )
        chosen = jnp.dot(
            pick, block, precision=lax.Precision.HIGHEST, preferred_element_type=jnp.float32
        )
        for k in range(step):
            n = first + k
            col_ref[n * TILES : (n + 1) * TILES, :] = chosen[:, k * LANES : (k + 1) * LANES]

    def one(half, carry):
        rebuild(col_ref, half, scale, f_ref)
        solid = solid_ref[pl.ds(pl.multiple_of(half * 8, 8), 8), :]
        collide(f_ref, d_ref, half, solid, beta, own_ref, False)
        return carry

    lax.fori_loop(0, 2, one, 0)
    send_x(own_ref, xa_ref, xb_ref, up_ref, down_ref)


def shift_x(own_ref, xa_ref, xb_ref, x_ref, ya_ref, yb_ref, low_ref, high_ref, up_ref, down_ref):
    route("gx", xb_ref, xa_ref, low_ref, high_ref)
    for i, v in enumerate(VECTORS):
        n = abs(v[0]) * WIDTH
        base = i * TILES
        if n == 0:
            x_ref[base : base + TILES, :] = own_ref[base : base + TILES, :]
        elif v[0] > 0:
            at = FACE_X[1][0][i] * WIDTH
            x_ref[base + n : base + TILES, :] = own_ref[base : base + TILES - n, :]
            x_ref[base : base + n, :] = low_ref[at : at + n, :]
        else:
            at = FACE_X[-1][0][i] * WIDTH
            x_ref[base : base + TILES - n, :] = own_ref[base + n : base + TILES, :]
            x_ref[base + TILES - n : base + TILES, :] = high_ref[at : at + n, :]
    for sign, out_ref in ((1, up_ref), (-1, down_ref)):
        place, _ = FACE_Y[sign]
        for i, at in place.items():
            n = abs(VECTORS[i][1])
            for k in range(n):
                row = WIDTH - n + k if sign > 0 else k
                out_ref[(at + k) * WIDTH : (at + k + 1) * WIDTH, :] = x_ref[
                    pl.ds(i * TILES + row, WIDTH, stride=WIDTH), :
                ]
    route("gy", up_ref, down_ref, ya_ref, yb_ref)


def shift_x_near(own_ref, xa_ref, xb_ref, x_ref, yb_ref, ya_ref, *scratch):
    shift_x(own_ref, xa_ref, xb_ref, x_ref, ya_ref, yb_ref, *scratch)


def assemble(x_ref, low_ref, high_ref, out_ref, first=0, last=Q):
    for i in range(first, last):
        v = VECTORS[i]
        base = i * TILES
        out_ref[base : base + TILES, :] = x_ref[base - v[1] : base - v[1] + TILES, :]
        n = abs(v[1])
        for k in range(n):
            if v[1] > 0:
                src_ref, at, row = low_ref, FACE_Y[1][0][i] + k, k
            else:
                src_ref, at, row = high_ref, FACE_Y[-1][0][i] + k, WIDTH - n + k
            out_ref[pl.ds(base + row, WIDTH, stride=WIDTH), :] = src_ref[
                at * WIDTH : (at + 1) * WIDTH, :
            ]


def second_kernel(
    x_ref, ya_ref, yb_ref, solid_ref, own_ref, xa_ref, xb_ref, f_ref, d_ref, low_ref, high_ref
):
    route("gy", yb_ref, ya_ref, low_ref, high_ref)
    assemble(x_ref, low_ref, high_ref, f_ref)

    def one(half, carry):
        solid = solid_ref[pl.ds(pl.multiple_of(half * 8, 8), 8), :]
        collide(f_ref, d_ref, half, solid, BETA_FINE, own_ref, True)
        return carry

    lax.fori_loop(0, 2, one, 0)
    send_x(own_ref, xa_ref, xb_ref, low_ref, high_ref)


PIECES = [(Q * k // 4, Q * (k + 1) // 4) for k in range(4)]


def last_kernel(weighted, x_ref, ya_ref, yb_ref, out_ref, new_ref, low_ref, high_ref, sems):
    def piece(k):
        first, last = PIECES[k]
        rows = pl.ds(first * TILES, (last - first) * TILES)
        return pltpu.make_async_copy(new_ref.at[rows, :], out_ref.at[rows, :], sems.at[k])

    route("gy", yb_ref, ya_ref, low_ref, high_ref)
    for k, (first, last) in enumerate(PIECES):
        assemble(x_ref, low_ref, high_ref, new_ref, first, last)
        if not weighted:
            for i in range(first, last):
                rows = slice(i * TILES, (i + 1) * TILES)
                new_ref[rows, :] = new_ref[rows, :] * float(WEIGHTS[i])
        piece(k).start()
    for k in range(len(PIECES)):
        piece(k).wait()


def call(kernel, outs, args, name, scratch=(), flops=4_000_000, far_args=0, far_outs=False, more=()):
    whole = pl.BlockSpec(memory_space=pltpu.VMEM)
    far = pl.BlockSpec(memory_space=pltpu.HBM)
    kind = pltpu.HBM if far_outs else jax.ShapeDtypeStruct
    shapes = [kind((rows, LANES), jnp.float32) for rows in outs]
    moved = sum(int(rows) * LANES for rows in outs) + sum(int(np.prod(a.shape)) for a in args)
    return pl.pallas_call(
        kernel,
        out_shape=shapes,
        in_specs=[far] * far_args + [whole] * (len(args) - far_args),
        out_specs=[far if far_outs else whole] * len(shapes),
        scratch_shapes=[pltpu.VMEM((rows, LANES), jnp.float32) for rows in scratch] + list(more),
        compiler_params=pltpu.CompilerParams(vmem_limit_bytes=24 << 20),
        cost_estimate=pl.CostEstimate(flops=flops, bytes_accessed=4 * moved, transcendentals=0),
        name=name,
    )(*args)


def swap_edges(first, second, axis, near_first=False):
    count = lax.axis_size(axis)
    odd = [(i, (i + 1) % count if i % 2 else (i - 1) % count) for i in range(count)]
    even = [(i, i ^ 1) for i in range(count)]
    if near_first:
        near = lax.ppermute(second, axis, even)
        return lax.ppermute(first, axis, odd), near
    return lax.ppermute(first, axis, odd), lax.ppermute(second, axis, even)


def shards(populations, solid_mask, recv_tiles, owner_gy, owner_tiles):
    peers = lax.axis_size("gy")
    count = owner_tiles.shape[-1]
    pops = populations.reshape(ROWS, LANES)
    solid = solid_mask.reshape(TILES, LANES)
    owners = owner_gy.reshape(1, count)
    wanted = owner_tiles.reshape(1, count)
    targets = recv_tiles.reshape(1, count)
    slots = peers * CAP
    tables = [owners, wanted, targets]
    mom, ask, pick = call(
        moments_kernel,
        [MOMENTS * TILES, slots, TILES],
        [pltpu.with_memory_space_constraint(a, pltpu.HBM) for a in [pops] + tables],
        "moments",
        [ROWS],
        far_args=4,
        more=[pltpu.VMEM((1, count), jnp.int32)] * 3 + [pltpu.SemaphoreType.DMA((4,))],
    )
    across = [
        (level * peers + g, (1 - level) * peers + (g ^ MIRROR))
        for level in range(lax.axis_size("level"))
        for g in range(peers)
    ]
    crossed = lax.ppermute(mom, ("level", "gy"), across)
    asked = lax.all_to_all(
        ask.reshape(peers, CAP, LANES), "gy", split_axis=0, concat_axis=0, tiled=True
    ).reshape(slots, LANES)
    (answer,) = call(pack_kernel, [slots * MOMENTS], [crossed, asked], "pack")
    reply = lax.all_to_all(
        answer.reshape(peers, CAP * MOMENTS, LANES), "gy", split_axis=0, concat_axis=0, tiled=True
    ).reshape(slots * MOMENTS, LANES)
    faces = [ROWS, FACE_ROWS, FACE_ROWS]
    own, xa, xb = call(
        rebuild_kernel,
        faces,
        [reply, pick, solid],
        "collide1",
        [MOMENTS * TILES, ROWS, ROWS] + [FACE_ROWS] * 2,
    )
    first, second = swap_edges(xa, xb, "gx")
    moved, ya, yb = call(
        shift_x,
        faces,
        [own, first, second],
        "shift1",
        [FACE_ROWS] * 4,
    )
    first, second = swap_edges(ya, yb, "gy")
    def last(weighted, moved, first, second):
        (out,) = call(
            functools.partial(last_kernel, weighted),
            [ROWS],
            [moved, first, second],
            "last",
            [ROWS] + [FACE_ROWS] * 2,
            far_outs=True,
            more=[pltpu.SemaphoreType.DMA((len(PIECES),))],
        )
        return out

    def fine_end(moved, first, second, solid):
        own, xa, xb = call(
            second_kernel,
            faces,
            [moved, first, second, solid],
            "collide2",
            [ROWS, ROWS] + [FACE_ROWS] * 2,
        )
        first, second = swap_edges(xa, xb, "gx")
        moved, yb, ya = call(shift_x_near, faces, [own, first, second], "shift2", [FACE_ROWS] * 4)
        first, second = swap_edges(ya, yb, "gy", True)
        return last(True, moved, first, second)

    def coarse_end(moved, first, second, solid):
        return last(False, moved, first, second)

    out = lax.cond(
        lax.axis_index("level") == 1, fine_end, coarse_end, moved, first, second, solid
    )
    return out.reshape(populations.shape)


def solution(mesh):
    placed = (
        P("level", None, "gx", "gy", None),
        P("level", "gx", "gy", None),
        P("level", "gx", "gy", None),
        P("level", "gx", "gy", None, None),
        P("level", "gx", "gy", None),
    )
    return jax.shard_map(
        shards,
        mesh=mesh,
        in_specs=placed,
        out_specs=P("level", None, "gx", "gy", None),
        check_vma=False,
    )
```

```python
import functools
import jax
import jax.numpy as jnp
import numpy as np
from jax import lax
from jax.experimental import pallas as pl
from jax.experimental.pallas import tpu as pltpu
from jax.sharding import PartitionSpec as P


CAP = 2
FLOOR = 0.05
BETA_COARSE = 0.9
BETA_FINE = 0.8
SCALE_FINE = 0.5
SCALE_COARSE = 1.5
WIDTH = 4
TILES = 16
LANES = 128
MIRROR = 3


def lattice():
    shells = [
        (0, 0, 0),
        (0, 0, 1),
        (0, 1, 1),
        (1, 1, 1),
        (0, 0, 2),
        (0, 2, 2),
        (2, 2, 2),
        (0, 0, 3),
        (0, 1, 2),
        (1, 1, 2),
    ]
    vectors = []
    for first in range(-3, 4):
        for second in range(-3, 4):
            for third in range(-3, 4):
                if tuple(sorted((abs(first), abs(second), abs(third)))) in shells:
                    vectors.append((first, second, third))
    offsets = np.array(vectors)
    speeds = offsets * 1.0
    raw = np.exp(-0.5 * np.sum(speeds * speeds, axis=1))
    total = np.sum(raw)
    weights = raw / total
    theta = float(np.sum(weights * speeds[:, 0] * speeds[:, 0]))
    return vectors, speeds, weights, theta, float(total)


VECTORS, SPEEDS, WEIGHTS, THETA, TOTAL = lattice()
Q = len(VECTORS)
ROWS = Q * TILES
INDEX = {v: i for i, v in enumerate(VECTORS)}
PAIRS = [(a, b) for a in range(3) for b in range(a, 3)]
TRIPLES = [(a, b, c) for a in range(3) for b in range(a, 3) for c in range(b, 3)]
MOMENTS = 1 + 3 + len(PAIRS) + len(TRIPLES)
GROUPS = {}
for _i, (_x, _y, _z) in enumerate(VECTORS):
    GROUPS.setdefault((_x, _y), []).append((_z, _i))


def norms():
    rows = [np.ones(Q)]
    for a in range(3):
        rows.append(SPEEDS[:, a])
    for a, b in PAIRS:
        rows.append(SPEEDS[:, a] * SPEEDS[:, b] - THETA * float(a == b))
    for a, b, c in TRIPLES:
        rows.append(
            SPEEDS[:, a] * SPEEDS[:, b] * SPEEDS[:, c]
            - THETA
            * (
                SPEEDS[:, a] * float(b == c)
                + SPEEDS[:, b] * float(a == c)
                + SPEEDS[:, c] * float(a == b)
            )
        )
    basis = np.stack(rows)
    return (basis * basis) @ WEIGHTS


NORMS = norms()


def face_layout(axis):
    sides = {}
    for sign in (1, -1):
        order = [i for n in (2, 1, 3) for i in range(Q) if VECTORS[i][axis] == sign * n]
        place, at = {}, 0
        for i in order:
            place[i] = at
            at += abs(VECTORS[i][axis])
        sides[sign] = (place, at)
    return sides


FACE_X = face_layout(0)
FACE_Y = face_layout(1)
FACE_ROWS = FACE_X[1][1] * WIDTH


SHELLS = {}
for _i, _v in enumerate(VECTORS):
    SHELLS.setdefault(sum(c * c for c in _v), []).append(_i)


def scaled(k, value):
    return value if k == 1 else value * float(k)


def combine(terms):
    total = None
    for k, value in terms:
        if k == 0:
            continue
        if total is None:
            total = scaled(k, value)
        elif k > 0:
            total = total + scaled(k, value)
        else:
            total = total - scaled(-k, value)
    return total


def tree(values):
    values = list(values)
    while len(values) > 1:
        values = [
            values[i] + values[i + 1] if i + 1 < len(values) else values[i]
            for i in range(0, len(values), 2)
        ]
    return values[0]


class Sums:
    def __init__(self, parts=4):
        self.parts = [None] * parts
        self.turn = 0

    def add(self, value):
        k = self.turn % len(self.parts)
        self.turn += 1
        self.parts[k] = value if self.parts[k] is None else self.parts[k] + value

    def total(self):
        return tree([p for p in self.parts if p is not None])


def half_rows(i, half):
    return pl.ds(pl.multiple_of(half * 8 + i * TILES, 8), 8)


def request_tables(owner_ref, wanted_ref, target_ref, ask_ref, pick_ref):
    own = owner_ref[...] ^ MIRROR
    count = own.shape[1]
    sub = lax.broadcasted_iota(jnp.int32, (count, count), 0)
    lane = lax.broadcasted_iota(jnp.int32, (count, count), 1)

    def down(row):
        return jnp.sum(
            jnp.where(sub == lane, jnp.broadcast_to(row, (count, count)), 0), axis=1, keepdims=True
        )

    same = jnp.where(
        jnp.logical_and(jnp.broadcast_to(own, (count, count)) == down(own), sub < lane), 1, 0
    )
    slot = own * CAP + jnp.sum(same, axis=0, keepdims=True)
    width = ask_ref.shape[0]
    by_slot = jnp.where(
        lax.broadcasted_iota(jnp.int32, (width, count), 0) == jnp.broadcast_to(slot, (width, count)),
        1.0,
        0.0,
    )
    wide = lax.broadcasted_iota(jnp.int32, (count, LANES), 1)
    tiles = jnp.where(wide == down(wanted_ref[...]), 1.0, 0.0)
    ask_ref[...] = jnp.dot(by_slot, tiles, preferred_element_type=jnp.float32)
    by_target = jnp.where(sub == jnp.broadcast_to(target_ref[...], (count, count)), 1.0, 0.0)
    slots = jnp.where(wide == down(slot), 1.0, 0.0)
    pick_ref[...] = jnp.dot(by_target, slots, preferred_element_type=jnp.float32)


def moments_kernel(
    pops_hbm,
    owner_hbm,
    wanted_hbm,
    target_hbm,
    mom_ref,
    ask_ref,
    pick_ref,
    pops_ref,
    owner_ref,
    wanted_ref,
    target_ref,
    sems,
):
    tables = [(owner_hbm, owner_ref), (wanted_hbm, wanted_ref), (target_hbm, target_ref)]
    copies = [pltpu.make_async_copy(a, b, sems.at[k]) for k, (a, b) in enumerate(tables)]
    planes = {}
    for x in range(-3, 4):
        members = [i for i, v in enumerate(VECTORS) if v[0] == x]
        rows = pl.ds(members[0] * TILES, len(members) * TILES)
        planes[x] = pltpu.make_async_copy(
            pops_hbm.at[rows, :], pops_ref.at[rows, :], sems.at[len(tables) + 3 + x]
        )
    for copy in copies + list(planes.values()):
        copy.start()
    for copy in copies:
        copy.wait()
    request_tables(owner_ref, wanted_ref, target_ref, ask_ref, pick_ref)
    raws = [{}, {}]

    def put(raw, key, k, value):
        if k == 0:
            return
        old = raw.get(key)
        term = scaled(abs(k), value)
        if old is None:
            raw[key] = term if k > 0 else -term
        else:
            raw[key] = old + term if k > 0 else old - term

    for x in range(-3, 4):
        planes[x].wait()
        for half in range(2):
            inner = {}
            for y in range(-3, 4):
                if (x, y) not in GROUPS:
                    continue
                f = {}
                for z, i in GROUPS[(x, y)]:
                    at = i * TILES + half * 8
                    f[z] = pops_ref[at : at + 8, :]
                even = {k: f[k] + f[-k] for k in (1, 2, 3) if k in f}
                odd = {k: f[k] - f[-k] for k in (1, 2, 3) if k in f}
                sums = [
                    combine([(1, f[0])] + [(1, v) for v in even.values()]),
                    combine([(k, v) for k, v in odd.items()]),
                    combine([(k * k, v) for k, v in even.items()]),
                    combine([(k * k * k, v) for k, v in odd.items()]),
                ]
                for c in range(4):
                    if sums[c] is None:
                        continue
                    for b in range(4 - c):
                        k = y**b
                        if k:
                            inner.setdefault((b, c), []).append((k, sums[c]))
            for (b, c), terms in inner.items():
                terms.sort(key=lambda t: -t[0])
                value = combine(terms) if terms[0][0] > 0 else -combine([(-k, v) for k, v in terms])
                for a in range(4 - b - c):
                    put(raws[half], (a, b, c), x**a, value)

    def power(*axes):
        return tuple(sum(1 for a in axes if a == d) for d in range(3))

    for half in range(2):
        raw = raws[half]
        out = [raw[(0, 0, 0)], raw[(1, 0, 0)], raw[(0, 1, 0)], raw[(0, 0, 1)]]
        for a, b in PAIRS:
            value = raw[power(a, b)]
            out.append(value - THETA * out[0] if a == b else value)
        for a, b, c in TRIPLES:
            value = raw[power(a, b, c)]
            if a == b == c:
                value = value - (3.0 * THETA) * out[1 + a]
            elif a == b:
                value = value - THETA * out[1 + c]
            elif b == c:
                value = value - THETA * out[1 + a]
            out.append(value)
        for n in range(MOMENTS):
            at = n * TILES + half * 8
            mom_ref[at : at + 8, :] = out[n]


def pack_kernel(mom_ref, ask_ref, reply_ref):
    ask = ask_ref[:, :TILES]
    width = ask_ref.shape[0]
    step = 4
    for first in range(0, MOMENTS, step):
        block = jnp.concatenate(
            [mom_ref[n * TILES : (n + 1) * TILES, :] for n in range(first, first + step)], axis=1
        )
        chosen = jnp.dot(
            ask, block, precision=lax.Precision.HIGHEST, preferred_element_type=jnp.float32
        )
        for k in range(step):
            reply_ref[pl.ds(first + k, width, stride=MOMENTS), :] = chosen[
                :, k * LANES : (k + 1) * LANES
            ]


def rebuild(col_ref, half, scale, f_ref):
    a = [col_ref[half_rows(n, half), :] for n in range(MOMENTS)]
    rho = a[0]
    inverse = 1.0 / rho
    flux = a[1:4]
    speed = [v * inverse for v in flux]
    b = [a[n] * (1.0 / NORMS[n]) for n in range(4)]
    n = 4
    names = {}
    for first, second in PAIRS:
        eq = flux[first] * speed[second]
        names[(first, second)] = (eq + scale * (a[n] - eq)) * (1.0 / NORMS[n])
        n += 1
    for first, second, third in TRIPLES:
        eq = flux[first] * speed[second] * speed[third]
        names[(first, second, third)] = (eq + scale * (a[n] - eq)) * (1.0 / NORMS[n])
        n += 1
    k0 = b[0] - THETA * (names[(0, 0)] + names[(1, 1)] + names[(2, 2)])
    lin = []
    for d in range(3):
        others = [names[tuple(sorted((d, e, e)))] for e in range(3) if e != d]
        lin.append(b[1 + d] - THETA * (3.0 * names[(d, d, d)] + (others[0] + others[1])))
    cubes = {k: names[(2, 2, 2)] * float(k**3) for k in (1, 2, 3)}

    def horner(k, parts):
        value = parts[-1]
        for part in parts[-2::-1]:
            if k == 0:
                value = part
            elif k == 1:
                value = part + value
            elif k == -1:
                value = part - value
            else:
                value = part + float(k) * value
        return value

    for x in range(-3, 4):
        q = [
            horner(x, [k0, lin[0], names[(0, 0)], names[(0, 0, 0)]]),
            horner(x, [lin[1], names[(0, 1)], names[(0, 0, 1)]]),
            horner(x, [names[(1, 1)], names[(0, 1, 1)]]),
            names[(1, 1, 1)],
        ]
        r = [
            horner(x, [lin[2], names[(0, 2)], names[(0, 0, 2)]]),
            horner(x, [names[(1, 2)], names[(0, 1, 2)]]),
            names[(1, 1, 2)],
        ]
        s = [horner(x, [names[(2, 2)], names[(0, 2, 2)]]), names[(1, 2, 2)]]
        for y in range(-3, 4):
            if (x, y) not in GROUPS:
                continue
            place = dict(GROUPS[(x, y)])
            p0, p1, p2 = horner(y, q), horner(y, r), horner(y, s)
            f_ref[half_rows(place[0], half), :] = p0
            for k in (1, 2, 3):
                if k in place:
                    even = p0 + scaled(k * k, p2)
                    odd = scaled(k, p1) + cubes[k]
                    f_ref[half_rows(place[k], half), :] = even + odd
                    f_ref[half_rows(place[-k], half), :] = even - odd


def collide(f_ref, d_ref, half, solid, beta, own_ref, weighted):
    w = [float(v) for v in WEIGHTS]

    def load(ref, i):
        return ref[half_rows(i, half), :]

    rho_s, flux_s = Sums(), [Sums(2) for _ in range(3)]
    rho_s.add(w[INDEX[(0, 0, 0)]] * load(f_ref, INDEX[(0, 0, 0)]))
    for i, v in enumerate(VECTORS):
        opposite = INDEX[tuple(-c for c in v)]
        if i >= opposite:
            continue
        plus, minus = load(f_ref, opposite), load(f_ref, i)
        rho_s.add(w[i] * (plus + minus))
        odd = w[i] * (plus - minus)
        for d in range(3):
            k = -v[d]
            if k:
                flux_s[d].add(odd if k == 1 else odd * float(k))
    rho = rho_s.total()
    inverse = 1.0 / rho
    powers, gauss = [], []
    for d in range(3):
        rate = flux_s[d].total() * inverse * (1.0 / THETA)
        up, down = jnp.exp(rate), jnp.exp(-rate)
        one = {0: None, 1: up, -1: down, 2: up * up, -2: down * down}
        one[3], one[-3] = one[2] * up, one[-2] * down
        powers.append(one)
        gauss.append({k: float(np.exp(-0.5 * k * k)) for k in range(-3, 4)})

    def pair_sum(d, k):
        return (powers[d][k] + powers[d][-k]) * gauss[d][k]

    zs = [pair_sum(2, k) for k in (1, 2, 3)]
    upto = {
        (0,): 1.0,
        (0, 1): 1.0 + zs[0],
        (0, 1, 2): 1.0 + zs[0] + zs[1],
        (0, 2): 1.0 + zs[1],
        (0, 1, 2, 3): 1.0 + zs[0] + zs[1] + zs[2],
    }
    xs = [1.0] + [pair_sum(0, k) for k in (1, 2, 3)]
    ys = [1.0] + [pair_sum(1, k) for k in (1, 2, 3)]
    rows = []
    for x in range(4):
        line = []
        for y in range(4):
            if (x, y) not in GROUPS:
                continue
            key = tuple(sorted(z for z, _ in GROUPS[(x, y)] if z >= 0))
            line.append(ys[y] * upto[key])
        rows.append(xs[x] * functools.reduce(lambda p, q: p + q, line))
    norm = functools.reduce(lambda p, q: p + q, rows)
    factor = rho * float(TOTAL) / norm

    least = None
    curves = {n: Sums(2) for n in SHELLS}
    starts = {n: Sums(2) for n in SHELLS}
    for x in range(-3, 4):
        base = factor if x == 0 else factor * powers[0][x]
        for y in range(-3, 4):
            if (x, y) not in GROUPS:
                continue
            plane = base if y == 0 else base * powers[1][y]
            for z, i in GROUPS[(x, y)]:
                f = load(f_ref, i)
                equil = plane if z == 0 else plane * powers[2][z]
                delta = equil - f
                d_ref[half_rows(i, half), :] = delta
                floored = jnp.maximum(f, FLOOR)
                ratio = delta / floored
                least = ratio if least is None else jnp.minimum(least, ratio)
                shell = x * x + y * y + z * z
                curves[shell].add(delta * ratio)
                starts[shell].add(floored * jnp.log(floored))
    ceiling = 0.95 / jnp.maximum(-least, 0.2375)
    of_shell = {n: w[members[0]] for n, members in SHELLS.items()}
    bound = 0.25 * (tree(of_shell[n] * curves[n].total() for n in SHELLS) + 1e-6)
    entropy = tree(of_shell[n] * starts[n].total() for n in SHELLS)

    def newton(turn, alpha):
        value, slope = Sums(), Sums()
        for members in SHELLS.values():
            of_value, of_slope = Sums(), Sums()
            for i in members:
                delta = load(d_ref, i)
                path = jnp.maximum(load(f_ref, i) + alpha * delta, FLOOR)
                logs = jnp.log(path)
                of_value.add(path * logs)
                of_slope.add(delta * logs)
            value.add(w[members[0]] * of_value.total())
            slope.add(w[members[0]] * of_slope.total())
        change = (value.total() - entropy) / jnp.maximum(slope.total(), bound)
        return jnp.minimum(jnp.maximum(alpha - change, 1.0), ceiling)

    alpha = lax.fori_loop(0, 3, newton, jnp.full(rho.shape, 2.0, jnp.float32))
    step = alpha * beta
    for i, v in enumerate(VECTORS):
        post = jnp.where(solid == 1, rho, load(f_ref, i) + step * load(d_ref, i))
        if weighted:
            post = post * w[i]
        if v[2]:
            post = pltpu.roll(post, v[2] % LANES, 1)
        own_ref[half_rows(i, half), :] = post


def route(axis, odd_ref, even_ref, one_ref, two_ref):
    odd = lax.axis_index(axis) % 2 == 1
    a, b = odd_ref[...], even_ref[...]
    one_ref[...] = jnp.where(odd, a, b)
    two_ref[...] = jnp.where(odd, b, a)


def send_x(own_ref, xa_ref, xb_ref, up_ref, down_ref):
    for sign, out_ref in ((1, up_ref), (-1, down_ref)):
        place, _ = FACE_X[sign]
        for i, at in place.items():
            n = abs(VECTORS[i][0]) * WIDTH
            first = i * TILES + (TILES - n if sign > 0 else 0)
            out_ref[at * WIDTH : at * WIDTH + n, :] = own_ref[first : first + n, :]
    route("gx", up_ref, down_ref, xa_ref, xb_ref)


def rebuild_kernel(
    reply_ref, pick_ref, solid_ref, own_ref, xa_ref, xb_ref, col_ref, f_ref, d_ref, up_ref, down_ref
):
    level = lax.axis_index("level")
    scale = jnp.where(level == 1, SCALE_FINE, SCALE_COARSE)
    beta = jnp.where(level == 1, BETA_FINE, BETA_COARSE)
    width = reply_ref.shape[0] // MOMENTS
    pick = pick_ref[:, :width]
    step = 4
    for first in range(0, MOMENTS, step):
        block = jnp.concatenate(
            [
                reply_ref[pl.ds(n, width, stride=MOMENTS), :]
                for n in range(first, first + step)
            ],
            axis=1,
        )
        chosen = jnp.dot(
            pick, block, precision=lax.Precision.HIGHEST, preferred_element_type=jnp.float32
        )
        for k in range(step):
            n = first + k
            col_ref[n * TILES : (n + 1) * TILES, :] = chosen[:, k * LANES : (k + 1) * LANES]

    def one(half, carry):
        rebuild(col_ref, half, scale, f_ref)
        solid = solid_ref[pl.ds(pl.multiple_of(half * 8, 8), 8), :]
        collide(f_ref, d_ref, half, solid, beta, own_ref, False)
        return carry

    lax.fori_loop(0, 2, one, 0)
    send_x(own_ref, xa_ref, xb_ref, up_ref, down_ref)


def shift_x(own_ref, xa_ref, xb_ref, x_ref, ya_ref, yb_ref, low_ref, high_ref, up_ref, down_ref):
    route("gx", xb_ref, xa_ref, low_ref, high_ref)
    for i, v in enumerate(VECTORS):
        n = abs(v[0]) * WIDTH
        base = i * TILES
        if n == 0:
            x_ref[base : base + TILES, :] = own_ref[base : base + TILES, :]
        elif v[0] > 0:
            at = FACE_X[1][0][i] * WIDTH
            x_ref[base + n : base + TILES, :] = own_ref[base : base + TILES - n, :]
            x_ref[base : base + n, :] = low_ref[at : at + n, :]
        else:
            at = FACE_X[-1][0][i] * WIDTH
            x_ref[base : base + TILES - n, :] = own_ref[base + n : base + TILES, :]
            x_ref[base + TILES - n : base + TILES, :] = high_ref[at : at + n, :]
    for sign, out_ref in ((1, up_ref), (-1, down_ref)):
        place, _ = FACE_Y[sign]
        for i, at in place.items():
            n = abs(VECTORS[i][1])
            for k in range(n):
                row = WIDTH - n + k if sign > 0 else k
                out_ref[(at + k) * WIDTH : (at + k + 1) * WIDTH, :] = x_ref[
                    pl.ds(i * TILES + row, WIDTH, stride=WIDTH), :
                ]
    route("gy", up_ref, down_ref, ya_ref, yb_ref)


def shift_x_near(own_ref, xa_ref, xb_ref, x_ref, yb_ref, ya_ref, *scratch):
    shift_x(own_ref, xa_ref, xb_ref, x_ref, ya_ref, yb_ref, *scratch)


def assemble(x_ref, low_ref, high_ref, out_ref, first=0, last=Q):
    for i in range(first, last):
        v = VECTORS[i]
        base = i * TILES
        out_ref[base : base + TILES, :] = x_ref[base - v[1] : base - v[1] + TILES, :]
        n = abs(v[1])
        for k in range(n):
            if v[1] > 0:
                src_ref, at, row = low_ref, FACE_Y[1][0][i] + k, k
            else:
                src_ref, at, row = high_ref, FACE_Y[-1][0][i] + k, WIDTH - n + k
            out_ref[pl.ds(base + row, WIDTH, stride=WIDTH), :] = src_ref[
                at * WIDTH : (at + 1) * WIDTH, :
            ]


def second_kernel(
    x_ref, ya_ref, yb_ref, solid_ref, own_ref, xa_ref, xb_ref, f_ref, d_ref, low_ref, high_ref
):
    route("gy", yb_ref, ya_ref, low_ref, high_ref)
    assemble(x_ref, low_ref, high_ref, f_ref)

    def one(half, carry):
        solid = solid_ref[pl.ds(pl.multiple_of(half * 8, 8), 8), :]
        collide(f_ref, d_ref, half, solid, BETA_FINE, own_ref, True)
        return carry

    lax.fori_loop(0, 2, one, 0)
    send_x(own_ref, xa_ref, xb_ref, low_ref, high_ref)


PIECES = [(Q * k // 4, Q * (k + 1) // 4) for k in range(4)]


def last_kernel(weighted, x_ref, ya_ref, yb_ref, out_ref, new_ref, low_ref, high_ref, sems):
    def piece(k):
        first, last = PIECES[k]
        rows = pl.ds(first * TILES, (last - first) * TILES)
        return pltpu.make_async_copy(new_ref.at[rows, :], out_ref.at[rows, :], sems.at[k])

    route("gy", yb_ref, ya_ref, low_ref, high_ref)
    for k, (first, last) in enumerate(PIECES):
        assemble(x_ref, low_ref, high_ref, new_ref, first, last)
        if not weighted:
            for i in range(first, last):
                rows = slice(i * TILES, (i + 1) * TILES)
                new_ref[rows, :] = new_ref[rows, :] * float(WEIGHTS[i])
        piece(k).start()
    for k in range(len(PIECES)):
        piece(k).wait()


def call(kernel, outs, args, name, scratch=(), flops=4_000_000, far_args=0, far_outs=False, more=()):
    whole = pl.BlockSpec(memory_space=pltpu.VMEM)
    far = pl.BlockSpec(memory_space=pltpu.HBM)
    kind = pltpu.HBM if far_outs else jax.ShapeDtypeStruct
    shapes = [kind((rows, LANES), jnp.float32) for rows in outs]
    moved = sum(int(rows) * LANES for rows in outs) + sum(int(np.prod(a.shape)) for a in args)
    return pl.pallas_call(
        kernel,
        out_shape=shapes,
        in_specs=[far] * far_args + [whole] * (len(args) - far_args),
        out_specs=[far if far_outs else whole] * len(shapes),
        scratch_shapes=[pltpu.VMEM((rows, LANES), jnp.float32) for rows in scratch] + list(more),
        compiler_params=pltpu.CompilerParams(vmem_limit_bytes=24 << 20),
        cost_estimate=pl.CostEstimate(flops=flops, bytes_accessed=4 * moved, transcendentals=0),
        name=name,
    )(*args)


def swap_edges(first, second, axis, near_first=False):
    count = lax.axis_size(axis)
    odd = [(i, (i + 1) % count if i % 2 else (i - 1) % count) for i in range(count)]
    even = [(i, i ^ 1) for i in range(count)]
    if near_first:
        near = lax.ppermute(second, axis, even)
        return lax.ppermute(first, axis, odd), near
    return lax.ppermute(first, axis, odd), lax.ppermute(second, axis, even)


def shards(populations, solid_mask, recv_tiles, owner_gy, owner_tiles):
    peers = lax.axis_size("gy")
    count = owner_tiles.shape[-1]
    pops = populations.reshape(ROWS, LANES)
    solid = solid_mask.reshape(TILES, LANES)
    owners = owner_gy.reshape(1, count)
    wanted = owner_tiles.reshape(1, count)
    targets = recv_tiles.reshape(1, count)
    slots = peers * CAP
    tables = [owners, wanted, targets]
    mom, ask, pick = call(
        moments_kernel,
        [MOMENTS * TILES, slots, TILES],
        [pltpu.with_memory_space_constraint(a, pltpu.HBM) for a in [pops] + tables],
        "moments",
        [ROWS],
        far_args=4,
        more=[pltpu.VMEM((1, count), jnp.int32)] * 3 + [pltpu.SemaphoreType.DMA((10,))],
    )
    across = [
        (level * peers + g, (1 - level) * peers + (g ^ MIRROR))
        for level in range(lax.axis_size("level"))
        for g in range(peers)
    ]
    crossed = lax.ppermute(mom, ("level", "gy"), across)
    asked = lax.all_to_all(
        ask.reshape(peers, CAP, LANES), "gy", split_axis=0, concat_axis=0, tiled=True
    ).reshape(slots, LANES)
    (answer,) = call(pack_kernel, [slots * MOMENTS], [crossed, asked], "pack")
    reply = lax.all_to_all(
        answer.reshape(peers, CAP * MOMENTS, LANES), "gy", split_axis=0, concat_axis=0, tiled=True
    ).reshape(slots * MOMENTS, LANES)
    faces = [ROWS, FACE_ROWS, FACE_ROWS]
    own, xa, xb = call(
        rebuild_kernel,
        faces,
        [reply, pick, solid],
        "collide1",
        [MOMENTS * TILES, ROWS, ROWS] + [FACE_ROWS] * 2,
    )
    first, second = swap_edges(xa, xb, "gx")
    moved, ya, yb = call(
        shift_x,
        faces,
        [own, first, second],
        "shift1",
        [FACE_ROWS] * 4,
    )
    first, second = swap_edges(ya, yb, "gy")
    def last(weighted, moved, first, second):
        (out,) = call(
            functools.partial(last_kernel, weighted),
            [ROWS],
            [moved, first, second],
            "last",
            [ROWS] + [FACE_ROWS] * 2,
            far_outs=True,
            more=[pltpu.SemaphoreType.DMA((len(PIECES),))],
        )
        return out

    def fine_end(moved, first, second, solid):
        own, xa, xb = call(
            second_kernel,
            faces,
            [moved, first, second, solid],
            "collide2",
            [ROWS, ROWS] + [FACE_ROWS] * 2,
        )
        first, second = swap_edges(xa, xb, "gx")
        moved, yb, ya = call(shift_x_near, faces, [own, first, second], "shift2", [FACE_ROWS] * 4)
        first, second = swap_edges(ya, yb, "gy", True)
        return last(True, moved, first, second)

    def coarse_end(moved, first, second, solid):
        return last(False, moved, first, second)

    out = lax.cond(
        lax.axis_index("level") == 1, fine_end, coarse_end, moved, first, second, solid
    )
    return out.reshape(populations.shape)


def solution(mesh):
    placed = (
        P("level", None, "gx", "gy", None),
        P("level", "gx", "gy", None),
        P("level", "gx", "gy", None),
        P("level", "gx", "gy", None, None),
        P("level", "gx", "gy", None),
    )
    return jax.shard_map(
        shards,
        mesh=mesh,
        in_specs=placed,
        out_specs=P("level", None, "gx", "gy", None),
        check_vma=False,
    )
```

```python
import functools
import jax
import jax.numpy as jnp
import numpy as np
from jax import lax
from jax.experimental import pallas as pl
from jax.experimental.pallas import tpu as pltpu
from jax.sharding import PartitionSpec as P


CAP = 2
FLOOR = 0.05
BETA_COARSE = 0.9
BETA_FINE = 0.8
SCALE_FINE = 0.5
SCALE_COARSE = 1.5
WIDTH = 4
TILES = 16
LANES = 128
MIRROR = 3


def lattice():
    shells = [
        (0, 0, 0),
        (0, 0, 1),
        (0, 1, 1),
        (1, 1, 1),
        (0, 0, 2),
        (0, 2, 2),
        (2, 2, 2),
        (0, 0, 3),
        (0, 1, 2),
        (1, 1, 2),
    ]
    vectors = []
    for first in range(-3, 4):
        for second in range(-3, 4):
            for third in range(-3, 4):
                if tuple(sorted((abs(first), abs(second), abs(third)))) in shells:
                    vectors.append((first, second, third))
    offsets = np.array(vectors)
    speeds = offsets * 1.0
    raw = np.exp(-0.5 * np.sum(speeds * speeds, axis=1))
    total = np.sum(raw)
    weights = raw / total
    theta = float(np.sum(weights * speeds[:, 0] * speeds[:, 0]))
    return vectors, speeds, weights, theta, float(total)


VECTORS, SPEEDS, WEIGHTS, THETA, TOTAL = lattice()
Q = len(VECTORS)
ROWS = Q * TILES
INDEX = {v: i for i, v in enumerate(VECTORS)}
PAIRS = [(a, b) for a in range(3) for b in range(a, 3)]
TRIPLES = [(a, b, c) for a in range(3) for b in range(a, 3) for c in range(b, 3)]
MOMENTS = 1 + 3 + len(PAIRS) + len(TRIPLES)
GROUPS = {}
for _i, (_x, _y, _z) in enumerate(VECTORS):
    GROUPS.setdefault((_x, _y), []).append((_z, _i))


def norms():
    rows = [np.ones(Q)]
    for a in range(3):
        rows.append(SPEEDS[:, a])
    for a, b in PAIRS:
        rows.append(SPEEDS[:, a] * SPEEDS[:, b] - THETA * float(a == b))
    for a, b, c in TRIPLES:
        rows.append(
            SPEEDS[:, a] * SPEEDS[:, b] * SPEEDS[:, c]
            - THETA
            * (
                SPEEDS[:, a] * float(b == c)
                + SPEEDS[:, b] * float(a == c)
                + SPEEDS[:, c] * float(a == b)
            )
        )
    basis = np.stack(rows)
    return (basis * basis) @ WEIGHTS


NORMS = norms()


def face_layout(axis):
    sides = {}
    for sign in (1, -1):
        order = [i for n in (2, 1, 3) for i in range(Q) if VECTORS[i][axis] == sign * n]
        place, at = {}, 0
        for i in order:
            place[i] = at
            at += abs(VECTORS[i][axis])
        sides[sign] = (place, at)
    return sides


FACE_X = face_layout(0)
FACE_Y = face_layout(1)
FACE_ROWS = FACE_X[1][1] * WIDTH


SHELLS = {}
for _i, _v in enumerate(VECTORS):
    SHELLS.setdefault(sum(c * c for c in _v), []).append(_i)


def scaled(k, value):
    return value if k == 1 else value * float(k)


def combine(terms):
    total = None
    for k, value in terms:
        if k == 0:
            continue
        if total is None:
            total = scaled(k, value)
        elif k > 0:
            total = total + scaled(k, value)
        else:
            total = total - scaled(-k, value)
    return total


def tree(values):
    values = list(values)
    while len(values) > 1:
        values = [
            values[i] + values[i + 1] if i + 1 < len(values) else values[i]
            for i in range(0, len(values), 2)
        ]
    return values[0]


class Sums:
    def __init__(self, parts=4):
        self.parts = [None] * parts
        self.turn = 0

    def add(self, value):
        k = self.turn % len(self.parts)
        self.turn += 1
        self.parts[k] = value if self.parts[k] is None else self.parts[k] + value

    def total(self):
        return tree([p for p in self.parts if p is not None])


def half_rows(i, half):
    return pl.ds(pl.multiple_of(half * 8 + i * TILES, 8), 8)


def request_tables(owner_ref, wanted_ref, target_ref, ask_ref, pick_ref):
    own = owner_ref[...] ^ MIRROR
    count = own.shape[1]
    sub = lax.broadcasted_iota(jnp.int32, (count, count), 0)
    lane = lax.broadcasted_iota(jnp.int32, (count, count), 1)

    def down(row):
        return jnp.sum(
            jnp.where(sub == lane, jnp.broadcast_to(row, (count, count)), 0), axis=1, keepdims=True
        )

    same = jnp.where(
        jnp.logical_and(jnp.broadcast_to(own, (count, count)) == down(own), sub < lane), 1, 0
    )
    slot = own * CAP + jnp.sum(same, axis=0, keepdims=True)
    width = ask_ref.shape[0]
    by_slot = jnp.where(
        lax.broadcasted_iota(jnp.int32, (width, count), 0) == jnp.broadcast_to(slot, (width, count)),
        1.0,
        0.0,
    )
    wide = lax.broadcasted_iota(jnp.int32, (count, LANES), 1)
    tiles = jnp.where(wide == down(wanted_ref[...]), 1.0, 0.0)
    ask_ref[...] = jnp.dot(by_slot, tiles, preferred_element_type=jnp.float32)
    by_target = jnp.where(sub == jnp.broadcast_to(target_ref[...], (count, count)), 1.0, 0.0)
    slots = jnp.where(wide == down(slot), 1.0, 0.0)
    pick_ref[...] = jnp.dot(by_target, slots, preferred_element_type=jnp.float32)


def moments_kernel(
    pops_hbm,
    owner_hbm,
    wanted_hbm,
    target_hbm,
    mom_ref,
    ask_ref,
    pick_ref,
    pops_ref,
    owner_ref,
    wanted_ref,
    target_ref,
    sems,
):
    pairs = [
        (owner_hbm, owner_ref),
        (wanted_hbm, wanted_ref),
        (target_hbm, target_ref),
        (pops_hbm, pops_ref),
    ]
    copies = [pltpu.make_async_copy(a, b, sems.at[k]) for k, (a, b) in enumerate(pairs)]
    for copy in copies:
        copy.start()
    for copy in copies[:3]:
        copy.wait()
    request_tables(owner_ref, wanted_ref, target_ref, ask_ref, pick_ref)
    copies[3].wait()

    def one(half, carry):
        raw = {}

        def put(key, k, value):
            if k == 0:
                return
            old = raw.get(key)
            term = scaled(abs(k), value)
            if old is None:
                raw[key] = term if k > 0 else -term
            else:
                raw[key] = old + term if k > 0 else old - term

        for x in range(-3, 4):
            inner = {}
            for y in range(-3, 4):
                if (x, y) not in GROUPS:
                    continue
                f = {z: pops_ref[half_rows(i, half), :] for z, i in GROUPS[(x, y)]}
                even = {k: f[k] + f[-k] for k in (1, 2, 3) if k in f}
                odd = {k: f[k] - f[-k] for k in (1, 2, 3) if k in f}
                sums = [
                    combine([(1, f[0])] + [(1, v) for v in even.values()]),
                    combine([(k, v) for k, v in odd.items()]),
                    combine([(k * k, v) for k, v in even.items()]),
                    combine([(k * k * k, v) for k, v in odd.items()]),
                ]
                for c in range(4):
                    if sums[c] is None:
                        continue
                    for b in range(4 - c):
                        k = y**b
                        if k:
                            inner.setdefault((b, c), []).append((k, sums[c]))
            for (b, c), terms in inner.items():
                terms.sort(key=lambda t: -t[0])
                value = combine(terms) if terms[0][0] > 0 else -combine([(-k, v) for k, v in terms])
                for a in range(4 - b - c):
                    put((a, b, c), x**a, value)
        out = [raw[(0, 0, 0)], raw[(1, 0, 0)], raw[(0, 1, 0)], raw[(0, 0, 1)]]

        def power(*axes):
            return tuple(sum(1 for a in axes if a == d) for d in range(3))

        for a, b in PAIRS:
            value = raw[power(a, b)]
            out.append(value - THETA * out[0] if a == b else value)
        for a, b, c in TRIPLES:
            value = raw[power(a, b, c)]
            if a == b == c:
                value = value - (3.0 * THETA) * out[1 + a]
            elif a == b:
                value = value - THETA * out[1 + c]
            elif b == c:
                value = value - THETA * out[1 + a]
            out.append(value)
        for n in range(MOMENTS):
            mom_ref[half_rows(n, half), :] = out[n]
        return carry

    lax.fori_loop(0, 2, one, 0)


def pack_kernel(mom_ref, ask_ref, reply_ref):
    ask = ask_ref[:, :TILES]
    width = ask_ref.shape[0]
    step = 4
    for first in range(0, MOMENTS, step):
        block = jnp.concatenate(
            [mom_ref[n * TILES : (n + 1) * TILES, :] for n in range(first, first + step)], axis=1
        )
        chosen = jnp.dot(
            ask, block, precision=lax.Precision.HIGHEST, preferred_element_type=jnp.float32
        )
        for k in range(step):
            reply_ref[pl.ds(first + k, width, stride=MOMENTS), :] = chosen[
                :, k * LANES : (k + 1) * LANES
            ]


def rebuild(col_ref, half, scale, f_ref):
    a = [col_ref[half_rows(n, half), :] for n in range(MOMENTS)]
    rho = a[0]
    inverse = 1.0 / rho
    flux = a[1:4]
    speed = [v * inverse for v in flux]
    b = [a[n] * (1.0 / NORMS[n]) for n in range(4)]
    n = 4
    names = {}
    for first, second in PAIRS:
        eq = flux[first] * speed[second]
        names[(first, second)] = (eq + scale * (a[n] - eq)) * (1.0 / NORMS[n])
        n += 1
    for first, second, third in TRIPLES:
        eq = flux[first] * speed[second] * speed[third]
        names[(first, second, third)] = (eq + scale * (a[n] - eq)) * (1.0 / NORMS[n])
        n += 1
    k0 = b[0] - THETA * (names[(0, 0)] + names[(1, 1)] + names[(2, 2)])
    lin = []
    for d in range(3):
        others = [names[tuple(sorted((d, e, e)))] for e in range(3) if e != d]
        lin.append(b[1 + d] - THETA * (3.0 * names[(d, d, d)] + (others[0] + others[1])))
    cubes = {k: names[(2, 2, 2)] * float(k**3) for k in (1, 2, 3)}

    def horner(k, parts):
        value = parts[-1]
        for part in parts[-2::-1]:
            if k == 0:
                value = part
            elif k == 1:
                value = part + value
            elif k == -1:
                value = part - value
            else:
                value = part + float(k) * value
        return value

    for x in range(-3, 4):
        q = [
            horner(x, [k0, lin[0], names[(0, 0)], names[(0, 0, 0)]]),
            horner(x, [lin[1], names[(0, 1)], names[(0, 0, 1)]]),
            horner(x, [names[(1, 1)], names[(0, 1, 1)]]),
            names[(1, 1, 1)],
        ]
        r = [
            horner(x, [lin[2], names[(0, 2)], names[(0, 0, 2)]]),
            horner(x, [names[(1, 2)], names[(0, 1, 2)]]),
            names[(1, 1, 2)],
        ]
        s = [horner(x, [names[(2, 2)], names[(0, 2, 2)]]), names[(1, 2, 2)]]
        for y in range(-3, 4):
            if (x, y) not in GROUPS:
                continue
            place = dict(GROUPS[(x, y)])
            p0, p1, p2 = horner(y, q), horner(y, r), horner(y, s)
            f_ref[half_rows(place[0], half), :] = p0
            for k in (1, 2, 3):
                if k in place:
                    even = p0 + scaled(k * k, p2)
                    odd = scaled(k, p1) + cubes[k]
                    f_ref[half_rows(place[k], half), :] = even + odd
                    f_ref[half_rows(place[-k], half), :] = even - odd


def collide(f_ref, d_ref, half, solid, beta, own_ref, weighted):
    w = [float(v) for v in WEIGHTS]

    def load(ref, i):
        return ref[half_rows(i, half), :]

    rho_s, flux_s = Sums(), [Sums(2) for _ in range(3)]
    rho_s.add(w[INDEX[(0, 0, 0)]] * load(f_ref, INDEX[(0, 0, 0)]))
    for i, v in enumerate(VECTORS):
        opposite = INDEX[tuple(-c for c in v)]
        if i >= opposite:
            continue
        plus, minus = load(f_ref, opposite), load(f_ref, i)
        rho_s.add(w[i] * (plus + minus))
        odd = w[i] * (plus - minus)
        for d in range(3):
            k = -v[d]
            if k:
                flux_s[d].add(odd if k == 1 else odd * float(k))
    rho = rho_s.total()
    inverse = 1.0 / rho
    powers, gauss = [], []
    for d in range(3):
        rate = flux_s[d].total() * inverse * (1.0 / THETA)
        up, down = jnp.exp(rate), jnp.exp(-rate)
        one = {0: None, 1: up, -1: down, 2: up * up, -2: down * down}
        one[3], one[-3] = one[2] * up, one[-2] * down
        powers.append(one)
        gauss.append({k: float(np.exp(-0.5 * k * k)) for k in range(-3, 4)})

    def pair_sum(d, k):
        return (powers[d][k] + powers[d][-k]) * gauss[d][k]

    zs = [pair_sum(2, k) for k in (1, 2, 3)]
    upto = {
        (0,): 1.0,
        (0, 1): 1.0 + zs[0],
        (0, 1, 2): 1.0 + zs[0] + zs[1],
        (0, 2): 1.0 + zs[1],
        (0, 1, 2, 3): 1.0 + zs[0] + zs[1] + zs[2],
    }
    xs = [1.0] + [pair_sum(0, k) for k in (1, 2, 3)]
    ys = [1.0] + [pair_sum(1, k) for k in (1, 2, 3)]
    rows = []
    for x in range(4):
        line = []
        for y in range(4):
            if (x, y) not in GROUPS:
                continue
            key = tuple(sorted(z for z, _ in GROUPS[(x, y)] if z >= 0))
            line.append(ys[y] * upto[key])
        rows.append(xs[x] * functools.reduce(lambda p, q: p + q, line))
    norm = functools.reduce(lambda p, q: p + q, rows)
    factor = rho * float(TOTAL) / norm

    least = None
    curves = {n: Sums(2) for n in SHELLS}
    starts = {n: Sums(2) for n in SHELLS}
    for x in range(-3, 4):
        base = factor if x == 0 else factor * powers[0][x]
        for y in range(-3, 4):
            if (x, y) not in GROUPS:
                continue
            plane = base if y == 0 else base * powers[1][y]
            for z, i in GROUPS[(x, y)]:
                f = load(f_ref, i)
                equil = plane if z == 0 else plane * powers[2][z]
                delta = equil - f
                d_ref[half_rows(i, half), :] = delta
                floored = jnp.maximum(f, FLOOR)
                ratio = delta / floored
                least = ratio if least is None else jnp.minimum(least, ratio)
                shell = x * x + y * y + z * z
                curves[shell].add(delta * ratio)
                starts[shell].add(floored * jnp.log(floored))
    ceiling = 0.95 / jnp.maximum(-least, 0.2375)
    of_shell = {n: w[members[0]] for n, members in SHELLS.items()}
    bound = 0.25 * (tree(of_shell[n] * curves[n].total() for n in SHELLS) + 1e-6)
    entropy = tree(of_shell[n] * starts[n].total() for n in SHELLS)

    def newton(turn, alpha):
        value, slope = Sums(), Sums()
        for members in SHELLS.values():
            of_value, of_slope = Sums(), Sums()
            for i in members:
                delta = load(d_ref, i)
                path = jnp.maximum(load(f_ref, i) + alpha * delta, FLOOR)
                logs = jnp.log(path)
                of_value.add(path * logs)
                of_slope.add(delta * logs)
            value.add(w[members[0]] * of_value.total())
            slope.add(w[members[0]] * of_slope.total())
        change = (value.total() - entropy) / jnp.maximum(slope.total(), bound)
        return jnp.minimum(jnp.maximum(alpha - change, 1.0), ceiling)

    alpha = lax.fori_loop(0, 3, newton, jnp.full(rho.shape, 2.0, jnp.float32))
    step = alpha * beta
    for i, v in enumerate(VECTORS):
        post = jnp.where(solid == 1, rho, load(f_ref, i) + step * load(d_ref, i))
        if weighted:
            post = post * w[i]
        if v[2]:
            post = pltpu.roll(post, v[2] % LANES, 1)
        own_ref[half_rows(i, half), :] = post


def route(axis, odd_ref, even_ref, one_ref, two_ref):
    odd = lax.axis_index(axis) % 2 == 1
    a, b = odd_ref[...], even_ref[...]
    one_ref[...] = jnp.where(odd, a, b)
    two_ref[...] = jnp.where(odd, b, a)


LATE_ROWS = 8


def face_rows(sign, own_ref, out_ref, first_half_only):
    place, _ = FACE_X[sign]
    for i, at in place.items():
        n = abs(VECTORS[i][0]) * WIDTH
        skip = n - 8 if first_half_only and n > 8 else 0
        base = i * TILES
        if sign > 0:
            out_ref[at * WIDTH + skip : at * WIDTH + n, :] = own_ref[
                base + TILES - n + skip : base + TILES, :
            ]
        else:
            out_ref[at * WIDTH : at * WIDTH + n - skip, :] = own_ref[base : base + n - skip, :]


def send_early(own_ref, xa_ref):
    odd = lax.axis_index("gx") % 2 == 1

    @pl.when(odd)
    def _():
        face_rows(1, own_ref, xa_ref, True)

    @pl.when(jnp.logical_not(odd))
    def _():
        face_rows(-1, own_ref, xa_ref, True)


def send_late(own_ref, xb_ref, late_ref):
    odd = lax.axis_index("gx") % 2 == 1
    late_ref[...] = jnp.zeros_like(late_ref)

    @pl.when(odd)
    def _():
        face_rows(-1, own_ref, xb_ref, False)
        at = INDEX[(3, 0, 0)] * TILES + WIDTH
        late_ref[0:WIDTH, :] = own_ref[at : at + WIDTH, :]

    @pl.when(jnp.logical_not(odd))
    def _():
        face_rows(1, own_ref, xb_ref, False)
        at = INDEX[(-3, 0, 0)] * TILES + 2 * WIDTH
        late_ref[0:WIDTH, :] = own_ref[at : at + WIDTH, :]


def put_late(late_ref, new_ref, on_odd):
    odd = lax.axis_index("gx") % 2 == 1

    @pl.when(odd if on_odd else jnp.logical_not(odd))
    def _():
        at = INDEX[(-3, 0, 0)] * TILES + TILES - WIDTH if on_odd else INDEX[(3, 0, 0)] * TILES
        new_ref[at : at + WIDTH, :] = late_ref[0:WIDTH, :]


def early_half():
    return lax.axis_index("gx") % 2


def solid_half(solid_ref, half):
    return solid_ref[pl.ds(pl.multiple_of(half * 8, 8), 8), :]


def level_constants():
    level = lax.axis_index("level")
    scale = jnp.where(level == 1, SCALE_FINE, SCALE_COARSE)
    return scale, jnp.where(level == 1, BETA_FINE, BETA_COARSE)


def rebuild_early(reply_ref, pick_ref, solid_ref, own_ref, xa_ref, col_ref, f_ref, d_ref):
    scale, beta = level_constants()
    width = reply_ref.shape[0] // MOMENTS
    pick = pick_ref[:, :width]
    step = 4
    for first in range(0, MOMENTS, step):
        block = jnp.concatenate(
            [
                reply_ref[pl.ds(n, width, stride=MOMENTS), :]
                for n in range(first, first + step)
            ],
            axis=1,
        )
        chosen = jnp.dot(
            pick, block, precision=lax.Precision.HIGHEST, preferred_element_type=jnp.float32
        )
        for k in range(step):
            n = first + k
            col_ref[n * TILES : (n + 1) * TILES, :] = chosen[:, k * LANES : (k + 1) * LANES]

    half = early_half()
    rebuild(col_ref, half, scale, f_ref)
    collide(f_ref, d_ref, half, solid_half(solid_ref, half), beta, own_ref, False)
    send_early(own_ref, xa_ref)


def rebuild_late(first_ref, col_ref, solid_ref, own_ref, xb_ref, late_ref, f_ref, d_ref):
    scale, beta = level_constants()
    half = 1 - early_half()
    rebuild(col_ref, half, scale, f_ref)
    collide(f_ref, d_ref, half, solid_half(solid_ref, half), beta, own_ref, False)
    send_late(own_ref, xb_ref, late_ref)


def shift_x(own_ref, xa_ref, xb_ref, x_ref, ya_ref, yb_ref, low_ref, high_ref, up_ref, down_ref):
    route("gx", xb_ref, xa_ref, low_ref, high_ref)
    for i, v in enumerate(VECTORS):
        n = abs(v[0]) * WIDTH
        base = i * TILES
        if n == 0:
            x_ref[base : base + TILES, :] = own_ref[base : base + TILES, :]
        elif v[0] > 0:
            at = FACE_X[1][0][i] * WIDTH
            x_ref[base + n : base + TILES, :] = own_ref[base : base + TILES - n, :]
            x_ref[base : base + n, :] = low_ref[at : at + n, :]
        else:
            at = FACE_X[-1][0][i] * WIDTH
            x_ref[base : base + TILES - n, :] = own_ref[base + n : base + TILES, :]
            x_ref[base + TILES - n : base + TILES, :] = high_ref[at : at + n, :]
    for sign, out_ref in ((1, up_ref), (-1, down_ref)):
        place, _ = FACE_Y[sign]
        for i, at in place.items():
            n = abs(VECTORS[i][1])
            for k in range(n):
                row = WIDTH - n + k if sign > 0 else k
                out_ref[(at + k) * WIDTH : (at + k + 1) * WIDTH, :] = x_ref[
                    pl.ds(i * TILES + row, WIDTH, stride=WIDTH), :
                ]
    route("gy", up_ref, down_ref, ya_ref, yb_ref)


def assemble(x_ref, low_ref, high_ref, out_ref, first=0, last=Q):
    for i in range(first, last):
        v = VECTORS[i]
        base = i * TILES
        out_ref[base : base + TILES, :] = x_ref[base - v[1] : base - v[1] + TILES, :]
        n = abs(v[1])
        for k in range(n):
            if v[1] > 0:
                src_ref, at, row = low_ref, FACE_Y[1][0][i] + k, k
            else:
                src_ref, at, row = high_ref, FACE_Y[-1][0][i] + k, WIDTH - n + k
            out_ref[pl.ds(base + row, WIDTH, stride=WIDTH), :] = src_ref[
                at * WIDTH : (at + 1) * WIDTH, :
            ]


def second_early(
    x_ref, ya_ref, yb_ref, late_ref, solid_ref, own_ref, xa_ref, f_ref, d_ref, low_ref, high_ref
):
    route("gy", yb_ref, ya_ref, low_ref, high_ref)
    assemble(x_ref, low_ref, high_ref, f_ref)
    put_late(late_ref, f_ref, True)
    put_late(late_ref, f_ref, False)
    half = early_half()
    collide(f_ref, d_ref, half, solid_half(solid_ref, half), BETA_FINE, own_ref, True)
    send_early(own_ref, xa_ref)


def second_late(first_ref, f_ref, solid_ref, own_ref, xb_ref, late_ref, d_ref):
    half = 1 - early_half()
    collide(f_ref, d_ref, half, solid_half(solid_ref, half), BETA_FINE, own_ref, True)
    send_late(own_ref, xb_ref, late_ref)


PIECES = [(Q * k // 4, Q * (k + 1) // 4) for k in range(4)]


def last_kernel(weighted, x_ref, ya_ref, yb_ref, late_ref, out_ref, new_ref, low_ref, high_ref, sems):
    def piece(k):
        first, last = PIECES[k]
        rows = pl.ds(first * TILES, (last - first) * TILES)
        return pltpu.make_async_copy(new_ref.at[rows, :], out_ref.at[rows, :], sems.at[k])

    route("gy", yb_ref, ya_ref, low_ref, high_ref)
    for k, (first, last) in enumerate(PIECES):
        assemble(x_ref, low_ref, high_ref, new_ref, first, last)
        if first == 0 or last == Q:
            put_late(late_ref, new_ref, first == 0)
        if not weighted:
            for i in range(first, last):
                rows = slice(i * TILES, (i + 1) * TILES)
                new_ref[rows, :] = new_ref[rows, :] * float(WEIGHTS[i])
        piece(k).start()
    for k in range(len(PIECES)):
        piece(k).wait()


def call(kernel, outs, args, scratch=(), flops=4_000_000, far_args=0, far_outs=False, more=(), alias=False):
    whole = pl.BlockSpec(memory_space=pltpu.VMEM)
    far = pl.BlockSpec(memory_space=pltpu.HBM)
    kind = pltpu.HBM if far_outs else jax.ShapeDtypeStruct
    shapes = [kind((rows, LANES), jnp.float32) for rows in outs]
    moved = sum(int(rows) * LANES for rows in outs) + sum(int(np.prod(a.shape)) for a in args)
    return pl.pallas_call(
        kernel,
        out_shape=shapes,
        in_specs=[far] * far_args + [whole] * (len(args) - far_args),
        out_specs=[far if far_outs else whole] * len(shapes),
        input_output_aliases={0: 0} if alias else {},
        scratch_shapes=[pltpu.VMEM((rows, LANES), jnp.float32) for rows in scratch] + list(more),
        compiler_params=pltpu.CompilerParams(vmem_limit_bytes=24 << 20),
        cost_estimate=pl.CostEstimate(flops=flops, bytes_accessed=4 * moved, transcendentals=0),
    )(*args)


def swap_edges(axis, messages):
    count = lax.axis_size(axis)
    odd = [(i, (i + 1) % count if i % 2 else (i - 1) % count) for i in range(count)]
    even = [(i, i ^ 1) for i in range(count)]
    to = {"odd": odd, "even": even}
    return [lax.ppermute(value, axis, to[edges]) for edges, value in messages]


def step(populations, solid_mask, recv_tiles, owner_gy, owner_tiles):
    peers = lax.axis_size("gy")
    count = owner_tiles.shape[-1]
    pops = populations.reshape(ROWS, LANES)
    solid = solid_mask.reshape(TILES, LANES)
    owners = owner_gy.reshape(1, count)
    wanted = owner_tiles.reshape(1, count)
    targets = recv_tiles.reshape(1, count)
    slots = peers * CAP
    tables = [owners, wanted, targets]
    mom, ask, pick = call(
        moments_kernel,
        [MOMENTS * TILES, slots, TILES],
        [pltpu.with_memory_space_constraint(a, pltpu.HBM) for a in [pops] + tables],
        [ROWS],
        far_args=4,
        more=[pltpu.VMEM((1, count), jnp.int32)] * 3 + [pltpu.SemaphoreType.DMA((4,))],
    )
    across = [
        (level * peers + g, (1 - level) * peers + (g ^ MIRROR))
        for level in range(lax.axis_size("level"))
        for g in range(peers)
    ]
    crossed = lax.ppermute(mom, ("level", "gy"), across)
    asked = lax.all_to_all(
        ask.reshape(peers, CAP, LANES), "gy", split_axis=0, concat_axis=0, tiled=True
    ).reshape(slots, LANES)
    (answer,) = call(pack_kernel, [slots * MOMENTS], [crossed, asked])
    reply = lax.all_to_all(
        answer.reshape(peers, CAP * MOMENTS, LANES), "gy", split_axis=0, concat_axis=0, tiled=True
    ).reshape(slots * MOMENTS, LANES)
    faces = [ROWS, FACE_ROWS, FACE_ROWS]
    early = [ROWS, FACE_ROWS]
    late_outs = [ROWS, FACE_ROWS, LATE_ROWS]

    def along_x(xa, finish):
        (first,) = swap_edges("gx", [("odd", xa)])
        own, xb, late = finish()
        second, late = swap_edges("gx", [("even", xb), ("odd", late)])
        return own, first, second, late

    def along_y(own, first, second):
        moved, ya, yb = call(shift_x, faces, [own, first, second], [FACE_ROWS] * 4)
        first, second = swap_edges("gy", [("odd", ya), ("even", yb)])
        return moved, first, second

    half_own, xa, col = call(
        rebuild_early, early + [MOMENTS * TILES], [reply, pick, solid], [ROWS, ROWS]
    )
    own, first, second, late = along_x(
        xa, lambda: call(rebuild_late, late_outs, [half_own, col, solid], [ROWS, ROWS], alias=True)
    )
    moved, first, second = along_y(own, first, second)

    def last(weighted, moved, first, second, late):
        (out,) = call(
            functools.partial(last_kernel, weighted),
            [ROWS],
            [moved, first, second, late],
            [ROWS] + [FACE_ROWS] * 2,
            far_outs=True,
            more=[pltpu.SemaphoreType.DMA((len(PIECES),))],
        )
        return out

    def fine_end(moved, first, second, late, solid):
        half_own, xa, f = call(
            second_early,
            early + [ROWS],
            [moved, first, second, late, solid],
            [ROWS] + [FACE_ROWS] * 2,
        )
        own, first, second, late = along_x(
            xa, lambda: call(second_late, late_outs, [half_own, f, solid], [ROWS], alias=True)
        )
        moved, first, second = along_y(own, first, second)
        return last(True, moved, first, second, late)

    def coarse_end(moved, first, second, late, solid):
        return last(False, moved, first, second, late)

    out = lax.cond(
        lax.axis_index("level") == 1, fine_end, coarse_end, moved, first, second, late, solid
    )
    return out.reshape(populations.shape)


def solution(mesh):
    placed = (
        P("level", None, "gx", "gy", None),
        P("level", "gx", "gy", None),
        P("level", "gx", "gy", None),
        P("level", "gx", "gy", None, None),
        P("level", "gx", "gy", None),
    )
    return jax.shard_map(
        step,
        mesh=mesh,
        in_specs=placed,
        out_specs=P("level", None, "gx", "gy", None),
        check_vma=False,
    )
```

```python
import functools
import jax
import jax.numpy as jnp
import numpy as np
from jax import lax
from jax.experimental import pallas as pl
from jax.experimental.pallas import tpu as pltpu
from jax.sharding import PartitionSpec as P


CAP = 2
FLOOR = 0.05
BETA_COARSE = 0.9
BETA_FINE = 0.8
SCALE_FINE = 0.5
SCALE_COARSE = 1.5
WIDTH = 4
TILES = 16
LANES = 128
MIRROR = 3


def lattice():
    shells = [
        (0, 0, 0),
        (0, 0, 1),
        (0, 1, 1),
        (1, 1, 1),
        (0, 0, 2),
        (0, 2, 2),
        (2, 2, 2),
        (0, 0, 3),
        (0, 1, 2),
        (1, 1, 2),
    ]
    vectors = []
    for first in range(-3, 4):
        for second in range(-3, 4):
            for third in range(-3, 4):
                if tuple(sorted((abs(first), abs(second), abs(third)))) in shells:
                    vectors.append((first, second, third))
    offsets = np.array(vectors)
    speeds = offsets * 1.0
    raw = np.exp(-0.5 * np.sum(speeds * speeds, axis=1))
    total = np.sum(raw)
    weights = raw / total
    theta = float(np.sum(weights * speeds[:, 0] * speeds[:, 0]))
    return vectors, speeds, weights, theta, float(total)


VECTORS, SPEEDS, WEIGHTS, THETA, TOTAL = lattice()
Q = len(VECTORS)
ROWS = Q * TILES
INDEX = {v: i for i, v in enumerate(VECTORS)}
PAIRS = [(a, b) for a in range(3) for b in range(a, 3)]
TRIPLES = [(a, b, c) for a in range(3) for b in range(a, 3) for c in range(b, 3)]
MOMENTS = 1 + 3 + len(PAIRS) + len(TRIPLES)
GROUPS = {}
for _i, (_x, _y, _z) in enumerate(VECTORS):
    GROUPS.setdefault((_x, _y), []).append((_z, _i))


def norms():
    rows = [np.ones(Q)]
    for a in range(3):
        rows.append(SPEEDS[:, a])
    for a, b in PAIRS:
        rows.append(SPEEDS[:, a] * SPEEDS[:, b] - THETA * float(a == b))
    for a, b, c in TRIPLES:
        rows.append(
            SPEEDS[:, a] * SPEEDS[:, b] * SPEEDS[:, c]
            - THETA
            * (
                SPEEDS[:, a] * float(b == c)
                + SPEEDS[:, b] * float(a == c)
                + SPEEDS[:, c] * float(a == b)
            )
        )
    basis = np.stack(rows)
    return (basis * basis) @ WEIGHTS


NORMS = norms()


def face_layout(axis):
    sides = {}
    for sign in (1, -1):
        order = [i for n in (2, 1, 3) for i in range(Q) if VECTORS[i][axis] == sign * n]
        place, at = {}, 0
        for i in order:
            place[i] = at
            at += abs(VECTORS[i][axis])
        sides[sign] = (place, at)
    return sides


FACE_X = face_layout(0)
FACE_Y = face_layout(1)
FACE_ROWS = FACE_X[1][1] * WIDTH


SHELLS = {}
for _i, _v in enumerate(VECTORS):
    SHELLS.setdefault(sum(c * c for c in _v), []).append(_i)


def scaled(k, value):
    return value if k == 1 else value * float(k)


def combine(terms):
    total = None
    for k, value in terms:
        if k == 0:
            continue
        if total is None:
            total = scaled(k, value)
        elif k > 0:
            total = total + scaled(k, value)
        else:
            total = total - scaled(-k, value)
    return total


def tree(values):
    values = list(values)
    while len(values) > 1:
        values = [
            values[i] + values[i + 1] if i + 1 < len(values) else values[i]
            for i in range(0, len(values), 2)
        ]
    return values[0]


class Sums:
    def __init__(self, parts=4):
        self.parts = [None] * parts
        self.turn = 0

    def add(self, value):
        k = self.turn % len(self.parts)
        self.turn += 1
        self.parts[k] = value if self.parts[k] is None else self.parts[k] + value

    def total(self):
        return tree([p for p in self.parts if p is not None])


def half_rows(i, half):
    return pl.ds(pl.multiple_of(half * 8 + i * TILES, 8), 8)


def request_tables(owner_ref, wanted_ref, target_ref, ask_ref, pick_ref):
    own = owner_ref[...] ^ MIRROR
    count = own.shape[1]
    sub = lax.broadcasted_iota(jnp.int32, (count, count), 0)
    lane = lax.broadcasted_iota(jnp.int32, (count, count), 1)

    def down(row):
        return jnp.sum(
            jnp.where(sub == lane, jnp.broadcast_to(row, (count, count)), 0), axis=1, keepdims=True
        )

    same = jnp.where(
        jnp.logical_and(jnp.broadcast_to(own, (count, count)) == down(own), sub < lane), 1, 0
    )
    slot = own * CAP + jnp.sum(same, axis=0, keepdims=True)
    width = ask_ref.shape[0]
    by_slot = jnp.where(
        lax.broadcasted_iota(jnp.int32, (width, count), 0) == jnp.broadcast_to(slot, (width, count)),
        1.0,
        0.0,
    )
    wide = lax.broadcasted_iota(jnp.int32, (count, LANES), 1)
    tiles = jnp.where(wide == down(wanted_ref[...]), 1.0, 0.0)
    ask_ref[...] = jnp.dot(by_slot, tiles, preferred_element_type=jnp.float32)
    by_target = jnp.where(sub == jnp.broadcast_to(target_ref[...], (count, count)), 1.0, 0.0)
    slots = jnp.where(wide == down(slot), 1.0, 0.0)
    pick_ref[...] = jnp.dot(by_target, slots, preferred_element_type=jnp.float32)


def moments_kernel(
    pops_hbm,
    owner_hbm,
    wanted_hbm,
    target_hbm,
    mom_ref,
    ask_ref,
    pick_ref,
    pops_ref,
    owner_ref,
    wanted_ref,
    target_ref,
    sems,
):
    pairs = [
        (owner_hbm, owner_ref),
        (wanted_hbm, wanted_ref),
        (target_hbm, target_ref),
        (pops_hbm, pops_ref),
    ]
    copies = [pltpu.make_async_copy(a, b, sems.at[k]) for k, (a, b) in enumerate(pairs)]
    for copy in copies:
        copy.start()
    for copy in copies[:3]:
        copy.wait()
    request_tables(owner_ref, wanted_ref, target_ref, ask_ref, pick_ref)
    copies[3].wait()

    def one(half, carry):
        raw = {}

        def put(key, k, value):
            if k == 0:
                return
            old = raw.get(key)
            term = scaled(abs(k), value)
            if old is None:
                raw[key] = term if k > 0 else -term
            else:
                raw[key] = old + term if k > 0 else old - term

        for x in range(-3, 4):
            inner = {}
            for y in range(-3, 4):
                if (x, y) not in GROUPS:
                    continue
                f = {z: pops_ref[half_rows(i, half), :] for z, i in GROUPS[(x, y)]}
                even = {k: f[k] + f[-k] for k in (1, 2, 3) if k in f}
                odd = {k: f[k] - f[-k] for k in (1, 2, 3) if k in f}
                sums = [
                    combine([(1, f[0])] + [(1, v) for v in even.values()]),
                    combine([(k, v) for k, v in odd.items()]),
                    combine([(k * k, v) for k, v in even.items()]),
                    combine([(k * k * k, v) for k, v in odd.items()]),
                ]
                for c in range(4):
                    if sums[c] is None:
                        continue
                    for b in range(4 - c):
                        k = y**b
                        if k:
                            inner.setdefault((b, c), []).append((k, sums[c]))
            for (b, c), terms in inner.items():
                terms.sort(key=lambda t: -t[0])
                value = combine(terms) if terms[0][0] > 0 else -combine([(-k, v) for k, v in terms])
                for a in range(4 - b - c):
                    put((a, b, c), x**a, value)
        out = [raw[(0, 0, 0)], raw[(1, 0, 0)], raw[(0, 1, 0)], raw[(0, 0, 1)]]

        def power(*axes):
            return tuple(sum(1 for a in axes if a == d) for d in range(3))

        for a, b in PAIRS:
            value = raw[power(a, b)]
            out.append(value - THETA * out[0] if a == b else value)
        for a, b, c in TRIPLES:
            value = raw[power(a, b, c)]
            if a == b == c:
                value = value - (3.0 * THETA) * out[1 + a]
            elif a == b:
                value = value - THETA * out[1 + c]
            elif b == c:
                value = value - THETA * out[1 + a]
            out.append(value)
        for n in range(MOMENTS):
            mom_ref[half_rows(n, half), :] = out[n]
        return carry

    lax.fori_loop(0, 2, one, 0)


def chosen_rows(pick, block):
    high = block.astype(jnp.bfloat16)
    rest = block - high.astype(jnp.float32)
    middle = rest.astype(jnp.bfloat16)
    low = (rest - middle.astype(jnp.float32)).astype(jnp.bfloat16)
    picks = jnp.concatenate([pick] * 3, axis=1).astype(jnp.bfloat16)
    return jnp.dot(
        picks, jnp.concatenate([high, middle, low], axis=0), preferred_element_type=jnp.float32
    )


def pack_kernel(mom_ref, ask_ref, reply_ref):
    ask = ask_ref[:, :TILES]
    width = ask_ref.shape[0]
    step = 4
    for first in range(0, MOMENTS, step):
        block = jnp.concatenate(
            [mom_ref[n * TILES : (n + 1) * TILES, :] for n in range(first, first + step)], axis=1
        )
        chosen = chosen_rows(ask, block)
        for k in range(step):
            reply_ref[pl.ds(first + k, width, stride=MOMENTS), :] = chosen[
                :, k * LANES : (k + 1) * LANES
            ]


def rebuild(col_ref, half, scale, f_ref):
    a = [col_ref[half_rows(n, half), :] for n in range(MOMENTS)]
    rho = a[0]
    inverse = 1.0 / rho
    flux = a[1:4]
    speed = [v * inverse for v in flux]
    b = [a[n] * (1.0 / NORMS[n]) for n in range(4)]
    n = 4
    names = {}
    for first, second in PAIRS:
        eq = flux[first] * speed[second]
        names[(first, second)] = (eq + scale * (a[n] - eq)) * (1.0 / NORMS[n])
        n += 1
    for first, second, third in TRIPLES:
        eq = flux[first] * speed[second] * speed[third]
        names[(first, second, third)] = (eq + scale * (a[n] - eq)) * (1.0 / NORMS[n])
        n += 1
    k0 = b[0] - THETA * (names[(0, 0)] + names[(1, 1)] + names[(2, 2)])
    lin = []
    for d in range(3):
        others = [names[tuple(sorted((d, e, e)))] for e in range(3) if e != d]
        lin.append(b[1 + d] - THETA * (3.0 * names[(d, d, d)] + (others[0] + others[1])))
    cubes = {k: names[(2, 2, 2)] * float(k**3) for k in (1, 2, 3)}

    def horner(k, parts):
        value = parts[-1]
        for part in parts[-2::-1]:
            if k == 0:
                value = part
            elif k == 1:
                value = part + value
            elif k == -1:
                value = part - value
            else:
                value = part + float(k) * value
        return value

    for x in range(-3, 4):
        q = [
            horner(x, [k0, lin[0], names[(0, 0)], names[(0, 0, 0)]]),
            horner(x, [lin[1], names[(0, 1)], names[(0, 0, 1)]]),
            horner(x, [names[(1, 1)], names[(0, 1, 1)]]),
            names[(1, 1, 1)],
        ]
        r = [
            horner(x, [lin[2], names[(0, 2)], names[(0, 0, 2)]]),
            horner(x, [names[(1, 2)], names[(0, 1, 2)]]),
            names[(1, 1, 2)],
        ]
        s = [horner(x, [names[(2, 2)], names[(0, 2, 2)]]), names[(1, 2, 2)]]
        for y in range(-3, 4):
            if (x, y) not in GROUPS:
                continue
            place = dict(GROUPS[(x, y)])
            p0, p1, p2 = horner(y, q), horner(y, r), horner(y, s)
            f_ref[half_rows(place[0], half), :] = p0
            for k in (1, 2, 3):
                if k in place:
                    even = p0 + scaled(k * k, p2)
                    odd = scaled(k, p1) + cubes[k]
                    f_ref[half_rows(place[k], half), :] = even + odd
                    f_ref[half_rows(place[-k], half), :] = even - odd


def collide(f_ref, d_ref, half, solid, beta, own_ref, weighted):
    w = [float(v) for v in WEIGHTS]

    def load(ref, i):
        return ref[half_rows(i, half), :]

    rho_s, flux_s = Sums(), [Sums(2) for _ in range(3)]
    rho_s.add(w[INDEX[(0, 0, 0)]] * load(f_ref, INDEX[(0, 0, 0)]))
    for i, v in enumerate(VECTORS):
        opposite = INDEX[tuple(-c for c in v)]
        if i >= opposite:
            continue
        plus, minus = load(f_ref, opposite), load(f_ref, i)
        rho_s.add(w[i] * (plus + minus))
        odd = w[i] * (plus - minus)
        for d in range(3):
            k = -v[d]
            if k:
                flux_s[d].add(odd if k == 1 else odd * float(k))
    rho = rho_s.total()
    inverse = 1.0 / rho
    powers, gauss = [], []
    for d in range(3):
        rate = flux_s[d].total() * inverse * (1.0 / THETA)
        up, down = jnp.exp(rate), jnp.exp(-rate)
        one = {0: None, 1: up, -1: down, 2: up * up, -2: down * down}
        one[3], one[-3] = one[2] * up, one[-2] * down
        powers.append(one)
        gauss.append({k: float(np.exp(-0.5 * k * k)) for k in range(-3, 4)})

    def pair_sum(d, k):
        return (powers[d][k] + powers[d][-k]) * gauss[d][k]

    zs = [pair_sum(2, k) for k in (1, 2, 3)]
    upto = {
        (0,): 1.0,
        (0, 1): 1.0 + zs[0],
        (0, 1, 2): 1.0 + zs[0] + zs[1],
        (0, 2): 1.0 + zs[1],
        (0, 1, 2, 3): 1.0 + zs[0] + zs[1] + zs[2],
    }
    xs = [1.0] + [pair_sum(0, k) for k in (1, 2, 3)]
    ys = [1.0] + [pair_sum(1, k) for k in (1, 2, 3)]
    rows = []
    for x in range(4):
        line = []
        for y in range(4):
            if (x, y) not in GROUPS:
                continue
            key = tuple(sorted(z for z, _ in GROUPS[(x, y)] if z >= 0))
            line.append(ys[y] * upto[key])
        rows.append(xs[x] * functools.reduce(lambda p, q: p + q, line))
    norm = functools.reduce(lambda p, q: p + q, rows)
    factor = rho * float(TOTAL) / norm

    least = None
    curves = {n: Sums(2) for n in SHELLS}
    starts = {n: Sums(2) for n in SHELLS}
    for x in range(-3, 4):
        base = factor if x == 0 else factor * powers[0][x]
        for y in range(-3, 4):
            if (x, y) not in GROUPS:
                continue
            plane = base if y == 0 else base * powers[1][y]
            for z, i in GROUPS[(x, y)]:
                f = load(f_ref, i)
                equil = plane if z == 0 else plane * powers[2][z]
                delta = equil - f
                d_ref[half_rows(i, half), :] = delta
                floored = jnp.maximum(f, FLOOR)
                ratio = delta / floored
                least = ratio if least is None else jnp.minimum(least, ratio)
                shell = x * x + y * y + z * z
                curves[shell].add(delta * ratio)
                starts[shell].add(floored * jnp.log(floored))
    ceiling = 0.95 / jnp.maximum(-least, 0.2375)
    of_shell = {n: w[members[0]] for n, members in SHELLS.items()}
    bound = 0.25 * (tree(of_shell[n] * curves[n].total() for n in SHELLS) + 1e-6)
    entropy = tree(of_shell[n] * starts[n].total() for n in SHELLS)

    def newton(turn, alpha):
        value, slope = Sums(), Sums()
        for members in SHELLS.values():
            of_value, of_slope = Sums(), Sums()
            for i in members:
                delta = load(d_ref, i)
                path = jnp.maximum(load(f_ref, i) + alpha * delta, FLOOR)
                logs = jnp.log(path)
                of_value.add(path * logs)
                of_slope.add(delta * logs)
            value.add(w[members[0]] * of_value.total())
            slope.add(w[members[0]] * of_slope.total())
        change = (value.total() - entropy) / jnp.maximum(slope.total(), bound)
        return jnp.minimum(jnp.maximum(alpha - change, 1.0), ceiling)

    alpha = lax.fori_loop(0, 3, newton, jnp.full(rho.shape, 2.0, jnp.float32))
    step = alpha * beta
    for i, v in enumerate(VECTORS):
        post = jnp.where(solid == 1, rho, load(f_ref, i) + step * load(d_ref, i))
        if weighted:
            post = post * w[i]
        if v[2]:
            post = pltpu.roll(post, v[2] % LANES, 1)
        own_ref[half_rows(i, half), :] = post


def route(axis, odd_ref, even_ref, one_ref, two_ref):
    odd = lax.axis_index(axis) % 2 == 1
    a, b = odd_ref[...], even_ref[...]
    one_ref[...] = jnp.where(odd, a, b)
    two_ref[...] = jnp.where(odd, b, a)


LATE_ROWS = 8


def face_rows(sign, own_ref, out_ref, first_half_only):
    place, _ = FACE_X[sign]
    for i, at in place.items():
        n = abs(VECTORS[i][0]) * WIDTH
        skip = n - 8 if first_half_only and n > 8 else 0
        base = i * TILES
        if sign > 0:
            out_ref[at * WIDTH + skip : at * WIDTH + n, :] = own_ref[
                base + TILES - n + skip : base + TILES, :
            ]
        else:
            out_ref[at * WIDTH : at * WIDTH + n - skip, :] = own_ref[base : base + n - skip, :]


def send_early(own_ref, xa_ref):
    odd = lax.axis_index("gx") % 2 == 1

    @pl.when(odd)
    def _():
        face_rows(1, own_ref, xa_ref, True)

    @pl.when(jnp.logical_not(odd))
    def _():
        face_rows(-1, own_ref, xa_ref, True)


def send_late(own_ref, xb_ref, late_ref):
    odd = lax.axis_index("gx") % 2 == 1
    late_ref[...] = jnp.zeros_like(late_ref)

    @pl.when(odd)
    def _():
        face_rows(-1, own_ref, xb_ref, False)
        at = INDEX[(3, 0, 0)] * TILES + WIDTH
        late_ref[0:WIDTH, :] = own_ref[at : at + WIDTH, :]

    @pl.when(jnp.logical_not(odd))
    def _():
        face_rows(1, own_ref, xb_ref, False)
        at = INDEX[(-3, 0, 0)] * TILES + 2 * WIDTH
        late_ref[0:WIDTH, :] = own_ref[at : at + WIDTH, :]


def put_late(late_ref, new_ref, on_odd):
    odd = lax.axis_index("gx") % 2 == 1

    @pl.when(odd if on_odd else jnp.logical_not(odd))
    def _():
        at = INDEX[(-3, 0, 0)] * TILES + TILES - WIDTH if on_odd else INDEX[(3, 0, 0)] * TILES
        new_ref[at : at + WIDTH, :] = late_ref[0:WIDTH, :]


def early_half():
    return lax.axis_index("gx") % 2


def solid_half(solid_ref, half):
    return solid_ref[pl.ds(pl.multiple_of(half * 8, 8), 8), :]


def level_constants():
    level = lax.axis_index("level")
    scale = jnp.where(level == 1, SCALE_FINE, SCALE_COARSE)
    return scale, jnp.where(level == 1, BETA_FINE, BETA_COARSE)


def rebuild_early(reply_ref, pick_ref, solid_ref, own_ref, xa_ref, col_ref, f_ref, d_ref):
    scale, beta = level_constants()
    width = reply_ref.shape[0] // MOMENTS
    pick = pick_ref[:, :width]
    step = 4
    for first in range(0, MOMENTS, step):
        block = jnp.concatenate(
            [
                reply_ref[pl.ds(n, width, stride=MOMENTS), :]
                for n in range(first, first + step)
            ],
            axis=1,
        )
        chosen = chosen_rows(pick, block)
        for k in range(step):
            n = first + k
            col_ref[n * TILES : (n + 1) * TILES, :] = chosen[:, k * LANES : (k + 1) * LANES]

    half = early_half()
    rebuild(col_ref, half, scale, f_ref)
    collide(f_ref, d_ref, half, solid_half(solid_ref, half), beta, own_ref, False)
    send_early(own_ref, xa_ref)


def rebuild_late(first_ref, col_ref, solid_ref, own_ref, xb_ref, late_ref, f_ref, d_ref):
    scale, beta = level_constants()
    half = 1 - early_half()
    rebuild(col_ref, half, scale, f_ref)
    collide(f_ref, d_ref, half, solid_half(solid_ref, half), beta, own_ref, False)
    send_late(own_ref, xb_ref, late_ref)


def shift_x(own_ref, xa_ref, xb_ref, x_ref, ya_ref, yb_ref, low_ref, high_ref, up_ref, down_ref):
    route("gx", xb_ref, xa_ref, low_ref, high_ref)
    for i, v in enumerate(VECTORS):
        n = abs(v[0]) * WIDTH
        base = i * TILES
        if n == 0:
            x_ref[base : base + TILES, :] = own_ref[base : base + TILES, :]
        elif v[0] > 0:
            at = FACE_X[1][0][i] * WIDTH
            x_ref[base + n : base + TILES, :] = own_ref[base : base + TILES - n, :]
            x_ref[base : base + n, :] = low_ref[at : at + n, :]
        else:
            at = FACE_X[-1][0][i] * WIDTH
            x_ref[base : base + TILES - n, :] = own_ref[base + n : base + TILES, :]
            x_ref[base + TILES - n : base + TILES, :] = high_ref[at : at + n, :]
    for sign, out_ref in ((1, up_ref), (-1, down_ref)):
        place, _ = FACE_Y[sign]
        for i, at in place.items():
            n = abs(VECTORS[i][1])
            for k in range(n):
                row = WIDTH - n + k if sign > 0 else k
                out_ref[(at + k) * WIDTH : (at + k + 1) * WIDTH, :] = x_ref[
                    pl.ds(i * TILES + row, WIDTH, stride=WIDTH), :
                ]
    route("gy", up_ref, down_ref, ya_ref, yb_ref)


def assemble(x_ref, low_ref, high_ref, out_ref, first=0, last=Q):
    for i in range(first, last):
        v = VECTORS[i]
        base = i * TILES
        out_ref[base : base + TILES, :] = x_ref[base - v[1] : base - v[1] + TILES, :]
        n = abs(v[1])
        for k in range(n):
            if v[1] > 0:
                src_ref, at, row = low_ref, FACE_Y[1][0][i] + k, k
            else:
                src_ref, at, row = high_ref, FACE_Y[-1][0][i] + k, WIDTH - n + k
            out_ref[pl.ds(base + row, WIDTH, stride=WIDTH), :] = src_ref[
                at * WIDTH : (at + 1) * WIDTH, :
            ]


def second_early(
    x_ref, ya_ref, yb_ref, late_ref, solid_ref, own_ref, xa_ref, f_ref, d_ref, low_ref, high_ref
):
    route("gy", yb_ref, ya_ref, low_ref, high_ref)
    assemble(x_ref, low_ref, high_ref, f_ref)
    put_late(late_ref, f_ref, True)
    put_late(late_ref, f_ref, False)
    half = early_half()
    collide(f_ref, d_ref, half, solid_half(solid_ref, half), BETA_FINE, own_ref, True)
    send_early(own_ref, xa_ref)


def second_late(first_ref, f_ref, solid_ref, own_ref, xb_ref, late_ref, d_ref):
    half = 1 - early_half()
    collide(f_ref, d_ref, half, solid_half(solid_ref, half), BETA_FINE, own_ref, True)
    send_late(own_ref, xb_ref, late_ref)


PIECES = [(Q * k // 4, Q * (k + 1) // 4) for k in range(4)]


def last_kernel(weighted, x_ref, ya_ref, yb_ref, late_ref, out_ref, new_ref, low_ref, high_ref, sems):
    def piece(k):
        first, last = PIECES[k]
        rows = pl.ds(first * TILES, (last - first) * TILES)
        return pltpu.make_async_copy(new_ref.at[rows, :], out_ref.at[rows, :], sems.at[k])

    route("gy", yb_ref, ya_ref, low_ref, high_ref)
    for k, (first, last) in enumerate(PIECES):
        assemble(x_ref, low_ref, high_ref, new_ref, first, last)
        if first == 0 or last == Q:
            put_late(late_ref, new_ref, first == 0)
        if not weighted:
            for i in range(first, last):
                rows = slice(i * TILES, (i + 1) * TILES)
                new_ref[rows, :] = new_ref[rows, :] * float(WEIGHTS[i])
        piece(k).start()
    for k in range(len(PIECES)):
        piece(k).wait()


def call(kernel, outs, args, scratch=(), flops=4_000_000, far_args=0, far_outs=False, more=(), alias=False):
    whole = pl.BlockSpec(memory_space=pltpu.VMEM)
    far = pl.BlockSpec(memory_space=pltpu.HBM)
    kind = pltpu.HBM if far_outs else jax.ShapeDtypeStruct
    shapes = [kind((rows, LANES), jnp.float32) for rows in outs]
    moved = sum(int(rows) * LANES for rows in outs) + sum(int(np.prod(a.shape)) for a in args)
    return pl.pallas_call(
        kernel,
        out_shape=shapes,
        in_specs=[far] * far_args + [whole] * (len(args) - far_args),
        out_specs=[far if far_outs else whole] * len(shapes),
        input_output_aliases={0: 0} if alias else {},
        scratch_shapes=[pltpu.VMEM((rows, LANES), jnp.float32) for rows in scratch] + list(more),
        compiler_params=pltpu.CompilerParams(vmem_limit_bytes=24 << 20),
        cost_estimate=pl.CostEstimate(flops=flops, bytes_accessed=4 * moved, transcendentals=0),
    )(*args)


def swap_edges(axis, messages):
    count = lax.axis_size(axis)
    odd = [(i, (i + 1) % count if i % 2 else (i - 1) % count) for i in range(count)]
    even = [(i, i ^ 1) for i in range(count)]
    to = {"odd": odd, "even": even}
    return [lax.ppermute(value, axis, to[edges]) for edges, value in messages]


def step(populations, solid_mask, recv_tiles, owner_gy, owner_tiles):
    peers = lax.axis_size("gy")
    count = owner_tiles.shape[-1]
    pops = populations.reshape(ROWS, LANES)
    solid = solid_mask.reshape(TILES, LANES)
    owners = owner_gy.reshape(1, count)
    wanted = owner_tiles.reshape(1, count)
    targets = recv_tiles.reshape(1, count)
    slots = peers * CAP
    tables = [owners, wanted, targets]
    mom, ask, pick = call(
        moments_kernel,
        [MOMENTS * TILES, slots, TILES],
        [pltpu.with_memory_space_constraint(a, pltpu.HBM) for a in [pops] + tables],
        [ROWS],
        far_args=4,
        more=[pltpu.VMEM((1, count), jnp.int32)] * 3 + [pltpu.SemaphoreType.DMA((4,))],
    )
    across = [
        (level * peers + g, (1 - level) * peers + (g ^ MIRROR))
        for level in range(lax.axis_size("level"))
        for g in range(peers)
    ]
    crossed = lax.ppermute(mom, ("level", "gy"), across)
    asked = lax.all_to_all(
        ask.reshape(peers, CAP, LANES), "gy", split_axis=0, concat_axis=0, tiled=True
    ).reshape(slots, LANES)
    (answer,) = call(pack_kernel, [slots * MOMENTS], [crossed, asked])
    reply = lax.all_to_all(
        answer.reshape(peers, CAP * MOMENTS, LANES), "gy", split_axis=0, concat_axis=0, tiled=True
    ).reshape(slots * MOMENTS, LANES)
    faces = [ROWS, FACE_ROWS, FACE_ROWS]
    early = [ROWS, FACE_ROWS]
    late_outs = [ROWS, FACE_ROWS, LATE_ROWS]

    def along_x(xa, finish):
        (first,) = swap_edges("gx", [("odd", xa)])
        own, xb, late = finish()
        second, late = swap_edges("gx", [("even", xb), ("odd", late)])
        return own, first, second, late

    def along_y(own, first, second):
        moved, ya, yb = call(shift_x, faces, [own, first, second], [FACE_ROWS] * 4)
        (first,) = swap_edges("gy", [("odd", ya)])
        (second,) = swap_edges("gy", [("even", yb)])
        return moved, first, second

    half_own, xa, col = call(
        rebuild_early, early + [MOMENTS * TILES], [reply, pick, solid], [ROWS, ROWS]
    )
    own, first, second, late = along_x(
        xa, lambda: call(rebuild_late, late_outs, [half_own, col, solid], [ROWS, ROWS], alias=True)
    )
    moved, first, second = along_y(own, first, second)

    def last(weighted, moved, first, second, late):
        (out,) = call(
            functools.partial(last_kernel, weighted),
            [ROWS],
            [moved, first, second, late],
            [ROWS] + [FACE_ROWS] * 2,
            far_outs=True,
            more=[pltpu.SemaphoreType.DMA((len(PIECES),))],
        )
        return out

    def fine_end(moved, first, second, late, solid):
        half_own, xa, f = call(
            second_early,
            early + [ROWS],
            [moved, first, second, late, solid],
            [ROWS] + [FACE_ROWS] * 2,
        )
        own, first, second, late = along_x(
            xa, lambda: call(second_late, late_outs, [half_own, f, solid], [ROWS], alias=True)
        )
        moved, first, second = along_y(own, first, second)
        return last(True, moved, first, second, late)

    def coarse_end(moved, first, second, late, solid):
        return last(False, moved, first, second, late)

    out = lax.cond(
        lax.axis_index("level") == 1, fine_end, coarse_end, moved, first, second, late, solid
    )
    return out.reshape(populations.shape)


def solution(mesh):
    placed = (
        P("level", None, "gx", "gy", None),
        P("level", "gx", "gy", None),
        P("level", "gx", "gy", None),
        P("level", "gx", "gy", None, None),
        P("level", "gx", "gy", None),
    )
    return jax.shard_map(
        step,
        mesh=mesh,
        in_specs=placed,
        out_specs=P("level", None, "gx", "gy", None),
        check_vma=False,
    )
```

```python
import functools
import jax
import jax.numpy as jnp
import numpy as np
from jax import lax
from jax.experimental import pallas as pl
from jax.experimental.pallas import tpu as pltpu
from jax.sharding import PartitionSpec as P


CAP = 2
FLOOR = 0.05
BETA_COARSE = 0.9
BETA_FINE = 0.8
SCALE_FINE = 0.5
SCALE_COARSE = 1.5
WIDTH = 4
TILES = 16
LANES = 128
MIRROR = 3


def lattice():
    shells = [
        (0, 0, 0),
        (0, 0, 1),
        (0, 1, 1),
        (1, 1, 1),
        (0, 0, 2),
        (0, 2, 2),
        (2, 2, 2),
        (0, 0, 3),
        (0, 1, 2),
        (1, 1, 2),
    ]
    vectors = []
    for first in range(-3, 4):
        for second in range(-3, 4):
            for third in range(-3, 4):
                if tuple(sorted((abs(first), abs(second), abs(third)))) in shells:
                    vectors.append((first, second, third))
    offsets = np.array(vectors)
    speeds = offsets * 1.0
    raw = np.exp(-0.5 * np.sum(speeds * speeds, axis=1))
    total = np.sum(raw)
    weights = raw / total
    theta = float(np.sum(weights * speeds[:, 0] * speeds[:, 0]))
    return vectors, speeds, weights, theta, float(total)


VECTORS, SPEEDS, WEIGHTS, THETA, TOTAL = lattice()
Q = len(VECTORS)
ROWS = Q * TILES
INDEX = {v: i for i, v in enumerate(VECTORS)}
PAIRS = [(a, b) for a in range(3) for b in range(a, 3)]
TRIPLES = [(a, b, c) for a in range(3) for b in range(a, 3) for c in range(b, 3)]
MOMENTS = 1 + 3 + len(PAIRS) + len(TRIPLES)
GROUPS = {}
for _i, (_x, _y, _z) in enumerate(VECTORS):
    GROUPS.setdefault((_x, _y), []).append((_z, _i))


def norms():
    rows = [np.ones(Q)]
    for a in range(3):
        rows.append(SPEEDS[:, a])
    for a, b in PAIRS:
        rows.append(SPEEDS[:, a] * SPEEDS[:, b] - THETA * float(a == b))
    for a, b, c in TRIPLES:
        rows.append(
            SPEEDS[:, a] * SPEEDS[:, b] * SPEEDS[:, c]
            - THETA
            * (
                SPEEDS[:, a] * float(b == c)
                + SPEEDS[:, b] * float(a == c)
                + SPEEDS[:, c] * float(a == b)
            )
        )
    basis = np.stack(rows)
    return (basis * basis) @ WEIGHTS


NORMS = norms()


def face_layout(axis):
    sides = {}
    for sign in (1, -1):
        order = [i for n in (2, 1, 3) for i in range(Q) if VECTORS[i][axis] == sign * n]
        place, at = {}, 0
        for i in order:
            place[i] = at
            at += abs(VECTORS[i][axis])
        sides[sign] = (place, at)
    return sides


FACE_X = face_layout(0)
FACE_Y = face_layout(1)
FACE_ROWS = FACE_X[1][1] * WIDTH


SHELLS = {}
for _i, _v in enumerate(VECTORS):
    SHELLS.setdefault(sum(c * c for c in _v), []).append(_i)


def scaled(k, value):
    return value if k == 1 else value * float(k)


def combine(terms):
    total = None
    for k, value in terms:
        if k == 0:
            continue
        if total is None:
            total = scaled(k, value)
        elif k > 0:
            total = total + scaled(k, value)
        else:
            total = total - scaled(-k, value)
    return total


def tree(values):
    values = list(values)
    while len(values) > 1:
        values = [
            values[i] + values[i + 1] if i + 1 < len(values) else values[i]
            for i in range(0, len(values), 2)
        ]
    return values[0]


class Sums:
    def __init__(self, parts=4):
        self.parts = [None] * parts
        self.turn = 0

    def add(self, value):
        k = self.turn % len(self.parts)
        self.turn += 1
        self.parts[k] = value if self.parts[k] is None else self.parts[k] + value

    def total(self):
        return tree([p for p in self.parts if p is not None])


def half_rows(i, half):
    return pl.ds(pl.multiple_of(half * 8 + i * TILES, 8), 8)


def request_tables(owner_ref, wanted_ref, target_ref, ask_ref, pick_ref):
    own = owner_ref[...] ^ MIRROR
    count = own.shape[1]
    sub = lax.broadcasted_iota(jnp.int32, (count, count), 0)
    lane = lax.broadcasted_iota(jnp.int32, (count, count), 1)

    def down(row):
        return jnp.sum(
            jnp.where(sub == lane, jnp.broadcast_to(row, (count, count)), 0), axis=1, keepdims=True
        )

    same = jnp.where(
        jnp.logical_and(jnp.broadcast_to(own, (count, count)) == down(own), sub < lane), 1, 0
    )
    slot = own * CAP + jnp.sum(same, axis=0, keepdims=True)
    width = ask_ref.shape[0]
    by_slot = jnp.where(
        lax.broadcasted_iota(jnp.int32, (width, count), 0) == jnp.broadcast_to(slot, (width, count)),
        1.0,
        0.0,
    )
    wide = lax.broadcasted_iota(jnp.int32, (count, LANES), 1)
    tiles = jnp.where(wide == down(wanted_ref[...]), 1.0, 0.0)
    ask_ref[...] = jnp.dot(by_slot, tiles, preferred_element_type=jnp.float32)
    by_target = jnp.where(sub == jnp.broadcast_to(target_ref[...], (count, count)), 1.0, 0.0)
    slots = jnp.where(wide == down(slot), 1.0, 0.0)
    pick_ref[...] = jnp.dot(by_target, slots, preferred_element_type=jnp.float32)


def moments_kernel(
    pops_hbm,
    owner_hbm,
    wanted_hbm,
    target_hbm,
    mom_ref,
    ask_ref,
    pick_ref,
    pops_ref,
    owner_ref,
    wanted_ref,
    target_ref,
    sems,
):
    pairs = [
        (owner_hbm, owner_ref),
        (wanted_hbm, wanted_ref),
        (target_hbm, target_ref),
        (pops_hbm, pops_ref),
    ]
    copies = [pltpu.make_async_copy(a, b, sems.at[k]) for k, (a, b) in enumerate(pairs)]
    for copy in copies:
        copy.start()
    for copy in copies[:3]:
        copy.wait()
    request_tables(owner_ref, wanted_ref, target_ref, ask_ref, pick_ref)
    copies[3].wait()

    def one(half, carry):
        raw = {}

        def put(key, k, value):
            if k == 0:
                return
            old = raw.get(key)
            term = scaled(abs(k), value)
            if old is None:
                raw[key] = term if k > 0 else -term
            else:
                raw[key] = old + term if k > 0 else old - term

        for x in range(-3, 4):
            inner = {}
            for y in range(-3, 4):
                if (x, y) not in GROUPS:
                    continue
                f = {z: pops_ref[half_rows(i, half), :] for z, i in GROUPS[(x, y)]}
                even = {k: f[k] + f[-k] for k in (1, 2, 3) if k in f}
                odd = {k: f[k] - f[-k] for k in (1, 2, 3) if k in f}
                sums = [
                    combine([(1, f[0])] + [(1, v) for v in even.values()]),
                    combine([(k, v) for k, v in odd.items()]),
                    combine([(k * k, v) for k, v in even.items()]),
                    combine([(k * k * k, v) for k, v in odd.items()]),
                ]
                for c in range(4):
                    if sums[c] is None:
                        continue
                    for b in range(4 - c):
                        k = y**b
                        if k:
                            inner.setdefault((b, c), []).append((k, sums[c]))
            for (b, c), terms in inner.items():
                terms.sort(key=lambda t: -t[0])
                value = combine(terms) if terms[0][0] > 0 else -combine([(-k, v) for k, v in terms])
                for a in range(4 - b - c):
                    put((a, b, c), x**a, value)
        out = [raw[(0, 0, 0)], raw[(1, 0, 0)], raw[(0, 1, 0)], raw[(0, 0, 1)]]

        def power(*axes):
            return tuple(sum(1 for a in axes if a == d) for d in range(3))

        for a, b in PAIRS:
            value = raw[power(a, b)]
            out.append(value - THETA * out[0] if a == b else value)
        for a, b, c in TRIPLES:
            value = raw[power(a, b, c)]
            if a == b == c:
                value = value - (3.0 * THETA) * out[1 + a]
            elif a == b:
                value = value - THETA * out[1 + c]
            elif b == c:
                value = value - THETA * out[1 + a]
            out.append(value)
        for n in range(MOMENTS):
            mom_ref[half_rows(n, half), :] = out[n]
        return carry

    lax.fori_loop(0, 2, one, 0)


def chosen_rows(pick, block):
    high = block.astype(jnp.bfloat16)
    rest = block - high.astype(jnp.float32)
    middle = rest.astype(jnp.bfloat16)
    low = (rest - middle.astype(jnp.float32)).astype(jnp.bfloat16)
    picks = jnp.concatenate([pick] * 3, axis=1).astype(jnp.bfloat16)
    return jnp.dot(
        picks, jnp.concatenate([high, middle, low], axis=0), preferred_element_type=jnp.float32
    )


def pack_kernel(mom_ref, ask_ref, reply_ref):
    ask = ask_ref[:, :TILES]
    width = ask_ref.shape[0]
    step = 4
    for first in range(0, MOMENTS, step):
        block = jnp.concatenate(
            [mom_ref[n * TILES : (n + 1) * TILES, :] for n in range(first, first + step)], axis=1
        )
        chosen = chosen_rows(ask, block)
        for k in range(step):
            reply_ref[pl.ds(first + k, width, stride=MOMENTS), :] = chosen[
                :, k * LANES : (k + 1) * LANES
            ]


def rebuild(col_ref, half, scale, f_ref):
    a = [col_ref[half_rows(n, half), :] for n in range(MOMENTS)]
    rho = a[0]
    inverse = 1.0 / rho
    flux = a[1:4]
    speed = [v * inverse for v in flux]
    b = [a[n] * (1.0 / NORMS[n]) for n in range(4)]
    n = 4
    names = {}
    for first, second in PAIRS:
        eq = flux[first] * speed[second]
        names[(first, second)] = (eq + scale * (a[n] - eq)) * (1.0 / NORMS[n])
        n += 1
    for first, second, third in TRIPLES:
        eq = flux[first] * speed[second] * speed[third]
        names[(first, second, third)] = (eq + scale * (a[n] - eq)) * (1.0 / NORMS[n])
        n += 1
    k0 = b[0] - THETA * (names[(0, 0)] + names[(1, 1)] + names[(2, 2)])
    lin = []
    for d in range(3):
        others = [names[tuple(sorted((d, e, e)))] for e in range(3) if e != d]
        lin.append(b[1 + d] - THETA * (3.0 * names[(d, d, d)] + (others[0] + others[1])))
    cubes = {k: names[(2, 2, 2)] * float(k**3) for k in (1, 2, 3)}

    def horner(k, parts):
        value = parts[-1]
        for part in parts[-2::-1]:
            if k == 0:
                value = part
            elif k == 1:
                value = part + value
            elif k == -1:
                value = part - value
            else:
                value = part + float(k) * value
        return value

    for x in range(-3, 4):
        q = [
            horner(x, [k0, lin[0], names[(0, 0)], names[(0, 0, 0)]]),
            horner(x, [lin[1], names[(0, 1)], names[(0, 0, 1)]]),
            horner(x, [names[(1, 1)], names[(0, 1, 1)]]),
            names[(1, 1, 1)],
        ]
        r = [
            horner(x, [lin[2], names[(0, 2)], names[(0, 0, 2)]]),
            horner(x, [names[(1, 2)], names[(0, 1, 2)]]),
            names[(1, 1, 2)],
        ]
        s = [horner(x, [names[(2, 2)], names[(0, 2, 2)]]), names[(1, 2, 2)]]
        for y in range(-3, 4):
            if (x, y) not in GROUPS:
                continue
            place = dict(GROUPS[(x, y)])
            p0, p1, p2 = horner(y, q), horner(y, r), horner(y, s)
            f_ref[half_rows(place[0], half), :] = p0
            for k in (1, 2, 3):
                if k in place:
                    even = p0 + scaled(k * k, p2)
                    odd = scaled(k, p1) + cubes[k]
                    f_ref[half_rows(place[k], half), :] = even + odd
                    f_ref[half_rows(place[-k], half), :] = even - odd


def collide(f_ref, d_ref, half, solid, beta, own_ref, weighted):
    w = [float(v) for v in WEIGHTS]

    def load(ref, i):
        return ref[half_rows(i, half), :]

    rho_s, flux_s = Sums(), [Sums(2) for _ in range(3)]
    rho_s.add(w[INDEX[(0, 0, 0)]] * load(f_ref, INDEX[(0, 0, 0)]))
    for i, v in enumerate(VECTORS):
        opposite = INDEX[tuple(-c for c in v)]
        if i >= opposite:
            continue
        plus, minus = load(f_ref, opposite), load(f_ref, i)
        rho_s.add(w[i] * (plus + minus))
        odd = w[i] * (plus - minus)
        for d in range(3):
            k = -v[d]
            if k:
                flux_s[d].add(odd if k == 1 else odd * float(k))
    rho = rho_s.total()
    inverse = 1.0 / rho
    powers, gauss = [], []
    for d in range(3):
        rate = flux_s[d].total() * inverse * (1.0 / THETA)
        up, down = jnp.exp(rate), jnp.exp(-rate)
        one = {0: None, 1: up, -1: down, 2: up * up, -2: down * down}
        one[3], one[-3] = one[2] * up, one[-2] * down
        powers.append(one)
        gauss.append({k: float(np.exp(-0.5 * k * k)) for k in range(-3, 4)})

    def pair_sum(d, k):
        return (powers[d][k] + powers[d][-k]) * gauss[d][k]

    zs = [pair_sum(2, k) for k in (1, 2, 3)]
    upto = {
        (0,): 1.0,
        (0, 1): 1.0 + zs[0],
        (0, 1, 2): 1.0 + zs[0] + zs[1],
        (0, 2): 1.0 + zs[1],
        (0, 1, 2, 3): 1.0 + zs[0] + zs[1] + zs[2],
    }
    xs = [1.0] + [pair_sum(0, k) for k in (1, 2, 3)]
    ys = [1.0] + [pair_sum(1, k) for k in (1, 2, 3)]
    rows = []
    for x in range(4):
        line = []
        for y in range(4):
            if (x, y) not in GROUPS:
                continue
            key = tuple(sorted(z for z, _ in GROUPS[(x, y)] if z >= 0))
            line.append(ys[y] * upto[key])
        rows.append(xs[x] * functools.reduce(lambda p, q: p + q, line))
    norm = functools.reduce(lambda p, q: p + q, rows)
    factor = rho * float(TOTAL) / norm

    least = None
    curves = {n: Sums(2) for n in SHELLS}
    starts = {n: Sums(2) for n in SHELLS}
    for x in range(-3, 4):
        base = factor if x == 0 else factor * powers[0][x]
        for y in range(-3, 4):
            if (x, y) not in GROUPS:
                continue
            plane = base if y == 0 else base * powers[1][y]
            for z, i in GROUPS[(x, y)]:
                f = load(f_ref, i)
                equil = plane if z == 0 else plane * powers[2][z]
                delta = equil - f
                d_ref[half_rows(i, half), :] = delta
                floored = jnp.maximum(f, FLOOR)
                ratio = delta / floored
                least = ratio if least is None else jnp.minimum(least, ratio)
                shell = x * x + y * y + z * z
                curves[shell].add(delta * ratio)
                starts[shell].add(floored * jnp.log(floored))
    ceiling = 0.95 / jnp.maximum(-least, 0.2375)
    of_shell = {n: w[members[0]] for n, members in SHELLS.items()}
    bound = 0.25 * (tree(of_shell[n] * curves[n].total() for n in SHELLS) + 1e-6)
    entropy = tree(of_shell[n] * starts[n].total() for n in SHELLS)

    def newton(turn, alpha):
        value, slope = Sums(), Sums()
        for members in SHELLS.values():
            of_value, of_slope = Sums(), Sums()
            for i in members:
                delta = load(d_ref, i)
                path = jnp.maximum(load(f_ref, i) + alpha * delta, FLOOR)
                logs = jnp.log(path)
                of_value.add(path * logs)
                of_slope.add(delta * logs)
            value.add(w[members[0]] * of_value.total())
            slope.add(w[members[0]] * of_slope.total())
        change = (value.total() - entropy) / jnp.maximum(slope.total(), bound)
        return jnp.minimum(jnp.maximum(alpha - change, 1.0), ceiling)

    alpha = lax.fori_loop(0, 3, newton, jnp.full(rho.shape, 2.0, jnp.float32))
    step = alpha * beta
    for i, v in enumerate(VECTORS):
        post = jnp.where(solid == 1, rho, load(f_ref, i) + step * load(d_ref, i))
        if weighted:
            post = post * w[i]
        if v[2]:
            post = pltpu.roll(post, v[2] % LANES, 1)
        own_ref[half_rows(i, half), :] = post


def route(axis, odd_ref, even_ref, one_ref, two_ref):
    odd = lax.axis_index(axis) % 2 == 1
    a, b = odd_ref[...], even_ref[...]
    one_ref[...] = jnp.where(odd, a, b)
    two_ref[...] = jnp.where(odd, b, a)


LATE_ROWS = 8


def face_rows(sign, own_ref, out_ref, first_half_only):
    place, _ = FACE_X[sign]
    for i, at in place.items():
        n = abs(VECTORS[i][0]) * WIDTH
        skip = n - 8 if first_half_only and n > 8 else 0
        base = i * TILES
        if sign > 0:
            out_ref[at * WIDTH + skip : at * WIDTH + n, :] = own_ref[
                base + TILES - n + skip : base + TILES, :
            ]
        else:
            out_ref[at * WIDTH : at * WIDTH + n - skip, :] = own_ref[base : base + n - skip, :]


def send_early(own_ref, xa_ref):
    odd = lax.axis_index("gx") % 2 == 1

    @pl.when(odd)
    def _():
        face_rows(1, own_ref, xa_ref, True)

    @pl.when(jnp.logical_not(odd))
    def _():
        face_rows(-1, own_ref, xa_ref, True)


def send_late(own_ref, xb_ref, late_ref):
    odd = lax.axis_index("gx") % 2 == 1
    late_ref[...] = jnp.zeros_like(late_ref)

    @pl.when(odd)
    def _():
        face_rows(-1, own_ref, xb_ref, False)
        at = INDEX[(3, 0, 0)] * TILES + WIDTH
        late_ref[0:WIDTH, :] = own_ref[at : at + WIDTH, :]

    @pl.when(jnp.logical_not(odd))
    def _():
        face_rows(1, own_ref, xb_ref, False)
        at = INDEX[(-3, 0, 0)] * TILES + 2 * WIDTH
        late_ref[0:WIDTH, :] = own_ref[at : at + WIDTH, :]


def put_late(late_ref, new_ref, on_odd):
    odd = lax.axis_index("gx") % 2 == 1

    @pl.when(odd if on_odd else jnp.logical_not(odd))
    def _():
        at = INDEX[(-3, 0, 0)] * TILES + TILES - WIDTH if on_odd else INDEX[(3, 0, 0)] * TILES
        new_ref[at : at + WIDTH, :] = late_ref[0:WIDTH, :]


def early_half():
    return lax.axis_index("gx") % 2


def solid_half(solid_ref, half):
    return solid_ref[pl.ds(pl.multiple_of(half * 8, 8), 8), :]


def level_constants():
    level = lax.axis_index("level")
    scale = jnp.where(level == 1, SCALE_FINE, SCALE_COARSE)
    return scale, jnp.where(level == 1, BETA_FINE, BETA_COARSE)


def rebuild_early(reply_ref, pick_ref, solid_ref, own_ref, xa_ref, col_ref, f_ref, d_ref):
    scale, beta = level_constants()
    width = reply_ref.shape[0] // MOMENTS
    pick = pick_ref[:, :width]
    step = 4
    for first in range(0, MOMENTS, step):
        block = jnp.concatenate(
            [
                reply_ref[pl.ds(n, width, stride=MOMENTS), :]
                for n in range(first, first + step)
            ],
            axis=1,
        )
        chosen = chosen_rows(pick, block)
        for k in range(step):
            n = first + k
            col_ref[n * TILES : (n + 1) * TILES, :] = chosen[:, k * LANES : (k + 1) * LANES]

    half = early_half()
    rebuild(col_ref, half, scale, f_ref)
    collide(f_ref, d_ref, half, solid_half(solid_ref, half), beta, own_ref, False)
    send_early(own_ref, xa_ref)


def rebuild_late(first_ref, col_ref, solid_ref, own_ref, xb_ref, late_ref, f_ref, d_ref):
    scale, beta = level_constants()
    half = 1 - early_half()
    rebuild(col_ref, half, scale, f_ref)
    collide(f_ref, d_ref, half, solid_half(solid_ref, half), beta, own_ref, False)
    send_late(own_ref, xb_ref, late_ref)


def shift_base(own_ref, x_ref):
    for i, v in enumerate(VECTORS):
        n = abs(v[0]) * WIDTH
        base = i * TILES
        if v[0] >= 0:
            x_ref[base + n : base + TILES, :] = own_ref[base : base + TILES - n, :]
        else:
            x_ref[base : base + TILES - n, :] = own_ref[base + n : base + TILES, :]


def shift_x(
    base_ref, xa_ref, xb_ref, x_ref, ya_ref, yb_ref, low_ref, high_ref, up_ref, down_ref
):
    route("gx", xb_ref, xa_ref, low_ref, high_ref)
    for i, v in enumerate(VECTORS):
        n = abs(v[0]) * WIDTH
        base = i * TILES
        if v[0] > 0:
            at = FACE_X[1][0][i] * WIDTH
            x_ref[base : base + n, :] = low_ref[at : at + n, :]
        elif v[0] < 0:
            at = FACE_X[-1][0][i] * WIDTH
            x_ref[base + TILES - n : base + TILES, :] = high_ref[at : at + n, :]
    for sign, out_ref in ((1, up_ref), (-1, down_ref)):
        place, _ = FACE_Y[sign]
        for i, at in place.items():
            n = abs(VECTORS[i][1])
            for k in range(n):
                row = WIDTH - n + k if sign > 0 else k
                out_ref[(at + k) * WIDTH : (at + k + 1) * WIDTH, :] = x_ref[
                    pl.ds(i * TILES + row, WIDTH, stride=WIDTH), :
                ]
    route("gy", up_ref, down_ref, ya_ref, yb_ref)


def assemble_base(x_ref, out_ref):
    for i, v in enumerate(VECTORS):
        base = i * TILES
        out_ref[base : base + TILES, :] = x_ref[base - v[1] : base - v[1] + TILES, :]


def assemble(low_ref, high_ref, out_ref, first=0, last=Q):
    for i in range(first, last):
        v = VECTORS[i]
        base = i * TILES
        n = abs(v[1])
        for k in range(n):
            if v[1] > 0:
                src_ref, at, row = low_ref, FACE_Y[1][0][i] + k, k
            else:
                src_ref, at, row = high_ref, FACE_Y[-1][0][i] + k, WIDTH - n + k
            out_ref[pl.ds(base + row, WIDTH, stride=WIDTH), :] = src_ref[
                at * WIDTH : (at + 1) * WIDTH, :
            ]


def second_early(
    base_ref, ya_ref, yb_ref, late_ref, solid_ref, own_ref, xa_ref, f_ref, d_ref, low_ref, high_ref
):
    route("gy", yb_ref, ya_ref, low_ref, high_ref)
    assemble(low_ref, high_ref, f_ref)
    put_late(late_ref, f_ref, True)
    put_late(late_ref, f_ref, False)
    half = early_half()
    collide(f_ref, d_ref, half, solid_half(solid_ref, half), BETA_FINE, own_ref, True)
    send_early(own_ref, xa_ref)


def second_late(first_ref, f_ref, solid_ref, own_ref, xb_ref, late_ref, d_ref):
    half = 1 - early_half()
    collide(f_ref, d_ref, half, solid_half(solid_ref, half), BETA_FINE, own_ref, True)
    send_late(own_ref, xb_ref, late_ref)


PIECES = [(Q * k // 4, Q * (k + 1) // 4) for k in range(4)]


def last_kernel(
    weighted, base_ref, ya_ref, yb_ref, late_ref, out_ref, new_ref, low_ref, high_ref, sems
):
    def piece(k):
        first, last = PIECES[k]
        rows = pl.ds(first * TILES, (last - first) * TILES)
        return pltpu.make_async_copy(new_ref.at[rows, :], out_ref.at[rows, :], sems.at[k])

    route("gy", yb_ref, ya_ref, low_ref, high_ref)
    for k, (first, last) in enumerate(PIECES):
        assemble(low_ref, high_ref, new_ref, first, last)
        if first == 0 or last == Q:
            put_late(late_ref, new_ref, first == 0)
        if not weighted:
            for i in range(first, last):
                rows = slice(i * TILES, (i + 1) * TILES)
                new_ref[rows, :] = new_ref[rows, :] * float(WEIGHTS[i])
        piece(k).start()
    for k in range(len(PIECES)):
        piece(k).wait()


def call(kernel, outs, args, scratch=(), flops=4_000_000, far_args=0, far_outs=0, more=(), alias=None):
    whole = pl.BlockSpec(memory_space=pltpu.VMEM)
    far = pl.BlockSpec(memory_space=pltpu.HBM)
    kinds = [pltpu.HBM] * far_outs + [jax.ShapeDtypeStruct] * (len(outs) - far_outs)
    shapes = [kind((rows, LANES), jnp.float32) for kind, rows in zip(kinds, outs)]
    moved = sum(int(rows) * LANES for rows in outs) + sum(int(np.prod(a.shape)) for a in args)
    return pl.pallas_call(
        kernel,
        out_shape=shapes,
        in_specs=[far] * far_args + [whole] * (len(args) - far_args),
        out_specs=[far] * far_outs + [whole] * (len(shapes) - far_outs),
        input_output_aliases={} if alias is None else {0: alias},
        scratch_shapes=[pltpu.VMEM((rows, LANES), jnp.float32) for rows in scratch] + list(more),
        compiler_params=pltpu.CompilerParams(vmem_limit_bytes=24 << 20),
        cost_estimate=pl.CostEstimate(flops=flops, bytes_accessed=4 * moved, transcendentals=0),
    )(*args)


def swap_edges(axis, messages):
    count = lax.axis_size(axis)
    odd = [(i, (i + 1) % count if i % 2 else (i - 1) % count) for i in range(count)]
    even = [(i, i ^ 1) for i in range(count)]
    to = {"odd": odd, "even": even}
    return [lax.ppermute(value, axis, to[edges]) for edges, value in messages]


def step(populations, solid_mask, recv_tiles, owner_gy, owner_tiles):
    peers = lax.axis_size("gy")
    count = owner_tiles.shape[-1]
    pops = populations.reshape(ROWS, LANES)
    solid = solid_mask.reshape(TILES, LANES)
    owners = owner_gy.reshape(1, count)
    wanted = owner_tiles.reshape(1, count)
    targets = recv_tiles.reshape(1, count)
    slots = peers * CAP
    tables = [owners, wanted, targets]
    mom, ask, pick = call(
        moments_kernel,
        [MOMENTS * TILES, slots, TILES],
        [pltpu.with_memory_space_constraint(a, pltpu.HBM) for a in [pops] + tables],
        [ROWS],
        far_args=4,
        more=[pltpu.VMEM((1, count), jnp.int32)] * 3 + [pltpu.SemaphoreType.DMA((4,))],
    )
    across = [
        (level * peers + g, (1 - level) * peers + (g ^ MIRROR))
        for level in range(lax.axis_size("level"))
        for g in range(peers)
    ]
    crossed = lax.ppermute(mom, ("level", "gy"), across)
    asked = lax.all_to_all(
        ask.reshape(peers, CAP, LANES), "gy", split_axis=0, concat_axis=0, tiled=True
    ).reshape(slots, LANES)
    (answer,) = call(pack_kernel, [slots * MOMENTS], [crossed, asked])
    reply = lax.all_to_all(
        answer.reshape(peers, CAP * MOMENTS, LANES), "gy", split_axis=0, concat_axis=0, tiled=True
    ).reshape(slots * MOMENTS, LANES)
    faces = [ROWS, FACE_ROWS, FACE_ROWS]
    early = [ROWS, FACE_ROWS]
    late_outs = [ROWS, FACE_ROWS, LATE_ROWS]

    def along_x(xa, finish):
        (first,) = swap_edges("gx", [("odd", xa)])
        own, xb, late = finish()
        (second,) = swap_edges("gx", [("even", xb)])
        (late,) = swap_edges("gx", [("odd", late)])
        return own, first, second, late

    def along_y(own, first, second):
        (base,) = call(shift_base, [ROWS], [own])
        moved, ya, yb = call(shift_x, faces, [base, first, second], [FACE_ROWS] * 4, alias=0)
        (first,) = swap_edges("gy", [("odd", ya)])
        (second,) = swap_edges("gy", [("even", yb)])
        (base,) = call(assemble_base, [ROWS], [moved])
        return base, first, second

    half_own, xa, col = call(
        rebuild_early, early + [MOMENTS * TILES], [reply, pick, solid], [ROWS, ROWS]
    )
    own, first, second, late = along_x(
        xa, lambda: call(rebuild_late, late_outs, [half_own, col, solid], [ROWS, ROWS], alias=0)
    )
    moved, first, second = along_y(own, first, second)

    def last(weighted, moved, first, second, late):
        out, _ = call(
            functools.partial(last_kernel, weighted),
            [ROWS, ROWS],
            [moved, first, second, late],
            [FACE_ROWS] * 2,
            far_outs=1,
            alias=1,
            more=[pltpu.SemaphoreType.DMA((len(PIECES),))],
        )
        return out

    def fine_end(moved, first, second, late, solid):
        half_own, xa, f = call(
            second_early,
            early + [ROWS],
            [moved, first, second, late, solid],
            [ROWS] + [FACE_ROWS] * 2,
            alias=2,
        )
        own, first, second, late = along_x(
            xa, lambda: call(second_late, late_outs, [half_own, f, solid], [ROWS], alias=0)
        )
        moved, first, second = along_y(own, first, second)
        return last(True, moved, first, second, late)

    def coarse_end(moved, first, second, late, solid):
        return last(False, moved, first, second, late)

    out = lax.cond(
        lax.axis_index("level") == 1, fine_end, coarse_end, moved, first, second, late, solid
    )
    return out.reshape(populations.shape)


def solution(mesh):
    placed = (
        P("level", None, "gx", "gy", None),
        P("level", "gx", "gy", None),
        P("level", "gx", "gy", None),
        P("level", "gx", "gy", None, None),
        P("level", "gx", "gy", None),
    )
    return jax.shard_map(
        step,
        mesh=mesh,
        in_specs=placed,
        out_specs=P("level", None, "gx", "gy", None),
        check_vma=False,
    )
```
